32 devices in a mesh: dp: 8 (over y, x, core), tensor: 4 (over z).
Axes of the slice: x: 2, y: 2, z: 4, core: 2. Of those that a mesh axis runs over, the one named last changes fastest.
Arguments:
- inputs: bfloat16 [8192, 1536], P(('dp', 'tensor')), may hold values from -12 to 12
- norm1_gain: float32 [1536], replicated, may hold values from 0.5 to 1.5
- w_in_x: bfloat16 [1536, 2048], P('dp', 'tensor'), may hold values from -0.15625 to 0.15625
- w_in_y: bfloat16 [1536, 2048], P('dp', 'tensor'), may hold values from -0.15625 to 0.15625
- conv_w: float32 [4, 2048], P(None, 'tensor'), may hold values from -3 to 3
- conv_b: float32 [2048], P('tensor'), may hold values from -1.8 to 1.8
- gates: bfloat16 [2, 16, 128, 128], P(None, 'tensor', 'dp'), may hold values from -0.5 to 0.5
- gate_bias: float32 [2, 2048], P(None, 'tensor'), may hold values from -1 to 1
- decay_param: float32 [2048], P('tensor'), may hold values from -7 to -1
- w_out: bfloat16 [1536, 2048], P('dp', 'tensor'), may hold values from -0.375 to 0.375
- norm2_gain: float32 [1536], replicated, may hold values from 0.5 to 1.5
- w_gate: bfloat16 [1536, 4608], P('dp', 'tensor'), may hold values from -0.15625 to 0.15625
- w_up: bfloat16 [1536, 4608], P('dp', 'tensor'), may hold values from -0.15625 to 0.15625
- w_down: bfloat16 [1536, 4608], P('dp', 'tensor'), may hold values from -0.125 to 0.125
- cotangent: bfloat16 [8192, 1536], P(('dp', 'tensor')), may hold values from -6 to 6
Outputs:
- output: bfloat16 [8192, 1536], P(('dp', 'tensor'))
- grad_inputs: bfloat16 [8192, 1536], P(('dp', 'tensor'))
- grad_norm1_gain: float32 [1536], replicated
- grad_w_in_x: float32 [1536, 2048], P('dp', 'tensor')
- grad_w_in_y: float32 [1536, 2048], P('dp', 'tensor')
- grad_conv_w: float32 [4, 2048], replicated
- grad_conv_b: float32 [2048], replicated
- grad_gates: float32 [2, 16, 128, 128], P(None, 'tensor', 'dp')
- grad_gate_bias: float32 [2, 2048], replicated
- grad_decay_param: float32 [2048], replicated
- grad_w_out: float32 [1536, 2048], P('dp', 'tensor')
- grad_norm2_gain: float32 [1536], replicated
- grad_w_gate: float32 [1536, 4608], P('dp', 'tensor')
- grad_w_up: float32 [1536, 4608], P('dp', 'tensor')
- grad_w_down: float32 [1536, 4608], P('dp', 'tensor')
- stream_rms: float32 [4], replicated
The draws below stay inside these ranges and needn't reach their ends.
All inputs are finite; a program needn't handle non-finite values.
Results may differ from the reference program's by a relative error of at most 0.0085.
Values may be sent and summed in bfloat16 or wider, within the bound.
A program may use at most 192 MiB of HBM per device.

```python
import jax
import jax.numpy as jnp
from jax import lax

D = 1536
LRU = 2048
BLOCKS = 16
FF = 4608
CONV = 4
SEQ_LEN = 1024
BW = 128
TOKENS = 8192


def draw_inputs(key, part):
    ramp = jnp.arange(TOKENS).astype(jnp.float32) / max(TOKENS - 1, 1)
    base = jnp.clip(jax.random.normal(key, (TOKENS, D), jnp.float32), -4.0, 4.0)
    scales = 1.0 + 2.0 * ramp
    return (base * scales[:, None]).astype(jnp.bfloat16)


def strengthened(drawn, own_key, source, target, parts, factor):
    owner, partner = [(jnp.arange(drawn.shape[axis_at]) // (drawn.shape[axis_at] // parts)).reshape([-1 if axis == axis_at else 1 for axis in range(drawn.ndim)]) for axis_at in (source, target)]
    chosen = jax.random.permutation(own_key, parts)[partner]
    strong = (owner == chosen) | (owner == (partner + parts // 2) % parts)
    return jnp.where(strong, factor * drawn, drawn)


def block_levels(rng, dims, shards, least, top_value):
    level = 1.0
    for position, parts in shards:
        steps = jax.random.uniform(jax.random.fold_in(jax.random.fold_in(rng, 6), position), (parts,), jnp.float32, least / len(shards), top_value / len(shards))
        level = level * jnp.repeat(jnp.exp(steps), dims[position] // parts).reshape((-1,) + (1,) * (len(dims) - 1 - position))
    return level


def normal_values(stream_key, dims, scale, reach, shards=(), kind=jnp.bfloat16):
    drawn = jax.random.normal(stream_key, dims, jnp.float32) * scale
    if len(shards) > 0:
        drawn = block_levels(stream_key, dims, shards, -0.22, 0.18) * drawn
    return jnp.clip(drawn, min=-reach, max=reach).astype(kind)


def noise_with(rng, shape, spread, reach, pieces, heavy, held_as=jnp.bfloat16):
    drawn = spread * jax.random.normal(rng, shape, jnp.float32)
    if pieces:
        drawn = drawn * block_levels(rng, shape, pieces, -0.22, 0.18)
    return jnp.clip(strengthened(drawn, jax.random.fold_in(rng, 3), *heavy), -reach, reach).astype(held_as)


def setup_inputs(seed: int = 0) -> dict:
    seeds = jax.random.split(jax.random.key(seed), 16)
    inputs = draw_inputs(jax.random.fold_in(seeds[15], 71), 0)
    norm1_gain = jnp.clip(1.0 + 0.1 * jax.random.normal(seeds[1], (D,), jnp.float32), 0.5, 1.5)
    w_in_x = normal_values(seeds[2], (D, LRU), D ** -0.5, 0.15625, ((0, 8), (1, 4)))
    w_in_y = normal_values(seeds[3], (D, LRU), D ** -0.5, 0.15625, ((0, 8), (1, 4)))
    conv_w = normal_values(seeds[4], (CONV, LRU), CONV ** -0.5, 3.0, ((1, 4),), jnp.float32)
    conv_b = normal_values(seeds[5], (LRU,), 0.3, 1.8, ((0, 4),), jnp.float32)
    gates = normal_values(seeds[6], (2, BLOCKS, BW, BW), BW ** -0.5, 0.5, ((1, 4), (2, 8)))
    gate_bias = jnp.clip(jax.random.uniform(seeds[7], (2, LRU), jnp.float32, -1.0, 1.0) * block_levels(seeds[7], (2, LRU), ((1, 4),), -0.4, 0.0), -1.0, 1.0)
    decay_param = jnp.clip(-7.0 + 6.0 * jax.random.uniform(seeds[8], (LRU,), jnp.float32) ** block_levels(seeds[8], (LRU,), ((0, 4),), -0.2, 0.2), -7.0, -1.0)
    w_out = normal_values(seeds[9], (D, LRU), (LRU // 8) ** -0.5, 0.375, ((0, 8), (1, 4)))
    norm2_gain = jnp.clip(1.0 + 0.1 * jax.random.normal(seeds[10], (D,), jnp.float32), 0.5, 1.5)
    w_gate = normal_values(seeds[11], (D, FF), D ** -0.5, 0.15625, ((0, 8), (1, 4)))
    w_up = normal_values(seeds[12], (D, FF), D ** -0.5, 0.15625, ((0, 8), (1, 4)))
    w_down = normal_values(seeds[13], (D, FF), (FF // 2) ** -0.5, 0.125, ((0, 8), (1, 4)))
    cotangent = noise_with(seeds[14], (TOKENS, D), 1.0, 6.0, ((0, 32),), (0, 1, 32, 2.75))
    return {"inputs": inputs, "norm1_gain": norm1_gain, "w_in_x": w_in_x, "w_in_y": w_in_y, "conv_w": conv_w, "conv_b": conv_b, "gates": gates, "gate_bias": gate_bias, "decay_param": decay_param, "w_out": w_out, "norm2_gain": norm2_gain, "w_gate": w_gate, "w_up": w_up, "w_down": w_down, "cotangent": cotangent}


epsilon = 1e-06
highest = lax.Precision.HIGHEST

@jax.custom_vjp
def low(v):
    return lax.optimization_barrier(v.astype(jnp.bfloat16)).astype(jnp.float32)

@jax.custom_vjp
def low_back(v):
    return v

def low_keep(v):
    return (low(v), None)

def low_pass(kept, grad):
    return (grad,)

def back_keep(v):
    return (v, None)

def back_low(kept, grad):
    return (low(grad),)
low.defvjp(low_keep, low_pass)
low_back.defvjp(back_keep, back_low)

def gelu_tanh(value):
    return jax.nn.gelu(value, approximate=True)

def rms_norm(value, gain):
    return value * lax.rsqrt(lax.optimization_barrier(jnp.mean(value * value, axis=-1, keepdims=True)) + epsilon) * gain

def advance(state, inputs):
    decay, inflow = inputs
    state = decay * state + inflow
    return (state, state)

def griffin_block(resid, norm1_gain, w_in_x, w_in_y, conv_w, conv_b, gates, gate_bias, decay_param, w_out, norm2_gain, w_gate, w_up, w_down):
    length = resid.shape[0]
    n_one = low(rms_norm(resid, norm1_gain))
    x_branch = low_back(jnp.dot(n_one, w_in_x, precision=highest))
    y_pre = low_back(jnp.dot(n_one, w_in_y, precision=highest))
    padded = jnp.pad(x_branch, ((CONV - 1, 0), (0, 0)))
    conv_sum = conv_b + jnp.zeros_like(x_branch)
    for k in range(CONV):
        conv_sum = conv_sum + conv_w[k] * padded[CONV - 1 - k:CONV - 1 - k + length]
    conv_low = low(conv_sum)
    blocked = conv_low.reshape(length, BLOCKS, BW)
    z_input = low_back(jnp.einsum('lbi,bij->lbj', blocked, gates[0], precision=highest).reshape(length, LRU) + gate_bias[0])
    z_decay = low_back(jnp.einsum('lbi,bij->lbj', blocked, gates[1], precision=highest).reshape(length, LRU) + gate_bias[1])
    log_decay = -8.0 * jax.nn.sigmoid(z_decay) * jax.nn.softplus(decay_param)
    seq_start = (jnp.arange(length) == 0)[:, None]
    mult = jnp.where(seq_start, 1.0, jnp.sqrt(-jnp.expm1(2.0 * log_decay)))
    inflow = mult * jax.nn.sigmoid(z_input) * conv_low
    _, states = lax.scan(jax.checkpoint(advance), jnp.zeros((LRU,), resid.dtype), (jnp.exp(log_decay), inflow))
    mixed_out = low(states * gelu_tanh(y_pre))
    branch = low_back(jnp.dot(mixed_out, w_out.T, precision=highest))
    stream = resid + branch
    n_two = low(rms_norm(stream, norm2_gain))
    gate_pre = low_back(jnp.dot(n_two, w_gate, precision=highest))
    up_pre = low_back(jnp.dot(n_two, w_up, precision=highest))
    hidden = low(gelu_tanh(gate_pre) * up_pre)
    ffn_out = low_back(jnp.dot(hidden, w_down.T, precision=highest))
    result = stream + ffn_out
    squares = jnp.stack([jnp.sum(stream * stream), jnp.sum(branch * branch), jnp.sum(ffn_out * ffn_out), jnp.sum(result * result)])
    return (result, squares)

def reference(inputs, norm1_gain, w_in_x, w_in_y, conv_w, conv_b, gates, gate_bias, decay_param, w_out, norm2_gain, w_gate, w_up, w_down, cotangent):
    params = tuple((value.astype(jnp.float32) for value in (norm1_gain, w_in_x, w_in_y, conv_w, conv_b, gates, gate_bias, decay_param, w_out, norm2_gain, w_gate, w_up, w_down)))
    seq_total = TOKENS // SEQ_LEN
    token_seqs = inputs.astype(jnp.float32).reshape(seq_total, SEQ_LEN, D)
    cot_seqs = cotangent.astype(jnp.float32).reshape(seq_total, SEQ_LEN, D)

    def per_sequence(carry, item):
        gradients, totals = carry
        token_seq, cot_seq = item
        result, pull, squares = jax.vjp(griffin_block, token_seq, *params, has_aux=True)
        pulled = pull(cot_seq)
        gradients = tuple((total + part for total, part in zip(gradients, pulled[1:])))
        return ((gradients, totals + squares), (result, pulled[0]))
    zero_grads = tuple((jnp.zeros_like(value) for value in params))
    (gradients, totals), (results, input_grads) = lax.scan(per_sequence, (zero_grads, jnp.zeros((4,), jnp.float32)), (token_seqs, cot_seqs))
    stream_rms = jnp.sqrt(totals / (TOKENS * D))
    output = results.reshape(TOKENS, D).astype(jnp.bfloat16)
    grad_inputs = input_grads.reshape(TOKENS, D).astype(jnp.bfloat16)
    return (output, grad_inputs, gradients[0], gradients[1], gradients[2], gradients[3], gradients[4], gradients[5], gradients[6], gradients[7], gradients[8], gradients[9], gradients[10], gradients[11], gradients[12], stream_rms)
```

```python
import jax
import jax.numpy as jnp
from jax import lax
from jax.experimental import pallas as pl
from jax.experimental.pallas import tpu as pltpu
from jax.sharding import PartitionSpec as P

CONV = 4
SEQ_LEN = 1024


epsilon = 1e-06


def gelu_tanh(value):
    return jax.nn.gelu(value, approximate=True)


def combine(earlier, later):
    return (earlier[0] * later[0], later[0] * earlier[1] + later[1])


def norm_back(value, scale, gain, grad):
    scaled = gain * grad
    return scale * scaled - value * scale * scale * scale * jnp.mean(
        scaled * value, axis=1, keepdims=True
    )


def row_product(left, right):
    return lax.dot_general(
        left, right, (((0,), (0,)), ((), ())), preferred_element_type=jnp.float32
    )


def back_product(left, right):
    return lax.dot_general(
        left, right, (((1,), (1,)), ((), ())), preferred_element_type=jnp.float32
    )


def local(
    inputs,
    norm1_gain,
    w_in_x,
    w_in_y,
    conv_w,
    conv_b,
    gates,
    gate_bias,
    decay_param,
    w_out,
    norm2_gain,
    w_gate,
    w_up,
    w_down,
    cotangent,
):
    row_count = inputs.shape[0]
    model_width = inputs.shape[1]
    tensor_count = lax.axis_size("tensor")
    group_rows = row_count * tensor_count
    seq_count = group_rows // SEQ_LEN
    rec_x, rec_y, rec_o, gate_mats = (
        lax.all_gather(w_in_x, "dp", axis=0, tiled=True),
        lax.all_gather(w_in_y, "dp", axis=0, tiled=True),
        lax.all_gather(w_out, "dp", axis=0, tiled=True),
        lax.all_gather(gates, "dp", axis=2, tiled=True),
    )
    channels = rec_x.shape[1]
    blocks_here = gate_mats.shape[1]
    block_width = gate_mats.shape[3]
    residual = inputs.astype(jnp.float32)
    scale_one = lax.rsqrt(jnp.mean(residual * residual, axis=1, keepdims=True) + epsilon)
    n_one = (residual * scale_one * norm1_gain).astype(jnp.bfloat16)
    full_one = lax.all_gather(n_one, "tensor", axis=0, tiled=True)
    x_branch = jnp.dot(full_one, rec_x, preferred_element_type=jnp.float32)
    y_pre = jnp.dot(full_one, rec_y, preferred_element_type=jnp.float32)
    seq_x = x_branch.reshape(seq_count, SEQ_LEN, channels)
    padded = jnp.pad(seq_x, ((0, 0), (CONV - 1, 0), (0, 0)))
    conv_sum = conv_b + jnp.zeros_like(seq_x)
    for k in range(CONV):
        conv_sum = conv_sum + conv_w[k] * padded[:, CONV - 1 - k : CONV - 1 - k + SEQ_LEN]
    conv_low = conv_sum.reshape(group_rows, channels).astype(jnp.bfloat16)
    conv_value = conv_low.astype(jnp.float32)
    blocked = conv_low.reshape(group_rows, blocks_here, block_width)
    z_input = (
        jnp.einsum(
            "gbi,bij->gbj", blocked, gate_mats[0], preferred_element_type=jnp.float32
        ).reshape(group_rows, channels)
        + gate_bias[0]
    )
    z_decay = (
        jnp.einsum(
            "gbi,bij->gbj", blocked, gate_mats[1], preferred_element_type=jnp.float32
        ).reshape(group_rows, channels)
        + gate_bias[1]
    )
    seq_start = (jnp.arange(group_rows) % SEQ_LEN == 0)[:, None]

    def coefficients(input_pre, decay_pre, conv_part, decay_raw):
        log_decay = -8.0 * jax.nn.sigmoid(decay_pre) * jax.nn.softplus(decay_raw)
        mult = jnp.where(seq_start, 1.0, jnp.sqrt(-jnp.expm1(2.0 * log_decay)))
        return (jnp.exp(log_decay), mult * jax.nn.sigmoid(input_pre) * conv_part)

    (decays, inflow), pull_coeff = jax.vjp(coefficients, z_input, z_decay, conv_value, decay_param)
    seq_decay = decays.reshape(seq_count, SEQ_LEN, channels)
    _, seq_states = lax.associative_scan(
        combine, (seq_decay, inflow.reshape(seq_count, SEQ_LEN, channels)), axis=1
    )
    states = seq_states.reshape(group_rows, channels)
    y_gate = gelu_tanh(y_pre)
    mixed_out = (states * y_gate).astype(jnp.bfloat16)
    branch = lax.psum_scatter(
        back_product(mixed_out, rec_o), "tensor", scatter_dimension=0, tiled=True
    )
    stream = residual + branch
    mlp_g, mlp_u, mlp_d = (
        lax.all_gather(w_gate, "dp", axis=0, tiled=True),
        lax.all_gather(w_up, "dp", axis=0, tiled=True),
        lax.all_gather(w_down, "dp", axis=0, tiled=True),
    )
    scale_two = lax.rsqrt(jnp.mean(stream * stream, axis=1, keepdims=True) + epsilon)
    n_two = (stream * scale_two * norm2_gain).astype(jnp.bfloat16)
    full_two = lax.all_gather(n_two, "tensor", axis=0, tiled=True)
    gate_pre = jnp.dot(full_two, mlp_g, preferred_element_type=jnp.float32)
    up_pre = jnp.dot(full_two, mlp_u, preferred_element_type=jnp.float32)
    hidden = (gelu_tanh(gate_pre) * up_pre).astype(jnp.bfloat16)
    ffn_out = lax.psum_scatter(
        back_product(hidden, mlp_d), "tensor", scatter_dimension=0, tiled=True
    )
    result = stream + ffn_out
    output = result.astype(jnp.bfloat16)
    squares = jnp.stack(
        [
            jnp.sum(stream * stream),
            jnp.sum(branch * branch),
            jnp.sum(ffn_out * ffn_out),
            jnp.sum(result * result),
        ]
    )
    upstream = cotangent.astype(jnp.float32)
    full_cot = lax.all_gather(cotangent, "tensor", axis=0, tiled=True)
    d_hidden = jnp.dot(full_cot, mlp_d, preferred_element_type=jnp.float32)
    grad_down = row_product(full_cot, hidden)
    _, pull_mlp = jax.vjp(
        lambda gate_value, up_value: gelu_tanh(gate_value) * up_value, gate_pre, up_pre
    )
    d_gate, d_up = pull_mlp(d_hidden)
    d_gate_low = d_gate.astype(jnp.bfloat16)
    d_up_low = d_up.astype(jnp.bfloat16)
    grad_gate_w = row_product(full_two, d_gate_low)
    grad_up_w = row_product(full_two, d_up_low)
    d_two = lax.psum_scatter(
        back_product(d_gate_low, mlp_g) + back_product(d_up_low, mlp_u),
        "tensor",
        scatter_dimension=0,
        tiled=True,
    )
    grad_gain_two = jnp.sum(d_two * stream * scale_two, axis=0)
    d_stream = upstream + norm_back(stream, scale_two, norm2_gain, d_two)
    mlp_summed = (grad_gate_w, grad_up_w, grad_down)
    full_branch = lax.all_gather(d_stream.astype(jnp.bfloat16), "tensor", axis=0, tiled=True)
    d_mixed = jnp.dot(full_branch, rec_o, preferred_element_type=jnp.float32)
    grad_out_w = row_product(full_branch, mixed_out)
    d_states = d_mixed * y_gate
    _, pull_gelu = jax.vjp(gelu_tanh, y_pre)
    d_y_low = pull_gelu(d_mixed * states)[0].astype(jnp.bfloat16)
    next_decay = jnp.concatenate([seq_decay[:, 1:], jnp.zeros_like(seq_decay[:, :1])], axis=1)
    _, carried = lax.associative_scan(
        combine, (next_decay, d_states.reshape(seq_count, SEQ_LEN, channels)), reverse=True, axis=1
    )
    prev_states = jnp.concatenate([jnp.zeros_like(seq_states[:, :1]), seq_states[:, :-1]], axis=1)
    d_decays = (carried * prev_states).reshape(group_rows, channels)
    d_input_pre, d_decay_pre, d_conv_direct, grad_decay = pull_coeff(
        (d_decays, carried.reshape(group_rows, channels))
    )
    d_input_low = d_input_pre.astype(jnp.bfloat16)
    d_decay_low = d_decay_pre.astype(jnp.bfloat16)
    grad_bias = jnp.stack(
        [
            jnp.sum(d_input_low, axis=0, dtype=jnp.float32),
            jnp.sum(d_decay_low, axis=0, dtype=jnp.float32),
        ]
    )
    input_blocks = d_input_low.reshape(group_rows, blocks_here, block_width)
    decay_blocks = d_decay_low.reshape(group_rows, blocks_here, block_width)
    grad_gate_mats = jnp.stack(
        [
            jnp.einsum("gbi,gbj->bij", blocked, input_blocks, preferred_element_type=jnp.float32),
            jnp.einsum("gbi,gbj->bij", blocked, decay_blocks, preferred_element_type=jnp.float32),
        ]
    )
    d_conv = d_conv_direct + jnp.einsum(
        "gbj,bij->gbi", input_blocks, gate_mats[0], preferred_element_type=jnp.float32
    ).reshape(group_rows, channels)
    d_conv = d_conv + jnp.einsum(
        "gbj,bij->gbi", decay_blocks, gate_mats[1], preferred_element_type=jnp.float32
    ).reshape(group_rows, channels)
    seq_dconv = d_conv.reshape(seq_count, SEQ_LEN, channels)
    grad_conv_b = jnp.sum(seq_dconv, axis=(0, 1))
    padded_back = jnp.pad(seq_dconv, ((0, 0), (0, CONV - 1), (0, 0)))
    tap_grads = []
    d_x_seq = jnp.zeros_like(seq_dconv)
    for k in range(CONV):
        tap_grads.append(
            jnp.sum(seq_dconv * padded[:, CONV - 1 - k : CONV - 1 - k + SEQ_LEN], axis=(0, 1))
        )
        d_x_seq = d_x_seq + conv_w[k] * padded_back[:, k : k + SEQ_LEN]
    grad_conv_w = jnp.stack(tap_grads)
    d_x_low = d_x_seq.reshape(group_rows, channels).astype(jnp.bfloat16)
    grad_in_x_w = row_product(full_one, d_x_low)
    grad_in_y_w = row_product(full_one, d_y_low)
    d_one = lax.psum_scatter(
        back_product(d_x_low, rec_x) + back_product(d_y_low, rec_y),
        "tensor",
        scatter_dimension=0,
        tiled=True,
    )
    grad_gain_one = jnp.sum(d_one * residual * scale_one, axis=0)
    grad_inputs = (d_stream + norm_back(residual, scale_one, norm1_gain, d_one)).astype(
        jnp.bfloat16
    )
    small_grads = jnp.concatenate(
        [grad_conv_w, grad_conv_b[None], grad_bias, grad_decay[None]], axis=0
    )
    spread_grads = lax.dynamic_update_slice(
        jnp.zeros((small_grads.shape[0], channels * tensor_count), jnp.float32),
        small_grads,
        (0, lax.axis_index("tensor") * channels),
    )
    gain_total, small_total, square_total = lax.psum(
        (jnp.stack([grad_gain_one, grad_gain_two]), spread_grads, squares), ("dp", "tensor")
    )
    stream_rms = jnp.sqrt(
        square_total / (row_count * lax.axis_size("dp") * tensor_count * model_width)
    )
    summed_all = (
        lax.psum_scatter(grad_in_x_w, "dp", scatter_dimension=0, tiled=True),
        lax.psum_scatter(grad_in_y_w, "dp", scatter_dimension=0, tiled=True),
        lax.psum_scatter(grad_out_w, "dp", scatter_dimension=0, tiled=True),
        lax.psum_scatter(grad_gate_mats, "dp", scatter_dimension=2, tiled=True),
        lax.psum_scatter(mlp_summed[0], "dp", scatter_dimension=0, tiled=True),
        lax.psum_scatter(mlp_summed[1], "dp", scatter_dimension=0, tiled=True),
        lax.psum_scatter(mlp_summed[2], "dp", scatter_dimension=0, tiled=True),
    )
    rec_summed = summed_all[:4]
    grad_gate_sum, grad_up_sum, grad_down_sum = (summed_all[4], summed_all[5], summed_all[6])
    return (
        output,
        grad_inputs,
        gain_total[0],
        rec_summed[0],
        rec_summed[1],
        small_total[0:CONV],
        small_total[CONV],
        rec_summed[3],
        small_total[CONV + 1 : CONV + 3],
        small_total[CONV + 3],
        rec_summed[2],
        gain_total[1],
        grad_gate_sum,
        grad_up_sum,
        grad_down_sum,
        stream_rms,
    )


MESH = pl.DeviceIdType.MESH
bf16 = jnp.bfloat16
f32 = jnp.float32
VMEM_BYTES = 67043328


def mm(a, b):
    return jnp.dot(a, b, preferred_element_type=f32)


def mm_nt(a, b):
    return lax.dot_general(a, b, (((1,), (1,)), ((), ())), preferred_element_type=f32)


def mm_tn(a, b):
    return lax.dot_general(a, b, (((0,), (0,)), ((), ())), preferred_element_type=f32)


def gelu_value(x):
    return 0.5 * x * (1.0 + jnp.tanh(0.7978845608028654 * x * (1.0 + 0.044715 * (x * x))))


def gelu_pair(x):
    x2 = x * x
    th = jnp.tanh(0.7978845608028654 * x * (1.0 + 0.044715 * x2))
    cdf = 0.5 * (1.0 + th)
    slope = 0.5 * x * (1.0 - th * th) * (0.7978845608028654 * (1.0 + 0.134145 * x2))
    return x * cdf, cdf + slope


def neg_expm1(x):
    series = x * (
        1.0
        + x * (0.5 + x * (1 / 6 + x * (1 / 24 + x * (1 / 120 + x * (1 / 720 + x * (1 / 5040))))))
    )
    return -jnp.where(x > -0.35, series, jnp.exp(x) - 1.0)


class Place:
    def __init__(self):
        self.d = lax.axis_index("dp")
        self.z = lax.axis_index("tensor")
        self.t = lax.div(self.d, 2)
        self.c = lax.rem(self.d, 2)
        self.tx = self.t + 1 - 2 * lax.rem(self.t, 2)
        self.ty = self.t + 2 - 4 * lax.div(self.t, 2)
        self.td = 3 - self.t
        self.peers = (self.tx, self.ty, self.td)

    def plane(self, t):
        return (2 * t + self.c, self.z)

    def line(self, z):
        return (self.d, z)

    def partner(self):
        return (2 * self.t + 1 - self.c, self.z)

    def around(self, k):
        return lax.rem(self.z + k, 4)

    def enter(self):
        barrier = pltpu.get_barrier_semaphore()
        targets = [self.plane(t) for t in self.peers] + [self.partner()]
        targets += [self.line(self.around(k)) for k in (1, 2, 3)]
        for target in targets:
            pl.semaphore_signal(barrier, inc=1, device_id=target, device_id_type=MESH)
        pl.semaphore_wait(barrier, len(targets))


class Wires:
    def __init__(self, place, send, recv, local):
        self.place, self.send, self.recv, self.local = place, send, recv, local
        self.used, self.used_local = 0, 0

    def slot(self):
        self.used += 1
        assert self.used <= self.send.shape[0]
        return self.used - 1

    def copy(self, src, dst, slot, device):
        return pltpu.make_async_remote_copy(
            src_ref=src,
            dst_ref=dst,
            send_sem=self.send.at[slot],
            recv_sem=self.recv.at[slot],
            device_id=device,
            device_id_type=MESH,
        )

    def landed(self, ref, slot):
        self.copy(ref, ref, slot, self.place.partner()).wait_recv()

    def sent(self, ref, slot):
        self.copy(ref, ref, slot, self.place.partner()).wait_send()

    def held_here(self, src, dst):
        self.used_local += 1
        assert self.used_local <= self.local.shape[0]
        return pltpu.make_async_copy(src, dst, self.local.at[self.used_local - 1])

    def here(self, src, dst):
        made = self.held_here(src, dst)
        made.start()
        return made


class Spread:
    def __init__(self, w, parts, homes):
        self.w, self.parts, self.homes = w, parts, homes
        self.slots = [[w.slot() for _ in range(3)] for _ in parts]

    def start(self):
        p = self.w.place
        self.local = []
        for part, home, slots in zip(self.parts, self.homes, self.slots):
            for peer, slot in zip(p.peers, slots):
                self.w.copy(part(peer), home(p.t), slot, p.plane(peer)).start()
            self.local.append(self.w.here(part(p.t), home(p.t)))

    def wait(self):
        p = self.w.place
        for made in self.local:
            made.wait()
        for home, slots in zip(self.homes, self.slots):
            for peer, slot in zip(p.peers, slots):
                self.w.landed(home(peer), slot)

    def drain(self):
        p = self.w.place
        for part, slots in zip(self.parts, self.slots):
            for peer, slot in zip(p.peers, slots):
                self.w.sent(part(peer), slot)


class OneSpread:
    def __init__(self, w, part, home):
        self.w, self.part, self.home = w, part, home
        self.slots = [w.slot() for _ in range(3)]
        self.kept = w.held_here(part, home(w.place.t))

    def start(self):
        p = self.w.place

        @pl.when(p.t == p.z)
        def _():
            self.kept.start()

        for peer, slot in zip(p.peers, self.slots):

            @pl.when(peer == p.z)
            def _():
                self.w.copy(self.part, self.home(p.t), slot, p.plane(peer)).start()

    def wait(self):
        p = self.w.place

        @pl.when(p.t == p.z)
        def _():
            self.kept.wait()
            for peer, slot in zip(p.peers, self.slots):
                self.w.landed(self.home(peer), slot)

    def drain(self):
        p = self.w.place
        for peer, slot in zip(p.peers, self.slots):

            @pl.when(peer == p.z)
            def _():
                self.w.sent(self.part, slot)


class LineGather:
    def __init__(self, w, regions):
        self.w, self.regions = w, regions
        self.slots = [
            {key: w.slot() for key in ["o", "r1", "r2", "r3", "l1", "l2", "l3"]
             + ["or1", "or2", "or3", "ol1", "ol2", "ol3"]}
            for _ in regions
        ]

    def _each(self, b, act, *conditions):
        p = self.w.place
        for (view, odd), slots in zip(self.regions, self.slots):
            terms = list(conditions) + ([b == p.t] if odd else [])
            if not terms:
                act(view, slots)
                continue
            ok = terms[0]
            for term in terms[1:]:
                ok = jnp.logical_and(ok, term)

            @pl.when(ok)
            def _():
                act(view, slots)

    def _start(self, view, b, slot, device):
        p = self.w.place
        self.w.copy(view(b, p.c), view(b, p.c), slot, device).start()

    def first(self):
        p = self.w.place
        z = p.z
        self._each(z, lambda v, s: self._start(v, z, s["r1"], p.line(z + 1)), z < 3)
        self._each(z, lambda v, s: self._start(v, z, s["l1"], p.line(z - 1)), z > 0)
        self._each(z, lambda v, s: self._start(v, z, s["o"], p.partner()))

    def step(self, k):
        p = self.w.place
        z = p.z
        for sign, left in ((1, "r"), (-1, "l")):
            b = z - sign * (k - 1)
            exists = b >= 0 if sign > 0 else b <= 3

            def take(v, s):
                self.w.landed(v(b, p.c), s[f"{left}{k - 1}"])
                self._start(v, b, s[f"o{left}{k - 1}"], p.partner())

            self._each(b, take, exists)
            if k < 4:
                more = z < 3 if sign > 0 else z > 0
                self._each(
                    b, lambda v, s: self._start(v, b, s[f"{left}{k}"], p.line(z + sign)), exists, more
                )

    def finish(self):
        p = self.w.place
        z = p.z
        other = 1 - p.c
        self._each(z, lambda v, s: self.w.landed(v(z, other), s["o"]))
        for k in (1, 2, 3):
            for sign, left in ((1, "r"), (-1, "l")):
                b = z - sign * k
                exists = b >= 0 if sign > 0 else b <= 3
                self._each(b, lambda v, s: self.w.landed(v(b, other), s[f"o{left}{k}"]), exists)

    def drain(self):
        p = self.w.place
        z = p.z
        self._each(z, lambda v, s: self.w.sent(v(z, p.c), s["o"]))
        for k in (1, 2, 3):
            for sign, left in ((1, "r"), (-1, "l")):
                b = z - sign * k
                exists = b >= 0 if sign > 0 else b <= 3
                self._each(b, lambda v, s: self.w.sent(v(b, p.c), s[f"o{left}{k}"]), exists)
                b2 = z - sign * (k - 1)
                exists2 = b2 >= 0 if sign > 0 else b2 <= 3
                more = z < 3 if sign > 0 else z > 0
                self._each(b2, lambda v, s: self.w.sent(v(b2, p.c), s[f"{left}{k}"]), exists2, more)


class PlaneGather:
    def __init__(self, w, buf):
        self.w, self.buf = w, buf
        self.half = buf.shape[1] // 2
        self.s = {key: w.slot() for key in ("x", "y", "fx", "fy")}

    def _low(self, t):
        return self.buf.at[t, pl.ds(0, self.half)]

    def _high(self, t):
        return self.buf.at[t, pl.ds(self.half, self.half)]

    def start(self, own=None):
        p, w = self.w.place, self.w
        self.own = self.buf.at[p.t] if own is None else own
        w.copy(self.own, self.buf.at[p.t], self.s["x"], p.plane(p.tx)).start()
        w.copy(self.own, self.buf.at[p.t], self.s["y"], p.plane(p.ty)).start()

    def forward(self):
        p, w = self.w.place, self.w
        w.landed(self.buf.at[p.tx], self.s["x"])
        w.copy(self._high(p.tx), self._high(p.tx), self.s["fy"], p.plane(p.ty)).start()
        w.landed(self.buf.at[p.ty], self.s["y"])
        w.copy(self._low(p.ty), self._low(p.ty), self.s["fx"], p.plane(p.tx)).start()

    def finish(self):
        p, w = self.w.place, self.w
        w.landed(self._low(p.td), self.s["fx"])
        w.landed(self._high(p.td), self.s["fy"])

    def drain(self):
        p, w = self.w.place, self.w
        w.sent(self.own, self.s["x"])
        w.sent(self.own, self.s["y"])
        w.sent(self._high(p.tx), self.s["fy"])
        w.sent(self._low(p.ty), self.s["fx"])


class PlaneSum:
    def __init__(self, w, part, far, near):
        self.w, self.part, self.far, self.near = w, part, far, near
        self.half = part.shape[1] // 2
        self.s = {key: w.slot() for key in ("dx", "dy", "x", "y")}

    def diagonal(self):
        p, w, h = self.w.place, self.w, self.half
        self.a = self.part.at[p.td, pl.ds(0, h)]
        self.b = self.part.at[p.td, pl.ds(h, h)]
        w.copy(self.a, self.far.at[0], self.s["dx"], p.plane(p.tx)).start()
        w.copy(self.b, self.far.at[1], self.s["dy"], p.plane(p.ty)).start()

    def _add(self, t, which):
        h = self.half

        @pl.loop(0, h // 32)
        def _(i):
            rows = pl.ds(pl.multiple_of(i * 32, 32), 32)
            mine = pl.ds(pl.multiple_of(which * h + i * 32, 32), 32)
            total = self.part[t, mine, :].astype(f32) + self.far[which, rows, :].astype(f32)
            self.part[t, mine, :] = total.astype(bf16)

    def to_y(self):
        p, w = self.w.place, self.w
        w.landed(self.far.at[0], self.s["dx"])
        self._add(p.ty, 0)
        w.copy(self.part.at[p.ty], self.near.at[1], self.s["y"], p.plane(p.ty)).start()

    def to_x(self):
        p, w = self.w.place, self.w
        w.landed(self.far.at[1], self.s["dy"])
        self._add(p.tx, 1)
        w.copy(self.part.at[p.tx], self.near.at[0], self.s["x"], p.plane(p.tx)).start()

    def finish(self):
        self.w.landed(self.near.at[0], self.s["x"])
        self.w.landed(self.near.at[1], self.s["y"])

    def drain(self):
        p, w = self.w.place, self.w
        w.sent(self.a, self.s["dx"])
        w.sent(self.b, self.s["dy"])
        w.sent(self.part.at[p.ty], self.s["y"])
        w.sent(self.part.at[p.tx], self.s["x"])


def add_into(dst, src):
    shape = dst.shape
    if len(shape) == 2:
        dst[...] = (dst[...].astype(f32) + src[...].astype(f32)).astype(bf16)
        return
    for i in range(shape[0]):
        add_into(dst.at[i], src.at[i])


class CoreSum:
    def __init__(self, w, half, landing):
        self.w, self.half, self.landing = w, half, landing
        self.slot = w.slot()

    def start(self):
        p = self.w.place
        self.w.copy(self.half(1 - p.c), self.landing, self.slot, p.partner()).start()

    def finish(self):
        self.w.landed(self.landing, self.slot)
        add_into(self.half(self.w.place.c), self.landing)

    def drain(self):
        self.w.sent(self.half(1 - self.w.place.c), self.slot)


class LineSum:
    def __init__(self, w, regions):
        self.w, self.regions = w, regions
        self.slots = [[w.slot() for _ in range(6)] for _ in regions]

    def _each(self, j, act, *conditions):
        p = self.w.place
        for (piece, landing, odd), slots in zip(self.regions, self.slots):
            terms = list(conditions) + ([j == p.t] if odd else [])
            ok = terms[0]
            for term in terms[1:]:
                ok = jnp.logical_and(ok, term)

            @pl.when(ok)
            def _():
                act(piece, landing, slots)

    def _send(self, k, act):
        z = self.w.place.z
        for side, sign in ((0, 1), (1, -1)):
            j = z + sign * (4 - k)
            valid = jnp.logical_and(j <= 3, z < 3) if sign > 0 else jnp.logical_and(j >= 0, z > 0)
            self._each(j, lambda piece, landing, s: act(piece, landing, s[side * 3 + k - 1], side, k, j, sign), valid)

    def _out(self, piece, landing, slot, side, k, j, sign):
        p = self.w.place
        self.w.copy(piece(j), landing(side, k), slot, p.line(p.z + sign)).start()

    def first(self):
        self._send(1, self._out)

    def _take(self, k):
        z = self.w.place.z
        for side, sign in ((0, 1), (1, -1)):
            j = z - sign + sign * (4 - k)
            valid = jnp.logical_and(j <= 3, z >= 1) if sign > 0 else jnp.logical_and(j >= 0, z <= 2)

            def act(piece, landing, s):
                self.w.landed(landing(side, k), s[side * 3 + k - 1])
                add_into(piece(j), landing(side, k))

            self._each(j, act, valid)

    def step(self, k):
        self._take(k - 1)
        if k < 4:
            self._send(k, self._out)

    def drain(self):
        for k in (1, 2, 3):
            self._send(k, lambda piece, landing, slot, side, kk, j, sign: self.w.sent(piece(j), slot))


def rows16(i, size=16):
    return pl.ds(pl.multiple_of(i * 16, 16), size)


def recurrence_forward(
    x_ref, gain_ref, small_ref, wx, wy, wo, gates, wg, wu, wd,
    x1_ref, stat_ref, sm_out,
    n1_out, win_out, wout_out, wg_out, a2u, a2d, gg_out,
    xb_out, zy_out, zx_out, za_out, c_out, a_out, h_out, o_out,
    win, wout, gg, n1, xb, zy, zx, za, cc, aa, hh, ac, oo, part, far, near, own,
    tail, sums, hin, sm_ref, send, recv, local,
):
    p = Place()
    w = Wires(p, send, recv, local)
    t, c, z = p.t, p.c, p.z
    p.enter()

    def cols(b, width=128):
        return pl.ds(pl.multiple_of(b * width, width), width)

    spread_in = Spread(
        w,
        [lambda q: wx.at[:, cols(q)], lambda q: wy.at[:, cols(q)], lambda q: gates.at[:, q]],
        [
            lambda q: win.at[0, q, c, :, cols(z)],
            lambda q: win.at[1, q, c, :, cols(z)],
            lambda q: gg.at[:, z, q, c],
        ],
    )
    spread_out = Spread(
        w, [lambda q: wo.at[:, cols(q)]], [lambda q: wout.at[q, c, :, cols(z)]]
    )
    spread_g = Spread(
        w, [lambda q: wg.at[:, cols(q, 256)]], [lambda q: wg_out.at[q, c, :, cols(z, 256)]]
    )
    odd_g = OneSpread(w, wg.at[:, pl.ds(1024, 128)], lambda q: wg_out.at[q, c, :, pl.ds(1024, 128)])
    spread_ud = Spread(
        w,
        [lambda q: wu.at[:, cols(q, 256)], lambda q: wd.at[:, cols(q, 256)]],
        [lambda q: a2u.at[q, :, pl.ds(0, 256)], lambda q: a2d.at[q, :, pl.ds(0, 256)]],
    )
    odd_u = OneSpread(w, wu.at[:, pl.ds(1024, 128)], lambda q: a2u.at[q, :, pl.ds(256, 128)])
    odd_d = OneSpread(w, wd.at[:, pl.ds(1024, 128)], lambda q: a2d.at[q, :, pl.ds(256, 128)])

    spread_in.start()
    spread_out.start()
    small_slots = [w.slot() for _ in range(3)]
    for k in (1, 2, 3):
        w.copy(
            small_ref.at[:, cols(t)], sm_ref.at[:, cols(z)], small_slots[k - 1], p.line(p.around(k))
        ).start()
    sm_ref[:, cols(z)] = small_ref[:, cols(t)]

    @pl.loop(0, 16)
    def _(i):
        v = x_ref[rows16(i), :].astype(f32)
        s = lax.rsqrt(jnp.mean(v * v, axis=1, keepdims=True) + epsilon)
        n1[t, rows16(i), :] = (v * s * gain_ref[...]).astype(bf16)

    gather = PlaneGather(w, n1)
    gather.start()

    spread_in.wait()
    line_in = LineGather(
        w,
        [
            (lambda b, q: win.at[:, :, q, :, cols(b)], False),
            (lambda b, q: gg.at[:, b, :, q], False),
        ],
    )
    line_in.first()
    spread_out.wait()
    line_out = LineGather(w, [(lambda b, q: wout.at[:, q, :, cols(b)], False)])
    line_in.step(2)
    gather.forward()
    line_in.step(3)
    line_out.first()
    spread_g.start()
    odd_g.start()
    line_in.step(4)
    line_in.finish()
    kept = [w.here(win, win_out), w.here(gg, gg_out)]
    gather.finish()
    kept.append(w.here(n1, n1_out))
    spread_ud.start()
    odd_u.start()
    odd_d.start()

    @pl.loop(0, 4)
    def _(j):
        xb[j, pl.ds(8, 256), :] = mm(n1[j], win[0].reshape(1536, 512))
        zy[j] = mm(n1[j], win[1].reshape(1536, 512))

    kept.append(w.here(zy, zy_out))
    halo = w.slot()

    @pl.when(z < 3)
    def _():
        w.copy(xb.at[:, pl.ds(256, 8)], xb.at[:, pl.ds(0, 8)], halo, p.line(z + 1)).start()

    @pl.when(z == 0)
    def _():
        xb[:, 0:8, :] = jnp.zeros((4, 8, 512), f32)

    line_out.step(2)
    spread_g.wait()
    odd_g.wait()
    line_g = LineGather(
        w,
        [
            (lambda b, q: wg_out.at[:, q, :, cols(b, 256)], False),
            (lambda b, q: wg_out.at[:, q, :, pl.ds(1024, 128)], True),
        ],
    )
    for k in (1, 2, 3):
        w.landed(sm_ref.at[:, cols(p.around(4 - k))], small_slots[k - 1])

    @pl.when(z > 0)
    def _():
        w.landed(xb.at[:, pl.ds(0, 8)], halo)

    @pl.loop(0, 4)
    def _(j):
        @pl.loop(0, 16)
        def _(i):
            v = xb[j, rows16(i, 24), :]
            total = sm_ref[4:5, :] + sm_ref[0:1, :] * v[8:24]
            for k in (1, 2, 3):
                total = total + sm_ref[k : k + 1, :] * v[8 - k : 24 - k]
            cc[j, rows16(i), :] = total.astype(bf16)

        for b in range(4):
            lanes = pl.ds(b * 128, 128)
            left = cc[j, :, lanes]
            zx[j, :, lanes] = mm(left, gg[0, b].reshape(128, 128)) + sm_ref[5:6, lanes]
            za[j, :, lanes] = mm(left, gg[1, b].reshape(128, 128)) + sm_ref[6:7, lanes]

    kept += [w.here(xb, xb_out), w.here(cc, c_out), w.here(zx, zx_out), w.here(za, za_out)]
    line_out.step(3)
    line_g.first()

    row = lax.broadcasted_iota(jnp.int32, (8, 512), 0)
    zero = jnp.zeros((8, 512), f32)

    def advance(i, carry):
        result = []
        for s in range(4):
            state, product = carry[s]
            pre_x, pre_a = zx[s, rows16(i), :], za[s, rows16(i), :]
            log_a = -8.0 * jax.nn.sigmoid(pre_a) * sm_ref[7:8, :]
            decay = jnp.exp(log_a)
            mult = jnp.sqrt(neg_expm1(2.0 * log_a))
            index = lax.broadcasted_iota(jnp.int32, (16, 512), 0) + i * 16 + z * 256
            mult = jnp.where(index == 0, 1.0, mult)
            inflow = mult * jax.nn.sigmoid(pre_x) * cc[s, rows16(i), :].astype(f32)
            aa[s, rows16(i), :] = decay
            for half in (0, 8):
                dv, uv = decay[half : half + 8], inflow[half : half + 8]
                for st in (1, 2, 4):
                    ok = row >= st
                    uv = uv + jnp.where(ok, dv * pltpu.roll(uv, st, 0), 0.0)
                    dv = jnp.where(ok, dv * pltpu.roll(dv, st, 0), dv)
                hv, pv = uv + dv * state, dv * product
                at = pl.ds(pl.multiple_of(i * 16 + half, 8), 8)
                hh[s, pl.ds(pl.multiple_of(i * 16 + half + 8, 8), 8), :] = hv
                ac[s, at, :] = pv
                state = jnp.broadcast_to(hv[7:8, :], (8, 512))
                product = jnp.broadcast_to(pv[7:8, :], (8, 512))
            result.append((state, product))
        return tuple(result)

    ends = lax.fori_loop(0, 16, advance, tuple((zero, zero + 1.0) for _ in range(4)))
    for s in range(4):
        tail[s, 0:8, :] = ends[s][0]
        tail[s, 8:16, :] = ends[s][1]

    base = [w.slot() for _ in range(3)]
    for away in (1, 2, 3):

        @pl.when(z + away <= 3)
        def _():
            w.copy(tail, sums.at[z], base[away - 1], p.line(z + away)).start()

    next_slot = w.slot()

    @pl.when(z > 0)
    def _():
        w.copy(aa.at[:, pl.ds(0, 8)], aa.at[:, pl.ds(256, 8)], next_slot, p.line(z - 1)).start()

    @pl.when(z == 3)
    def _():
        aa[:, 256:264, :] = jnp.zeros((4, 8, 512), f32)

    line_out.step(4)
    line_out.finish()
    kept.append(w.here(wout, wout_out))
    hin[...] = jnp.zeros((4, 8, 512), f32)
    for away in (1, 2, 3):

        @pl.when(z >= away)
        def _():
            w.landed(sums.at[z - away], base[away - 1])

    for src in range(3):

        @pl.when(z > src)
        def _():
            hin[...] = sums[src, :, 0:8, :] + sums[src, :, 8:16, :] * hin[...]

    line_g.step(2)

    @pl.loop(0, 4)
    def _(j):
        enter = hin[j]
        hh[j, 0:8, :] = enter
        first = jnp.concatenate([enter, enter], axis=0)

        @pl.loop(0, 16)
        def _(i):
            at = pl.ds(pl.multiple_of(i * 16 + 8, 8), 16)
            hv = hh[j, at, :] + ac[j, rows16(i), :] * first
            hh[j, at, :] = hv
            oo[j, rows16(i), :] = (hv * gelu_value(zy[j, rows16(i), :])).astype(bf16)

    kept += [w.here(hh, h_out), w.here(oo, o_out)]

    @pl.when(z < 3)
    def _():
        w.landed(aa.at[:, pl.ds(256, 8)], next_slot)

    kept.append(w.here(aa, a_out))

    def project(j):
        for n in range(2):
            part[j, :, n * 768 : (n + 1) * 768] = mm_nt(
                oo[j], wout[2 * n : 2 * n + 2].reshape(768, 512)
            ).astype(bf16)

    summed = PlaneSum(w, part, far, near)
    project(p.td)
    summed.diagonal()
    project(p.ty)
    project(p.tx)
    summed.to_y()
    summed.to_x()
    for n in range(2):
        own[:, n * 768 : (n + 1) * 768] = mm_nt(
            oo[t], wout[2 * n : 2 * n + 2].reshape(768, 512)
        )
    line_g.step(3)
    summed.finish()

    def last(i, carry):
        at = rows16(i)
        branch = own[at, :] + near[0, at, :].astype(f32) + near[1, at, :].astype(f32)
        stream = x_ref[at, :].astype(f32) + branch
        x1_ref[at, :] = stream
        s2, b2 = stream * stream, branch * branch
        return carry[0] + s2[0:8] + s2[8:16], carry[1] + b2[0:8] + b2[8:16]

    zw = jnp.zeros((8, 1536), f32)
    s2, b2 = lax.fori_loop(0, 16, last, (zw, zw))
    stat_ref[...] = zw
    stat_ref[0:1, :] = jnp.sum(s2, axis=0, keepdims=True)
    stat_ref[1:2, :] = jnp.sum(b2, axis=0, keepdims=True)
    sm_out[...] = sm_ref[...]

    line_g.step(4)
    line_g.finish()
    spread_ud.wait()
    odd_u.wait()
    odd_d.wait()
    for made in kept:
        made.wait()
    spread_in.drain()
    spread_out.drain()
    spread_g.drain()
    odd_g.drain()
    spread_ud.drain()
    odd_u.drain()
    odd_d.drain()
    for k in (1, 2, 3):
        w.sent(small_ref.at[:, cols(t)], small_slots[k - 1])
    gather.drain()
    line_in.drain()
    line_out.drain()
    line_g.drain()

    @pl.when(z < 3)
    def _():
        w.sent(xb.at[:, pl.ds(256, 8)], halo)

    for away in (1, 2, 3):

        @pl.when(z + away <= 3)
        def _():
            w.sent(tail, base[away - 1])

    @pl.when(z > 0)
    def _():
        w.sent(aa.at[:, pl.ds(0, 8)], next_slot)

    summed.drain()


def shape(dims, dtype):
    return jax.ShapeDtypeStruct(dims, dtype)


def call(kernel, number, args, spaces, outs, out_spaces, scratch, wires, locals_, name):
    v = pl.BlockSpec(memory_space=pltpu.VMEM)
    a = pl.BlockSpec(memory_space=pl.ANY)
    kinds = {"v": v, "a": a}
    return pl.pallas_call(
        kernel,
        out_shape=outs,
        in_specs=[kinds[k] for k in spaces],
        out_specs=[kinds[k] for k in out_spaces],
        scratch_shapes=list(scratch)
        + [
            pltpu.SemaphoreType.DMA((wires,)),
            pltpu.SemaphoreType.DMA((wires,)),
            pltpu.SemaphoreType.DMA((locals_,)),
        ],
        compiler_params=pltpu.CompilerParams(
            collective_id=number, has_side_effects=True, vmem_limit_bytes=VMEM_BYTES
        ),
        name=name,
    )(*args)


def forward_recurrence(x, g1, small, wx, wy, wo, gates, wg, wu, wd):
    V = pltpu.VMEM
    outs = [
        shape((256, 1536), f32), shape((8, 1536), f32), shape((16, 512), f32),
        shape((4, 256, 1536), bf16), shape((2, 4, 2, 192, 512), bf16), shape((4, 2, 192, 512), bf16),
        shape((4, 2, 192, 1152), bf16), shape((4, 192, 384), bf16), shape((4, 192, 384), bf16),
        shape((2, 4, 4, 2, 16, 128), bf16),
        shape((4, 264, 512), f32), shape((4, 256, 512), f32), shape((4, 256, 512), f32),
        shape((4, 256, 512), f32), shape((4, 256, 512), bf16), shape((4, 264, 512), f32),
        shape((4, 264, 512), f32), shape((4, 256, 512), bf16),
    ]
    scratch = [
        V((2, 4, 2, 192, 512), bf16), V((4, 2, 192, 512), bf16), V((2, 4, 4, 2, 16, 128), bf16),
        V((4, 256, 1536), bf16), V((4, 264, 512), f32), V((4, 256, 512), f32),
        V((4, 256, 512), f32), V((4, 256, 512), f32), V((4, 256, 512), bf16),
        V((4, 264, 512), f32), V((4, 264, 512), f32), V((4, 256, 512), f32),
        V((4, 256, 512), bf16), V((4, 256, 1536), bf16), V((2, 128, 1536), bf16),
        V((2, 256, 1536), bf16), V((256, 1536), f32),
        V((4, 16, 512), f32), V((4, 4, 16, 512), f32), V((4, 8, 512), f32), V((16, 512), f32),
    ]
    return call(
        recurrence_forward, 0, (x, g1, small, wx, wy, wo, gates, wg, wu, wd), "vvvaaaaaaa",
        outs, "vvv" + "a" * 15, scratch, 128, 32, "recurrence_forward",
    )


class OddScatter:
    def __init__(self, w, part, home):
        self.w, self.part, self.home = w, part, home
        self.slots = [w.slot() for _ in range(3)]
        self.kept = w.held_here(part(w.place.t), home)

    def start(self):
        p = self.w.place

        @pl.when(p.t == p.z)
        def _():
            self.kept.start()
            for peer, slot in zip(p.peers, self.slots):
                self.w.copy(self.part(peer), self.home, slot, p.plane(peer)).start()

    def finish(self):
        p = self.w.place
        for peer, slot in zip(p.peers, self.slots):

            @pl.when(peer == p.z)
            def _():
                self.w.landed(self.home, slot)

        @pl.when(p.t == p.z)
        def _():
            self.kept.wait()
            for peer, slot in zip(p.peers, self.slots):
                self.w.sent(self.part(peer), slot)


def cols(b, width=128):
    return pl.ds(pl.multiple_of(b * width, width), width)


def norm_rows(v):
    return lax.rsqrt(jnp.mean(v * v, axis=1, keepdims=True) + epsilon)


def feed_forward(
    x1_ref, gain_ref, cot, wg_in, a2u, a2d,
    dx1_ref, y_ref, stat_ref, half_out, gd_out,
    wg, wu, wd, n2, ct, gate, up, hid, dga, dup, part, far, near, far2, near2, own, own2,
    gdown, cb, landing, landing_odd, send, recv, local,
):
    p = Place()
    w = Wires(p, send, recv, local)
    t, c, z = p.t, p.c, p.z
    p.enter()
    odd = pl.ds(1024, 128)

    first = [
        w.here(a2u.at[:, :, pl.ds(0, 256)], wu.at[:, c, :, cols(z, 256)]),
        w.here(a2d.at[:, :, pl.ds(0, 256)], wd.at[:, c, :, cols(z, 256)]),
    ]
    first_odd = [
        w.held_here(a2u.at[:, :, pl.ds(256, 128)], wu.at[:, c, :, odd]),
        w.held_here(a2d.at[:, :, pl.ds(256, 128)], wd.at[:, c, :, odd]),
    ]

    @pl.when(t == z)
    def _():
        for made in first_odd:
            made.start()

    load_gate = w.here(wg_in, wg)
    load_cot = w.here(cot, ct.at[t])
    for made in first:
        made.wait()

    @pl.when(t == z)
    def _():
        for made in first_odd:
            made.wait()

    line_u = LineGather(
        w, [(lambda b, q: wu.at[:, q, :, cols(b, 256)], False), (lambda b, q: wu.at[:, q, :, odd], True)]
    )
    line_d = LineGather(
        w, [(lambda b, q: wd.at[:, q, :, cols(b, 256)], False), (lambda b, q: wd.at[:, q, :, odd], True)]
    )
    line_u.first()

    @pl.loop(0, 16)
    def _(i):
        v = x1_ref[rows16(i), :]
        n2[t, rows16(i), :] = (v * norm_rows(v) * gain_ref[...]).astype(bf16)

    gather = PlaneGather(w, n2)
    gather.start()
    load_gate.wait()

    def gate_rows(j):
        gate[j] = mm(n2[j], wg[...].reshape(1536, 1152))

    gate_rows(t)
    line_u.step(2)
    load_cot.wait()
    gather.forward()
    gather_cot = PlaneGather(w, ct)
    gather_cot.start()
    line_u.step(3)
    line_d.first()
    gate_rows(p.tx)
    gate_rows(p.ty)
    gather.finish()
    gate_rows(p.td)
    line_u.step(4)
    line_u.finish()

    @pl.loop(0, 4)
    def _(j):
        up[j] = mm(n2[j], wu[...].reshape(1536, 1152))

        @pl.loop(0, 16)
        def _(i):
            at = rows16(i)
            value, slope = gelu_pair(gate[j, at, :])
            u = up[j, at, :]
            hid[j, at, :] = (value * u).astype(bf16)
            gate[j, at, :] = value
            up[j, at, :] = u * slope

    line_d.step(2)
    gather_cot.forward()
    line_d.step(3)
    gather_cot.finish()

    def weight_grad(left, right, out):
        @pl.loop(0, 4)
        def _(i):
            lanes = cols(i, 384)
            out[i] = (
                mm_tn(left[:, :, lanes].reshape(1024, 384), right[...].reshape(1024, 1152))
                .astype(bf16)
                .reshape(2, 192, 1152)
            )

    weight_grad(ct, hid, gdown)
    core_d = CoreSum(w, lambda q: gdown.at[:, q], cb.at[0])
    core_d.start()
    line_d.step(4)
    line_d.finish()

    def grads_rows(j):
        dh = mm(ct[j], wd[...].reshape(1536, 1152))
        dga[j] = (dh * up[j]).astype(bf16)
        dup[j] = (dh * gate[j]).astype(bf16)

    def back_rows(j, n):
        wide = pl.ds(2 * n, 2)
        return mm_nt(dga[j], wg[wide].reshape(768, 1152)) + mm_nt(dup[j], wu[wide].reshape(768, 1152))

    def back(j):
        grads_rows(j)
        for n in range(2):
            part[j, :, n * 768 : (n + 1) * 768] = back_rows(j, n).astype(bf16)

    summed = PlaneSum(w, part, far, near)
    back(p.td)
    summed.diagonal()
    core_d.finish()
    line_sum = LineSum(
        w,
        [
            (lambda j: gdown.at[:, c, :, cols(j, 256)], lambda s, k: landing.at[s * 3 + k - 1], False),
            (lambda j: gdown.at[:, c, :, odd], lambda s, k: landing_odd.at[s], True),
        ],
    )
    line_sum.first()
    back(p.ty)
    summed.to_y()
    back(p.tx)
    summed.to_x()
    line_sum.step(2)
    grads_rows(t)
    for n in range(2):
        own[:, n * 768 : (n + 1) * 768] = back_rows(t, n)
    line_u.drain()
    line_d.drain()
    gather_cot.drain()

    def mid(j):
        for n in range(2):
            ct[j, :, n * 768 : (n + 1) * 768] = mm_nt(
                hid[j], wd[2 * n : 2 * n + 2].reshape(768, 1152)
            ).astype(bf16)

    branch = PlaneSum(w, ct, far2, near2)
    mid(p.td)
    branch.diagonal()
    mid(p.ty)
    branch.to_y()
    mid(p.tx)
    branch.to_x()
    for n in range(2):
        own2[:, n * 768 : (n + 1) * 768] = mm_nt(hid[t], wd[2 * n : 2 * n + 2].reshape(768, 1152))
    line_sum.step(3)
    weight_grad(n2, dga, wg)
    core_g = CoreSum(w, lambda q: wg.at[:, q], cb.at[1])
    core_g.start()
    weight_grad(n2, dup, wu)
    core_u = CoreSum(w, lambda q: wu.at[:, q], cb.at[2])
    core_u.start()
    core_g.finish()
    kept = [w.here(wg.at[:, c], half_out.at[0])]
    line_sum.step(4)
    down = Spread(
        w, [lambda q: gdown.at[q, c, :, cols(z, 256)]], [lambda q: gd_out.at[:, cols(q, 256)]]
    )
    down_odd = OddScatter(w, lambda q: gdown.at[q, c, :, odd], gd_out.at[:, odd])
    summed.finish()

    def dx(i, carry):
        at = rows16(i)
        v = x1_ref[at, :]
        s = norm_rows(v)
        dn = own[at, :] + near[0, at, :].astype(f32) + near[1, at, :].astype(f32)
        q = gain_ref[...] * dn
        dx1_ref[at, :] = (
            ct[t, at, :].astype(f32) + s * q - v * (s * s * s * jnp.mean(q * v, axis=1, keepdims=True))
        )
        g2 = dn * v * s
        return carry + g2[0:8] + g2[8:16]

    zw = jnp.zeros((8, 1536), f32)
    g2 = lax.fori_loop(0, 16, dx, zw)
    core_u.finish()
    kept.append(w.here(wu.at[:, c], half_out.at[1]))
    down.start()
    down_odd.start()
    branch.finish()

    def last(i, carry):
        at = rows16(i)
        m = own2[at, :] + near2[0, at, :].astype(f32) + near2[1, at, :].astype(f32)
        y = x1_ref[at, :] + m
        y_ref[at, :] = y.astype(bf16)
        m2, y2 = m * m, y * y
        return carry[0] + m2[0:8] + m2[8:16], carry[1] + y2[0:8] + y2[8:16]

    m2, y2 = lax.fori_loop(0, 16, last, (zw, zw))
    stat_ref[...] = zw
    stat_ref[2:3, :] = jnp.sum(m2, axis=0, keepdims=True)
    stat_ref[3:4, :] = jnp.sum(y2, axis=0, keepdims=True)
    stat_ref[4:5, :] = jnp.sum(g2, axis=0, keepdims=True)
    down.wait()
    down_odd.finish()
    down.drain()
    for made in kept:
        made.wait()
    gather.drain()
    summed.drain()
    branch.drain()
    line_sum.drain()
    core_d.drain()
    core_g.drain()
    core_u.drain()


def recurrence_backward(
    x_ref, gain_ref, dx1_ref, sm_ref, stat1, stat2,
    win_in, wout_in, n1_in, xb_in, zy_in, zx_in, za_in, c_in, a_in, h_in, o_in, gg_in, half_in,
    gi_ref, v1_ref, v2_ref, gin_out, gout_out, gff_out, ggate_out,
    win, wout, n1, dr, xb, zy, zx, za, cc, aa, hh, oo, gg, hgu, tmp, bc, dzy, dzx, dza,
    part, far, near, own, gin, gout, ggr, cbi, cbo, cbg, land_i, land_o, land_g, land_f, land_fo,
    tail, sums, gnext, acc8, v1, v2, v1c, v2c, v1z, v2z, send, recv, local,
):
    p = Place()
    w = Wires(p, send, recv, local)
    t, c, z = p.t, p.c, p.z
    p.enter()
    odd = pl.ds(1024, 128)

    load_half = w.here(half_in, hgu)
    load_out = w.here(wout_in, wout)
    early = [w.here(a, b) for a, b in ((zy_in, zy), (h_in, hh), (a_in, aa))]
    later = [
        w.here(a, b)
        for a, b in (
            (zx_in, zx), (za_in, za), (c_in, cc), (gg_in, gg), (o_in, oo), (xb_in, xb), (n1_in, n1), (win_in, win),
        )
    ]

    @pl.loop(0, 16)
    def _(i):
        dr[t, rows16(i), :] = dx1_ref[rows16(i), :].astype(bf16)

    gather = PlaneGather(w, dr)
    gather.start()
    line_f = LineSum(
        w,
        [
            (lambda j: hgu.at[:, :, :, cols(j, 256)], lambda s, k: land_f.at[s * 3 + k - 1], False),
            (lambda j: hgu.at[:, :, :, odd], lambda s, k: land_fo.at[s], True),
        ],
    )
    load_half.wait()
    line_f.first()
    load_out.wait()
    for made in early:
        made.wait()

    row = lax.broadcasted_iota(jnp.int32, (8, 512), 0)
    zero = jnp.zeros((8, 512), f32)

    def scan_rows(j):
        tmp[...] = mm(dr[j], wout[...].reshape(1536, 512))

        def step(k, carry):
            i = 15 - k
            state, product = carry
            at = rows16(i)
            value, slope = gelu_pair(zy[j, at, :])
            do = tmp[at, :]
            h = hh[j, pl.ds(pl.multiple_of(i * 16 + 8, 8), 16), :]
            dzy[j, at, :] = (do * h * slope).astype(bf16)
            flow = do * value
            follow = aa[j, rows16(i, 24), :][1:17]
            for half in (8, 0):
                uv, dv = flow[half : half + 8], follow[half : half + 8]
                for st in (1, 2, 4):
                    ok = row < 8 - st
                    uv = uv + jnp.where(ok, dv * pltpu.roll(uv, 8 - st, 0), 0.0)
                    dv = jnp.where(ok, dv * pltpu.roll(dv, 8 - st, 0), dv)
                gv, pv = uv + dv * state, dv * product
                here = pl.ds(pl.multiple_of(i * 16 + half, 8), 8)
                zy[j, here, :] = gv
                bc[j, here, :] = pv
                state = jnp.broadcast_to(gv[0:1, :], (8, 512))
                product = jnp.broadcast_to(pv[0:1, :], (8, 512))
            return state, product

        state, product = lax.fori_loop(0, 16, step, (zero, zero + 1.0))
        tail[j, 0:8, :] = state
        tail[j, 8:16, :] = product

    scan_rows(t)
    gather.forward()
    scan_rows(p.tx)
    scan_rows(p.ty)
    gather.finish()
    scan_rows(p.td)
    line_f.step(2)

    base = [w.slot() for _ in range(3)]
    for away in (1, 2, 3):

        @pl.when(z >= away)
        def _():
            w.copy(tail, sums.at[z], base[away - 1], p.line(z - away)).start()

    for made in later:
        made.wait()

    def out_grad():
        @pl.loop(0, 4)
        def _(i):
            gout[i] = (
                mm_tn(dr[:, :, cols(i, 384)].reshape(1024, 384), oo[...].reshape(1024, 512))
                .astype(bf16)
                .reshape(2, 192, 512)
            )

    out_grad()
    core_o = CoreSum(w, lambda q: gout.at[:, q], cbo)
    core_o.start()

    gnext[...] = jnp.zeros((4, 8, 512), f32)
    for away in (1, 2, 3):

        @pl.when(z + away <= 3)
        def _():
            w.landed(sums.at[z + away], base[away - 1])

    for src in (3, 2, 1):

        @pl.when(z < src)
        def _():
            gnext[...] = sums[src, :, 0:8, :] + sums[src, :, 8:16, :] * gnext[...]

    def through(j, carry):
        after = jnp.concatenate([gnext[j], gnext[j]], axis=0)

        def step(i, carry):
            sum_x, sum_a, sum_d = carry
            at = rows16(i)
            g = zy[j, at, :] + bc[j, at, :] * after
            before = hh[j, rows16(i, 24), :][7:23]
            pre_x, pre_a, value = zx[j, at, :], za[j, at, :], cc[j, at, :].astype(f32)
            rate = jax.nn.sigmoid(pre_a)
            entry = jax.nn.sigmoid(pre_x)
            log_a = -8.0 * rate * sm_ref[7:8, :]
            decay = aa[j, at, :]
            index = lax.broadcasted_iota(jnp.int32, (16, 512), 0) + i * 16 + z * 256
            start = index == 0
            mult = jnp.where(start, 1.0, jnp.sqrt(neg_expm1(2.0 * log_a)))
            gm = g * mult
            d_entry = gm * value
            bc[j, at, :] = gm * entry
            low_x = (d_entry * entry * (1.0 - entry)).astype(bf16)
            dzx[j, at, :] = low_x
            d_mult = g * entry * value
            d_log = g * before * decay - jnp.where(start, 0.0, d_mult * decay * decay / mult)
            low_a = (d_log * (-8.0 * sm_ref[7:8, :]) * rate * (1.0 - rate)).astype(bf16)
            dza[j, at, :] = low_a
            wide_x, wide_a, d_decay = low_x.astype(f32), low_a.astype(f32), d_log * rate
            return (
                sum_x + wide_x[0:8] + wide_x[8:16],
                sum_a + wide_a[0:8] + wide_a[8:16],
                sum_d + d_decay[0:8] + d_decay[8:16],
            )

        carry = lax.fori_loop(0, 16, step, carry)
        for b in range(4):
            lanes = pl.ds(b * 128, 128)
            bc[j, pl.ds(0, 256), lanes] += mm_nt(
                dzx[j, :, lanes], gg[0, b].reshape(128, 128)
            ) + mm_nt(dza[j, :, lanes], gg[1, b].reshape(128, 128))
        return carry

    sum_x, sum_a, sum_d = lax.fori_loop(0, 4, through, (zero, zero, zero))
    acc8[5:6, :] = jnp.sum(sum_x, axis=0, keepdims=True)
    acc8[6:7, :] = jnp.sum(sum_a, axis=0, keepdims=True)
    acc8[7:8, :] = -8.0 * sm_ref[8:9, :] * jnp.sum(sum_d, axis=0, keepdims=True)

    halo = w.slot()

    @pl.when(z > 0)
    def _():
        w.copy(bc.at[:, pl.ds(0, 8)], bc.at[:, pl.ds(256, 8)], halo, p.line(z - 1)).start()

    @pl.when(z == 3)
    def _():
        bc[:, 256:264, :] = jnp.zeros((4, 8, 512), f32)

    line_f.step(3)
    core_o.finish()
    line_o = LineSum(w, [(lambda j: gout.at[:, c, :, cols(j)], lambda s, k: land_o.at[s * 3 + k - 1], False)])

    for b in range(4):
        lanes = pl.ds(b * 128, 128)
        left = cc[:, :, lanes].reshape(1024, 128)
        for i, right in ((0, dzx), (1, dza)):
            ggr[i, b] = (
                mm_tn(left, right[:, :, lanes].reshape(1024, 128)).astype(bf16).reshape(4, 2, 16, 128)
            )

    @pl.when(z < 3)
    def _():
        w.landed(bc.at[:, pl.ds(256, 8)], halo)

    def taps(j, carry):
        def step(i, carry):
            at = rows16(i)
            v = bc[j, rows16(i, 24), :]
            xv = xb[j, rows16(i, 24), :]
            total = sm_ref[0:1, :] * v[0:16]
            for k in (1, 2, 3):
                total = total + sm_ref[k : k + 1, :] * v[k : k + 16]
            cc[j, at, :] = total.astype(bf16)
            now = v[0:16]
            new = []
            for k in range(4):
                product = now * xv[8 - k : 24 - k]
                new.append(carry[k] + product[0:8] + product[8:16])
            new.append(carry[4] + now[0:8] + now[8:16])
            return tuple(new)

        return lax.fori_loop(0, 16, step, carry)

    tap_sums = lax.fori_loop(0, 4, taps, (zero,) * 5)
    for k in range(5):
        acc8[k : k + 1, :] = jnp.sum(tap_sums[k], axis=0, keepdims=True)

    def back_rows(j, n):
        wide = pl.ds(2 * n, 2)
        return mm_nt(cc[j], win[0, wide].reshape(768, 512)) + mm_nt(dzy[j], win[1, wide].reshape(768, 512))

    def back(j):
        for n in range(2):
            part[j, :, n * 768 : (n + 1) * 768] = back_rows(j, n).astype(bf16)

    summed = PlaneSum(w, part, far, near)
    back(p.td)
    summed.diagonal()

    @pl.loop(0, 4)
    def _(i):
        left = n1[:, :, cols(i, 384)].reshape(1024, 384)
        gin[0, i] = mm_tn(left, cc[...].reshape(1024, 512)).astype(bf16).reshape(2, 192, 512)
        gin[1, i] = mm_tn(left, dzy[...].reshape(1024, 512)).astype(bf16).reshape(2, 192, 512)

    core_i = CoreSum(w, lambda q: gin.at[:, :, q], cbi)
    core_i.start()
    core_g = CoreSum(w, lambda q: ggr.at[:, :, :, q], cbg)
    core_g.start()
    back(p.ty)
    summed.to_y()
    back(p.tx)
    summed.to_x()
    line_f.step(4)
    line_o.first()
    send_f = Spread(
        w,
        [lambda q: hgu.at[:, q, :, cols(z, 256)]],
        [lambda q: gff_out.at[:, :, cols(q, 256)]],
    )
    send_fo = OddScatter(w, lambda q: hgu.at[:, q, :, odd], gff_out.at[:, :, odd])
    core_i.finish()
    core_g.finish()
    line_i = LineSum(
        w,
        [
            (lambda j: gin.at[:, :, c, :, cols(j)], lambda s, k: land_i.at[s * 3 + k - 1], False),
            (lambda j: ggr.at[:, j, :, c], lambda s, k: land_g.at[s * 3 + k - 1], False),
        ],
    )
    line_i.first()
    for n in range(2):
        own[:, n * 768 : (n + 1) * 768] = back_rows(t, n)
    line_o.step(2)
    line_i.step(2)
    line_o.step(3)
    line_i.step(3)
    summed.finish()
    send_f.start()
    send_fo.start()

    def last(i, carry):
        at = rows16(i)
        v = x_ref[at, :].astype(f32)
        s = norm_rows(v)
        dn = own[at, :] + near[0, at, :].astype(f32) + near[1, at, :].astype(f32)
        q = gain_ref[...] * dn
        gi_ref[at, :] = (
            dx1_ref[at, :] + s * q - v * (s * s * s * jnp.mean(q * v, axis=1, keepdims=True))
        ).astype(bf16)
        g1 = dn * v * s
        return carry + g1[0:8] + g1[8:16]

    g1 = lax.fori_loop(0, 16, last, jnp.zeros((8, 1536), f32))
    v1[0] = stat1[...] + stat2[...]
    v1[0, 5:6, :] = jnp.sum(g1, axis=0, keepdims=True)
    v2[0] = jnp.zeros((32, 512), f32)
    v2[0, pl.ds(pl.multiple_of(t * 8, 8), 8), :] = acc8[...]
    stage_slots = [(w.slot(), w.slot()) for _ in range(3)]
    for n, device in enumerate((p.partner(), p.plane(p.tx), p.plane(p.ty))):
        s1, s2 = stage_slots[n]
        w.copy(v1.at[n], v1c.at[n], s1, device).start()
        w.copy(v2.at[n], v2c.at[n], s2, device).start()
        if n == 0:
            line_o.step(4)
            send_o = Spread(w, [lambda q: gout.at[q, c, :, cols(z)]], [lambda q: gout_out.at[:, cols(q)]])
            send_o.start()
        if n == 1:
            line_i.step(4)
            send_i = Spread(
                w,
                [lambda q: gin.at[:, q, c, :, cols(z)], lambda q: ggr.at[:, z, q, c]],
                [lambda q: gin_out.at[:, :, cols(q)], lambda q: ggate_out.at[:, q]],
            )
            send_i.start()
        w.landed(v1c.at[n], s1)
        w.landed(v2c.at[n], s2)
        v1[n + 1] = v1[n] + v1c[n]
        v2[n + 1] = v2[n] + v2c[n]
    line_slots = [(w.slot(), w.slot()) for _ in range(3)]
    for k in (1, 2, 3):
        s1, s2 = line_slots[k - 1]
        w.copy(v1.at[3], v1z.at[z], s1, p.line(p.around(k))).start()
        w.copy(v2.at[3], v2z.at[z], s2, p.line(p.around(k))).start()
    v1z[z] = v1[3]
    v2z[z] = v2[3]
    for k in (1, 2, 3):
        s1, s2 = line_slots[k - 1]
        w.landed(v1z.at[p.around(4 - k)], s1)
        w.landed(v2z.at[p.around(4 - k)], s2)
    v1_ref[...] = v1z[0] + v1z[1] + v1z[2] + v1z[3]
    v2_ref[...] = v2z[0] + v2z[1] + v2z[2] + v2z[3]

    send_f.wait()
    send_fo.finish()
    send_o.wait()
    send_i.wait()
    send_f.drain()
    send_o.drain()
    send_i.drain()
    for n in range(3):
        s1, s2 = stage_slots[n]
        w.sent(v1.at[n], s1)
        w.sent(v2.at[n], s2)
        s1, s2 = line_slots[n]
        w.sent(v1.at[3], s1)
        w.sent(v2.at[3], s2)
    gather.drain()
    summed.drain()
    line_f.drain()
    line_o.drain()
    line_i.drain()
    core_o.drain()
    core_i.drain()
    core_g.drain()

    for away in (1, 2, 3):

        @pl.when(z >= away)
        def _():
            w.sent(tail, base[away - 1])

    @pl.when(z > 0)
    def _():
        w.sent(bc.at[:, pl.ds(0, 8)], halo)


def forward_backward_ff(x1, g2, cot, wg, a2u, a2d):
    V = pltpu.VMEM
    outs = [
        shape((256, 1536), f32), shape((256, 1536), bf16), shape((8, 1536), f32),
        shape((2, 4, 192, 1152), bf16), shape((192, 1152), bf16),
    ]
    weights = V((4, 2, 192, 1152), bf16)
    tokens = V((4, 256, 1536), bf16)
    hidden, hidden_low = V((4, 256, 1152), f32), V((4, 256, 1152), bf16)
    far, near, own = V((2, 128, 1536), bf16), V((2, 256, 1536), bf16), V((256, 1536), f32)
    scratch = [
        weights, weights, weights, tokens, tokens, hidden, hidden, hidden_low, hidden_low, hidden_low,
        tokens, far, near, far, near, own, own, weights, V((3, 4, 192, 1152), bf16),
        V((6, 4, 192, 256), bf16), V((2, 4, 192, 128), bf16),
    ]
    return call(
        feed_forward, 1, (x1, g2, cot, wg, a2u, a2d), "vvaaaa", outs, "vvvaa", scratch, 128, 24, "feed_forward"
    )


def backward_recurrence(x, g1, dx1, sm, stat1, stat2, *saved):
    V = pltpu.VMEM
    outs = [
        shape((256, 1536), bf16), shape((8, 1536), f32), shape((32, 512), f32),
        shape((2, 192, 512), bf16), shape((192, 512), bf16), shape((2, 192, 1152), bf16), shape((2, 4, 16, 128), bf16),
    ]
    tokens = V((4, 256, 1536), bf16)
    wide, padded, low = V((4, 256, 512), f32), V((4, 264, 512), f32), V((4, 256, 512), bf16)
    scratch = [
        V((2, 4, 2, 192, 512), bf16), V((4, 2, 192, 512), bf16), tokens, tokens, padded, wide, wide, wide, low,
        padded, padded, low, V((2, 4, 4, 2, 16, 128), bf16), V((2, 4, 192, 1152), bf16), V((256, 512), f32),
        padded, low, low, low,
        tokens, V((2, 128, 1536), bf16), V((2, 256, 1536), bf16), V((256, 1536), f32),
        V((2, 4, 2, 192, 512), bf16), V((4, 2, 192, 512), bf16), V((2, 4, 4, 2, 16, 128), bf16),
        V((2, 4, 192, 512), bf16), V((4, 192, 512), bf16), V((2, 4, 4, 16, 128), bf16),
        V((6, 2, 4, 192, 128), bf16), V((6, 4, 192, 128), bf16), V((6, 2, 4, 16, 128), bf16),
        V((6, 2, 4, 192, 256), bf16), V((2, 2, 4, 192, 128), bf16),
        V((4, 16, 512), f32), V((4, 4, 16, 512), f32), V((4, 8, 512), f32), V((8, 512), f32),
        V((4, 8, 1536), f32), V((4, 32, 512), f32), V((3, 8, 1536), f32), V((3, 32, 512), f32),
        V((4, 8, 1536), f32), V((4, 32, 512), f32),
    ]
    return call(
        recurrence_backward, 2, (x, g1, dx1, sm, stat1, stat2) + saved, "vvvvvv" + "a" * 13,
        outs, "vvvaaaa", scratch, 160, 24, "recurrence_backward",
    )


def fast_local(
    inputs, norm1_gain, w_in_x, w_in_y, conv_w, conv_b, gates, gate_bias, decay_param, w_out,
    norm2_gain, w_gate, w_up, w_down, cotangent,
):
    channels = conv_b.shape[0]
    small = jnp.concatenate(
        [
            conv_w, conv_b[None], gate_bias, jax.nn.softplus(decay_param)[None],
            jax.nn.sigmoid(decay_param)[None], jnp.zeros((7, channels), f32),
        ],
        axis=0,
    )
    g1, g2 = norm1_gain[None], norm2_gain[None]
    (x1, stat1, sm, n1, win, wout, wg, a2u, a2d, gg, xb, zy, zx, za, cc, aa, hh, oo) = forward_recurrence(
        inputs, g1, small, w_in_x, w_in_y, w_out, gates, w_gate, w_up, w_down
    )
    dx1, output, stat2, halves, gd = forward_backward_ff(x1, g2, cotangent, wg, a2u, a2d)
    gi, v1, v2, gin, gout, gff, ggate = backward_recurrence(
        inputs, g1, dx1, sm, stat1, stat2, win, wout, n1, xb, zy, zx, za, cc, aa, hh, oo, gg, halves
    )
    squares = jnp.sum(v1[0:4], axis=1)
    count = inputs.shape[0] * lax.axis_size("dp") * lax.axis_size("tensor") * inputs.shape[1]
    stream_rms = jnp.sqrt(squares / count)
    rows = v2.reshape(4, 8, 4, 128).transpose(1, 2, 0, 3).reshape(8, 4 * channels)
    return (
        output, gi, v1[5], gin[0].astype(f32), gin[1].astype(f32), rows[0:4], rows[4], ggate.astype(f32),
        rows[5:7], rows[7], gout.astype(f32), v1[4], gff[0].astype(f32), gff[1].astype(f32), gd.astype(f32),
        stream_rms,
    )


def solution(mesh):
    fits = mesh.shape["dp"] == 8 and mesh.shape["tensor"] == 4
    return jax.shard_map(
        fast_local if fits else local,
        mesh=mesh,
        in_specs=(
            P(("dp", "tensor"), None),
            P(),
            P("dp", "tensor"),
            P("dp", "tensor"),
            P(None, "tensor"),
            P("tensor"),
            P(None, "tensor", "dp", None),
            P(None, "tensor"),
            P("tensor"),
            P("dp", "tensor"),
            P(),
            P("dp", "tensor"),
            P("dp", "tensor"),
            P("dp", "tensor"),
            P(("dp", "tensor"), None),
        ),
        out_specs=(
            P(("dp", "tensor"), None),
            P(("dp", "tensor"), None),
            P(),
            P("dp", "tensor"),
            P("dp", "tensor"),
            P(),
            P(),
            P(None, "tensor", "dp", None),
            P(),
            P(),
            P("dp", "tensor"),
            P(),
            P("dp", "tensor"),
            P("dp", "tensor"),
            P("dp", "tensor"),
            P(),
        ),
        check_vma=False,
    )
```

```python
import functools

import jax
import jax.numpy as jnp
from jax import lax
from jax.experimental import pallas as pl
from jax.experimental.pallas import tpu as pltpu
from jax.sharding import PartitionSpec as P

CONV = 4
SEQ_LEN = 1024


epsilon = 1e-06


def gelu_tanh(value):
    return jax.nn.gelu(value, approximate=True)


def combine(earlier, later):
    return (earlier[0] * later[0], later[0] * earlier[1] + later[1])


def norm_back(value, scale, gain, grad):
    scaled = gain * grad
    return scale * scaled - value * scale * scale * scale * jnp.mean(
        scaled * value, axis=1, keepdims=True
    )


def row_product(left, right):
    return lax.dot_general(
        left, right, (((0,), (0,)), ((), ())), preferred_element_type=jnp.float32
    )


def back_product(left, right):
    return lax.dot_general(
        left, right, (((1,), (1,)), ((), ())), preferred_element_type=jnp.float32
    )


def local(
    inputs,
    norm1_gain,
    w_in_x,
    w_in_y,
    conv_w,
    conv_b,
    gates,
    gate_bias,
    decay_param,
    w_out,
    norm2_gain,
    w_gate,
    w_up,
    w_down,
    cotangent,
):
    row_count = inputs.shape[0]
    model_width = inputs.shape[1]
    tensor_count = lax.axis_size("tensor")
    group_rows = row_count * tensor_count
    seq_count = group_rows // SEQ_LEN
    rec_x, rec_y, rec_o, gate_mats = (
        lax.all_gather(w_in_x, "dp", axis=0, tiled=True),
        lax.all_gather(w_in_y, "dp", axis=0, tiled=True),
        lax.all_gather(w_out, "dp", axis=0, tiled=True),
        lax.all_gather(gates, "dp", axis=2, tiled=True),
    )
    channels = rec_x.shape[1]
    blocks_here = gate_mats.shape[1]
    block_width = gate_mats.shape[3]
    residual = inputs.astype(jnp.float32)
    scale_one = lax.rsqrt(jnp.mean(residual * residual, axis=1, keepdims=True) + epsilon)
    n_one = (residual * scale_one * norm1_gain).astype(jnp.bfloat16)
    full_one = lax.all_gather(n_one, "tensor", axis=0, tiled=True)
    x_branch = jnp.dot(full_one, rec_x, preferred_element_type=jnp.float32)
    y_pre = jnp.dot(full_one, rec_y, preferred_element_type=jnp.float32)
    seq_x = x_branch.reshape(seq_count, SEQ_LEN, channels)
    padded = jnp.pad(seq_x, ((0, 0), (CONV - 1, 0), (0, 0)))
    conv_sum = conv_b + jnp.zeros_like(seq_x)
    for k in range(CONV):
        conv_sum = conv_sum + conv_w[k] * padded[:, CONV - 1 - k : CONV - 1 - k + SEQ_LEN]
    conv_low = conv_sum.reshape(group_rows, channels).astype(jnp.bfloat16)
    conv_value = conv_low.astype(jnp.float32)
    blocked = conv_low.reshape(group_rows, blocks_here, block_width)
    z_input = (
        jnp.einsum(
            "gbi,bij->gbj", blocked, gate_mats[0], preferred_element_type=jnp.float32
        ).reshape(group_rows, channels)
        + gate_bias[0]
    )
    z_decay = (
        jnp.einsum(
            "gbi,bij->gbj", blocked, gate_mats[1], preferred_element_type=jnp.float32
        ).reshape(group_rows, channels)
        + gate_bias[1]
    )
    seq_start = (jnp.arange(group_rows) % SEQ_LEN == 0)[:, None]

    def coefficients(input_pre, decay_pre, conv_part, decay_raw):
        log_decay = -8.0 * jax.nn.sigmoid(decay_pre) * jax.nn.softplus(decay_raw)
        mult = jnp.where(seq_start, 1.0, jnp.sqrt(-jnp.expm1(2.0 * log_decay)))
        return (jnp.exp(log_decay), mult * jax.nn.sigmoid(input_pre) * conv_part)

    (decays, inflow), pull_coeff = jax.vjp(coefficients, z_input, z_decay, conv_value, decay_param)
    seq_decay = decays.reshape(seq_count, SEQ_LEN, channels)
    _, seq_states = lax.associative_scan(
        combine, (seq_decay, inflow.reshape(seq_count, SEQ_LEN, channels)), axis=1
    )
    states = seq_states.reshape(group_rows, channels)
    y_gate = gelu_tanh(y_pre)
    mixed_out = (states * y_gate).astype(jnp.bfloat16)
    branch = lax.psum_scatter(
        back_product(mixed_out, rec_o), "tensor", scatter_dimension=0, tiled=True
    )
    stream = residual + branch
    mlp_g, mlp_u, mlp_d = (
        lax.all_gather(w_gate, "dp", axis=0, tiled=True),
        lax.all_gather(w_up, "dp", axis=0, tiled=True),
        lax.all_gather(w_down, "dp", axis=0, tiled=True),
    )
    scale_two = lax.rsqrt(jnp.mean(stream * stream, axis=1, keepdims=True) + epsilon)
    n_two = (stream * scale_two * norm2_gain).astype(jnp.bfloat16)
    full_two = lax.all_gather(n_two, "tensor", axis=0, tiled=True)
    gate_pre = jnp.dot(full_two, mlp_g, preferred_element_type=jnp.float32)
    up_pre = jnp.dot(full_two, mlp_u, preferred_element_type=jnp.float32)
    hidden = (gelu_tanh(gate_pre) * up_pre).astype(jnp.bfloat16)
    ffn_out = lax.psum_scatter(
        back_product(hidden, mlp_d), "tensor", scatter_dimension=0, tiled=True
    )
    result = stream + ffn_out
    output = result.astype(jnp.bfloat16)
    squares = jnp.stack(
        [
            jnp.sum(stream * stream),
            jnp.sum(branch * branch),
            jnp.sum(ffn_out * ffn_out),
            jnp.sum(result * result),
        ]
    )
    upstream = cotangent.astype(jnp.float32)
    full_cot = lax.all_gather(cotangent, "tensor", axis=0, tiled=True)
    d_hidden = jnp.dot(full_cot, mlp_d, preferred_element_type=jnp.float32)
    grad_down = row_product(full_cot, hidden)
    _, pull_mlp = jax.vjp(
        lambda gate_value, up_value: gelu_tanh(gate_value) * up_value, gate_pre, up_pre
    )
    d_gate, d_up = pull_mlp(d_hidden)
    d_gate_low = d_gate.astype(jnp.bfloat16)
    d_up_low = d_up.astype(jnp.bfloat16)
    grad_gate_w = row_product(full_two, d_gate_low)
    grad_up_w = row_product(full_two, d_up_low)
    d_two = lax.psum_scatter(
        back_product(d_gate_low, mlp_g) + back_product(d_up_low, mlp_u),
        "tensor",
        scatter_dimension=0,
        tiled=True,
    )
    grad_gain_two = jnp.sum(d_two * stream * scale_two, axis=0)
    d_stream = upstream + norm_back(stream, scale_two, norm2_gain, d_two)
    mlp_summed = (grad_gate_w, grad_up_w, grad_down)
    full_branch = lax.all_gather(d_stream.astype(jnp.bfloat16), "tensor", axis=0, tiled=True)
    d_mixed = jnp.dot(full_branch, rec_o, preferred_element_type=jnp.float32)
    grad_out_w = row_product(full_branch, mixed_out)
    d_states = d_mixed * y_gate
    _, pull_gelu = jax.vjp(gelu_tanh, y_pre)
    d_y_low = pull_gelu(d_mixed * states)[0].astype(jnp.bfloat16)
    next_decay = jnp.concatenate([seq_decay[:, 1:], jnp.zeros_like(seq_decay[:, :1])], axis=1)
    _, carried = lax.associative_scan(
        combine, (next_decay, d_states.reshape(seq_count, SEQ_LEN, channels)), reverse=True, axis=1
    )
    prev_states = jnp.concatenate([jnp.zeros_like(seq_states[:, :1]), seq_states[:, :-1]], axis=1)
    d_decays = (carried * prev_states).reshape(group_rows, channels)
    d_input_pre, d_decay_pre, d_conv_direct, grad_decay = pull_coeff(
        (d_decays, carried.reshape(group_rows, channels))
    )
    d_input_low = d_input_pre.astype(jnp.bfloat16)
    d_decay_low = d_decay_pre.astype(jnp.bfloat16)
    grad_bias = jnp.stack(
        [
            jnp.sum(d_input_low, axis=0, dtype=jnp.float32),
            jnp.sum(d_decay_low, axis=0, dtype=jnp.float32),
        ]
    )
    input_blocks = d_input_low.reshape(group_rows, blocks_here, block_width)
    decay_blocks = d_decay_low.reshape(group_rows, blocks_here, block_width)
    grad_gate_mats = jnp.stack(
        [
            jnp.einsum("gbi,gbj->bij", blocked, input_blocks, preferred_element_type=jnp.float32),
            jnp.einsum("gbi,gbj->bij", blocked, decay_blocks, preferred_element_type=jnp.float32),
        ]
    )
    d_conv = d_conv_direct + jnp.einsum(
        "gbj,bij->gbi", input_blocks, gate_mats[0], preferred_element_type=jnp.float32
    ).reshape(group_rows, channels)
    d_conv = d_conv + jnp.einsum(
        "gbj,bij->gbi", decay_blocks, gate_mats[1], preferred_element_type=jnp.float32
    ).reshape(group_rows, channels)
    seq_dconv = d_conv.reshape(seq_count, SEQ_LEN, channels)
    grad_conv_b = jnp.sum(seq_dconv, axis=(0, 1))
    padded_back = jnp.pad(seq_dconv, ((0, 0), (0, CONV - 1), (0, 0)))
    tap_grads = []
    d_x_seq = jnp.zeros_like(seq_dconv)
    for k in range(CONV):
        tap_grads.append(
            jnp.sum(seq_dconv * padded[:, CONV - 1 - k : CONV - 1 - k + SEQ_LEN], axis=(0, 1))
        )
        d_x_seq = d_x_seq + conv_w[k] * padded_back[:, k : k + SEQ_LEN]
    grad_conv_w = jnp.stack(tap_grads)
    d_x_low = d_x_seq.reshape(group_rows, channels).astype(jnp.bfloat16)
    grad_in_x_w = row_product(full_one, d_x_low)
    grad_in_y_w = row_product(full_one, d_y_low)
    d_one = lax.psum_scatter(
        back_product(d_x_low, rec_x) + back_product(d_y_low, rec_y),
        "tensor",
        scatter_dimension=0,
        tiled=True,
    )
    grad_gain_one = jnp.sum(d_one * residual * scale_one, axis=0)
    grad_inputs = (d_stream + norm_back(residual, scale_one, norm1_gain, d_one)).astype(
        jnp.bfloat16
    )
    small_grads = jnp.concatenate(
        [grad_conv_w, grad_conv_b[None], grad_bias, grad_decay[None]], axis=0
    )
    spread_grads = lax.dynamic_update_slice(
        jnp.zeros((small_grads.shape[0], channels * tensor_count), jnp.float32),
        small_grads,
        (0, lax.axis_index("tensor") * channels),
    )
    gain_total, small_total, square_total = lax.psum(
        (jnp.stack([grad_gain_one, grad_gain_two]), spread_grads, squares), ("dp", "tensor")
    )
    stream_rms = jnp.sqrt(
        square_total / (row_count * lax.axis_size("dp") * tensor_count * model_width)
    )
    summed_all = (
        lax.psum_scatter(grad_in_x_w, "dp", scatter_dimension=0, tiled=True),
        lax.psum_scatter(grad_in_y_w, "dp", scatter_dimension=0, tiled=True),
        lax.psum_scatter(grad_out_w, "dp", scatter_dimension=0, tiled=True),
        lax.psum_scatter(grad_gate_mats, "dp", scatter_dimension=2, tiled=True),
        lax.psum_scatter(mlp_summed[0], "dp", scatter_dimension=0, tiled=True),
        lax.psum_scatter(mlp_summed[1], "dp", scatter_dimension=0, tiled=True),
        lax.psum_scatter(mlp_summed[2], "dp", scatter_dimension=0, tiled=True),
    )
    rec_summed = summed_all[:4]
    grad_gate_sum, grad_up_sum, grad_down_sum = (summed_all[4], summed_all[5], summed_all[6])
    return (
        output,
        grad_inputs,
        gain_total[0],
        rec_summed[0],
        rec_summed[1],
        small_total[0:CONV],
        small_total[CONV],
        rec_summed[3],
        small_total[CONV + 1 : CONV + 3],
        small_total[CONV + 3],
        rec_summed[2],
        gain_total[1],
        grad_gate_sum,
        grad_up_sum,
        grad_down_sum,
        stream_rms,
    )


MESH = pl.DeviceIdType.MESH
bf16 = jnp.bfloat16
f32 = jnp.float32
VMEM_BYTES = 67043328


def mm(a, b):
    return jnp.dot(a, b, preferred_element_type=f32)


def mm_nt(a, b):
    return lax.dot_general(a, b, (((1,), (1,)), ((), ())), preferred_element_type=f32)


def mm_tn(a, b):
    return lax.dot_general(a, b, (((0,), (0,)), ((), ())), preferred_element_type=f32)


def gelu_value(x):
    return 0.5 * x * (1.0 + jnp.tanh(0.7978845608028654 * x * (1.0 + 0.044715 * (x * x))))


def gelu_pair(x):
    x2 = x * x
    th = jnp.tanh(0.7978845608028654 * x * (1.0 + 0.044715 * x2))
    cdf = 0.5 * (1.0 + th)
    slope = 0.5 * x * (1.0 - th * th) * (0.7978845608028654 * (1.0 + 0.134145 * x2))
    return x * cdf, cdf + slope


def one_minus_square(x, decay):
    series = x * (
        1.0
        + x * (0.5 + x * (1 / 6 + x * (1 / 24 + x * (1 / 120 + x * (1 / 720 + x * (1 / 5040))))))
    )
    return jnp.where(x > -0.35, -series, 1.0 - decay * decay)


class Place:
    def __init__(self):
        self.d = lax.axis_index("dp")
        self.z = lax.axis_index("tensor")
        self.t = lax.div(self.d, 2)
        self.c = lax.rem(self.d, 2)
        self.tx = self.t + 1 - 2 * lax.rem(self.t, 2)
        self.ty = self.t + 2 - 4 * lax.div(self.t, 2)
        self.td = 3 - self.t
        self.peers = (self.tx, self.ty, self.td)

    def member(self, r):
        x, y = lax.rem(self.t, 2), lax.div(self.t, 2)
        b, e = lax.rem(r, 2), lax.div(r, 2)
        return x + b - 2 * x * b + 2 * (y + e - 2 * y * e)

    def plane(self, t):
        return (2 * t + self.c, self.z)

    def line(self, z):
        return (self.d, z)

    def partner(self):
        return (2 * self.t + 1 - self.c, self.z)

    def around(self, k):
        return lax.rem(self.z + k, 4)

    def enter(self):
        barrier = pltpu.get_barrier_semaphore()
        targets = [self.plane(t) for t in self.peers] + [self.partner()]
        targets += [self.line(self.around(k)) for k in (1, 2, 3)]
        for target in targets:
            pl.semaphore_signal(barrier, inc=1, device_id=target, device_id_type=MESH)
        pl.semaphore_wait(barrier, len(targets))


class Wires:
    def __init__(self, place, send, recv, local):
        self.place, self.send, self.recv, self.local = place, send, recv, local
        self.used, self.used_local = 0, 0

    def slot(self):
        self.used += 1
        assert self.used <= self.send.shape[0]
        return self.used - 1

    def block(self, count):
        self.used += count
        assert self.used <= self.send.shape[0]
        return self.used - count

    def copy(self, src, dst, slot, device):
        return pltpu.make_async_remote_copy(
            src_ref=src,
            dst_ref=dst,
            send_sem=self.send.at[slot],
            recv_sem=self.recv.at[slot],
            device_id=device,
            device_id_type=MESH,
        )

    def landed(self, ref, slot):
        self.copy(ref, ref, slot, self.place.partner()).wait_recv()

    def sent(self, ref, slot):
        self.copy(ref, ref, slot, self.place.partner()).wait_send()

    def held_here(self, src, dst):
        self.used_local += 1
        assert self.used_local <= self.local.shape[0]
        return pltpu.make_async_copy(src, dst, self.local.at[self.used_local - 1])

    def here(self, src, dst):
        made = self.held_here(src, dst)
        made.start()
        return made


class Spread:
    def __init__(self, w, parts, homes):
        self.w, self.parts, self.homes = w, parts, homes
        self.slots = [[w.slot() for _ in range(3)] for _ in parts]
        self.first = w.used_local
        w.used_local += len(parts)

    def _kept(self, act):
        t = self.w.place.t
        for n, (part, home) in enumerate(zip(self.parts, self.homes)):
            act(pltpu.make_async_copy(part(t), home(t), self.w.local.at[self.first + n]))

    def start(self):
        p = self.w.place
        for part, home, slots in zip(self.parts, self.homes, self.slots):
            for peer, slot in zip(p.peers, slots):
                self.w.copy(part(peer), home(p.t), slot, p.plane(peer)).start()
        self._kept(lambda made: made.start())

    def wait(self):
        p = self.w.place
        self._kept(lambda made: made.wait())
        for home, slots in zip(self.homes, self.slots):
            for peer, slot in zip(p.peers, slots):
                self.w.landed(home(peer), slot)

    def drain(self):
        p = self.w.place
        for part, slots in zip(self.parts, self.slots):
            for peer, slot in zip(p.peers, slots):
                self.w.sent(part(peer), slot)


class OneSpread:
    def __init__(self, w, part, home):
        self.w, self.part, self.home = w, part, home
        self.slots = [w.slot() for _ in range(3)]
        self.kept = w.held_here(part, home(w.place.t))

    def start(self):
        p = self.w.place

        @pl.when(p.t == p.z)
        def _():
            self.kept.start()

        for peer, slot in zip(p.peers, self.slots):

            @pl.when(peer == p.z)
            def _():
                self.w.copy(self.part, self.home(p.t), slot, p.plane(peer)).start()

    def wait(self):
        p = self.w.place

        @pl.when(p.t == p.z)
        def _():
            self.kept.wait()
            for peer, slot in zip(p.peers, self.slots):
                self.w.landed(self.home(peer), slot)

    def drain(self):
        p = self.w.place
        for peer, slot in zip(p.peers, self.slots):

            @pl.when(peer == p.z)
            def _():
                self.w.sent(self.part, slot)


class LineGather:
    def __init__(self, w, regions):
        self.w, self.regions = w, regions
        self.slots = [
            {key: w.slot() for key in ["o", "r1", "r2", "r3", "l1", "l2", "l3"]
             + ["or1", "or2", "or3", "ol1", "ol2", "ol3"]}
            for _ in regions
        ]

    def _each(self, b, act, *conditions):
        p = self.w.place
        for (view, odd), slots in zip(self.regions, self.slots):
            terms = list(conditions) + ([b == p.t] if odd else [])
            if not terms:
                act(view, slots)
                continue
            ok = terms[0]
            for term in terms[1:]:
                ok = jnp.logical_and(ok, term)

            @pl.when(ok)
            def _():
                act(view, slots)

    def _start(self, view, b, slot, device):
        p = self.w.place
        self.w.copy(view(b, p.c), view(b, p.c), slot, device).start()

    def first(self):
        p = self.w.place
        z = p.z
        self._each(z, lambda v, s: self._start(v, z, s["r1"], p.line(z + 1)), z < 3)
        self._each(z, lambda v, s: self._start(v, z, s["l1"], p.line(z - 1)), z > 0)
        self._each(z, lambda v, s: self._start(v, z, s["o"], p.partner()))

    def step(self, k):
        p = self.w.place
        z = p.z
        for sign, left in ((1, "r"), (-1, "l")):
            b = z - sign * (k - 1)
            exists = b >= 0 if sign > 0 else b <= 3

            def take(v, s):
                self.w.landed(v(b, p.c), s[f"{left}{k - 1}"])
                self._start(v, b, s[f"o{left}{k - 1}"], p.partner())

            self._each(b, take, exists)
            if k < 4:
                more = z < 3 if sign > 0 else z > 0
                self._each(
                    b, lambda v, s: self._start(v, b, s[f"{left}{k}"], p.line(z + sign)), exists, more
                )

    def finish(self):
        p = self.w.place
        z = p.z
        other = 1 - p.c
        self._each(z, lambda v, s: self.w.landed(v(z, other), s["o"]))
        for k in (1, 2, 3):
            for sign, left in ((1, "r"), (-1, "l")):
                b = z - sign * k
                exists = b >= 0 if sign > 0 else b <= 3
                self._each(b, lambda v, s: self.w.landed(v(b, other), s[f"o{left}{k}"]), exists)

    def drain(self):
        p = self.w.place
        z = p.z
        self._each(z, lambda v, s: self.w.sent(v(z, p.c), s["o"]))
        for k in (1, 2, 3):
            for sign, left in ((1, "r"), (-1, "l")):
                b = z - sign * k
                exists = b >= 0 if sign > 0 else b <= 3
                self._each(b, lambda v, s: self.w.sent(v(b, p.c), s[f"o{left}{k}"]), exists)
                b2 = z - sign * (k - 1)
                exists2 = b2 >= 0 if sign > 0 else b2 <= 3
                more = z < 3 if sign > 0 else z > 0
                self._each(b2, lambda v, s: self.w.sent(v(b2, p.c), s[f"{left}{k}"]), exists2, more)


class PlaneGather:
    def __init__(self, w, buf):
        self.w, self.buf = w, buf
        self.half = buf.shape[1] // 2
        self.s = {key: w.slot() for key in ("x", "y", "fx", "fy")}

    def _low(self, t):
        return self.buf.at[t, pl.ds(0, self.half)]

    def _high(self, t):
        return self.buf.at[t, pl.ds(self.half, self.half)]

    def start(self, own=None):
        p, w = self.w.place, self.w
        self.own = self.buf.at[p.t] if own is None else own
        w.copy(self.own, self.buf.at[p.t], self.s["x"], p.plane(p.tx)).start()
        w.copy(self.own, self.buf.at[p.t], self.s["y"], p.plane(p.ty)).start()

    def forward(self):
        p, w = self.w.place, self.w
        w.landed(self.buf.at[p.tx], self.s["x"])
        w.copy(self._high(p.tx), self._high(p.tx), self.s["fy"], p.plane(p.ty)).start()
        w.landed(self.buf.at[p.ty], self.s["y"])
        w.copy(self._low(p.ty), self._low(p.ty), self.s["fx"], p.plane(p.tx)).start()

    def finish(self):
        p, w = self.w.place, self.w
        w.landed(self._low(p.td), self.s["fx"])
        w.landed(self._high(p.td), self.s["fy"])

    def drain(self):
        p, w = self.w.place, self.w
        w.sent(self.own, self.s["x"])
        w.sent(self.own, self.s["y"])
        w.sent(self._high(p.tx), self.s["fy"])
        w.sent(self._low(p.ty), self.s["fx"])


class PlaneSum:
    def __init__(self, w, part, far, near):
        self.w, self.part, self.far, self.near = w, part, far, near
        self.half = part.shape[1] // 2
        self.s = {key: w.slot() for key in ("dx", "dy", "x", "y")}

    def diagonal(self):
        p, w, h = self.w.place, self.w, self.half
        self.a = self.part.at[p.td, pl.ds(0, h)]
        self.b = self.part.at[p.td, pl.ds(h, h)]
        w.copy(self.a, self.far.at[0], self.s["dx"], p.plane(p.tx)).start()
        w.copy(self.b, self.far.at[1], self.s["dy"], p.plane(p.ty)).start()

    def _add(self, t, which):
        h = self.half

        @pl.loop(0, h // 32)
        def _(i):
            rows = pl.ds(pl.multiple_of(i * 32, 32), 32)
            mine = pl.ds(pl.multiple_of(which * h + i * 32, 32), 32)
            total = self.part[t, mine, :].astype(f32) + self.far[which, rows, :].astype(f32)
            self.part[t, mine, :] = total.astype(bf16)

    def arrive(self):
        p = self.w.place
        self.w.landed(self.far.at[0], self.s["dx"])
        self._add(p.ty, 0)
        self.w.landed(self.far.at[1], self.s["dy"])
        self._add(p.tx, 1)

    def to_y(self):
        p, w = self.w.place, self.w
        w.copy(self.part.at[p.ty], self.near.at[1], self.s["y"], p.plane(p.ty)).start()

    def to_x(self):
        p, w = self.w.place, self.w
        w.copy(self.part.at[p.tx], self.near.at[0], self.s["x"], p.plane(p.tx)).start()

    def finish(self):
        self.w.landed(self.near.at[0], self.s["x"])
        self.w.landed(self.near.at[1], self.s["y"])

    def drain(self):
        p, w = self.w.place, self.w
        w.sent(self.a, self.s["dx"])
        w.sent(self.b, self.s["dy"])
        w.sent(self.part.at[p.ty], self.s["y"])
        w.sent(self.part.at[p.tx], self.s["x"])


def add_into(dst, *sources):
    lead, rows = dst.shape[:-2], dst.shape[-2]
    size = 64 if rows % 64 == 0 else rows
    count = rows // size
    total = count
    for n in lead:
        total *= n

    @pl.loop(0, total)
    def _(i):
        at = []
        rest = lax.div(i, count)
        for n in reversed(lead):
            at.insert(0, lax.rem(rest, n))
            rest = lax.div(rest, n)
        at.append(pl.ds(pl.multiple_of(lax.rem(i, count) * size, size), size))
        at = tuple(at)
        value = dst.at[at][...].astype(f32)
        for src in sources:
            value = value + src.at[at][...].astype(f32)
        dst.at[at][...] = value.astype(bf16)


class CoreSum:
    def __init__(self, w, half, landing):
        self.w, self.half, self.landing = w, half, landing
        self.slot = w.slot()

    def start(self):
        p = self.w.place
        self.w.copy(self.half(1 - p.c), self.landing, self.slot, p.partner()).start()

    def finish(self):
        self.w.landed(self.landing, self.slot)
        add_into(self.half(self.w.place.c), self.landing)

    def drain(self):
        self.w.sent(self.half(1 - self.w.place.c), self.slot)


class LineSum:
    def __init__(self, w, parts, odd=None):
        self.w, self.parts, self.odd = w, parts, odd
        self.slots = [[w.slot() for _ in range(6)] for _ in parts]
        if odd is not None:
            self.odd_slots = w.block(3)

    def _each(self, act, ok):
        @pl.when(ok)
        def _():
            for (piece, landing), slots in zip(self.parts, self.slots):
                act(piece, landing, slots)

    def _send(self, k, act, which):
        z = self.w.place.z
        for side, sign in ((0, 1), (1, -1)):
            j = z + sign * (4 - k)
            end = z == 0 if sign > 0 else z == 3
            inner = jnp.logical_and(z > 0, z < 3)
            there = j <= 3 if sign > 0 else j >= 0
            valid = end if which == "end" else jnp.logical_and(inner, there)
            self._each(lambda piece, landing, s: act(piece, landing, s[side * 3 + k - 1], side, k, j, sign), valid)

    def _out(self, piece, landing, slot, side, k, j, sign):
        p = self.w.place
        self.w.copy(piece(j), landing(side, k), slot, p.line(p.z + sign)).start()

    def first(self):
        p = self.w.place
        for k in (1, 2, 3):
            self._send(k, self._out, "end")
        if self.odd is not None:
            piece, landing = self.odd

            @pl.when(p.z != p.t)
            def _():
                k = lax.rem(p.t - p.z + 4, 4) - 1
                self.w.copy(piece, landing(k), self.odd_slots + k, p.line(p.t)).start()

    def _take(self, k):
        z = self.w.place.z
        for side, sign in ((0, 1), (1, -1)):
            j = z - sign + sign * (4 - k)
            valid = jnp.logical_and(j <= 3, z >= 1) if sign > 0 else jnp.logical_and(j >= 0, z <= 2)

            def act(piece, landing, s):
                self.w.landed(landing(side, k), s[side * 3 + k - 1])
                add_into(piece(j), landing(side, k))

            self._each(act, valid)

    def step(self, k):
        self._take(k - 1)
        if k < 4:
            self._send(k, self._out, "inner")
        elif self.odd is not None:
            p = self.w.place
            piece, landing = self.odd

            @pl.when(p.z == p.t)
            def _():
                for n in range(3):
                    self.w.landed(landing(n), self.odd_slots + n)
                add_into(piece, landing(0), landing(1), landing(2))

    def drain(self):
        p = self.w.place
        for k in (1, 2, 3):
            for which in ("end", "inner"):
                self._send(k, lambda piece, landing, slot, side, kk, j, sign: self.w.sent(piece(j), slot), which)
        if self.odd is not None:

            @pl.when(p.z != p.t)
            def _():
                self.w.sent(self.odd[0], self.odd_slots + lax.rem(p.t - p.z + 4, 4) - 1)


class SmallSum:
    def __init__(self, w, places, keep):
        self.w, self.places, self.keep = w, places, keep
        self.slots = [w.block(7) for _ in places]

    def line(self):
        p, w = self.w.place, self.w
        for (own, line, core, plane), s in zip(self.places, self.slots):
            line[p.z] = own[...]
            for k in (1, 2, 3):
                w.copy(own, line.at[p.z], s + k - 1, p.line(p.around(k))).start()

    def core(self):
        p, w = self.w.place, self.w
        for (own, line, core, plane), s in zip(self.places, self.slots):
            for k in (1, 2, 3):
                w.landed(line.at[p.around(4 - k)], s + k - 1)
            core[0] = line[0] + line[1] + line[2] + line[3]
            w.copy(core.at[0], core.at[1], s + 3, p.partner()).start()

    def plane(self):
        p, w = self.w.place, self.w
        for (own, line, core, plane), s in zip(self.places, self.slots):
            w.landed(core.at[1], s + 3)
            core[2] = core[0] + core[1]
            plane[p.t] = core[2]
            for n, peer in enumerate(p.peers):
                w.copy(core.at[2], plane.at[p.t], s + 4 + n, p.plane(peer)).start()

    def result(self):
        p, w = self.w.place, self.w
        values = []
        for (own, line, core, plane), s, keep in zip(self.places, self.slots, self.keep):
            for n, peer in enumerate(p.peers):
                w.landed(plane.at[peer], s + 4 + n)
            values.append(plane[...] if keep else plane[0] + plane[1] + plane[2] + plane[3])
        return values

    def drain(self):
        w = self.w
        for (own, line, core, plane), s in zip(self.places, self.slots):
            for k in (1, 2, 3):
                w.sent(own, s + k - 1)
                w.sent(core.at[2], s + 3 + k)
            w.sent(core.at[0], s + 3)


def stack_rows(v, out):
    for n in range(12):
        out[n : n + 1, :] = v[:, n * 128 : (n + 1) * 128]


class OddScatter:
    def __init__(self, w, part, home):
        self.w, self.part, self.home = w, part, home
        self.slots = [w.slot() for _ in range(3)]
        self.kept = w.held_here(part(w.place.t), home)

    def start(self):
        p = self.w.place

        @pl.when(p.t == p.z)
        def _():
            self.kept.start()
            for peer, slot in zip(p.peers, self.slots):
                self.w.copy(self.part(peer), self.home, slot, p.plane(peer)).start()

    def finish(self):
        p = self.w.place
        for peer, slot in zip(p.peers, self.slots):

            @pl.when(peer == p.z)
            def _():
                self.w.landed(self.home, slot)

        @pl.when(p.t == p.z)
        def _():
            self.kept.wait()
            for peer, slot in zip(p.peers, self.slots):
                self.w.sent(self.part(peer), slot)


def rows16(i, size=16):
    return pl.ds(pl.multiple_of(i * 16, 16), size)


def cols(b, width=128):
    return pl.ds(pl.multiple_of(b * width, width), width)


def norm_rows(v):
    return lax.rsqrt(jnp.mean(v * v, axis=1, keepdims=True) + epsilon)


def log1p_series(y):
    s = y / (2.0 + y)
    q = s * s
    total = 1.0 / 17
    for n in (15, 13, 11, 9, 7, 5, 3, 1):
        total = total * q + 1.0 / n
    return 2.0 * s * total


def turn(src, dst, j):
    @pl.loop(0, 12)
    def _(i):
        dst[cols(i), cols(j, 256)] = src[j, :, cols(i)].T


def fold(state, product):
    rows = [v[0:1, b * 128 : (b + 1) * 128] for v in (state, product) for b in range(4)]
    return jnp.concatenate(rows, axis=0)


def unfold(tile, first):
    return jnp.concatenate([jnp.broadcast_to(tile[first + b : first + b + 1, :], (8, 128)) for b in range(4)], axis=1)


def recurrence_forward(
    x_ref, gain_1d, conv_w, conv_b, gate_bias, decay, wx, wy, wo, gates, wg, wu, wd, cot,
    x1_ref, stat_ref, sm_out,
    n1t_out, win_out, wout_out, wg_out, wu_out, a2d, cot_out, gg_out,
    xb_out, zy_out, zx_out, za_out, c_out, a_out, h_out, o_out,
    win, wout, gg, n1, n1t, xb, zy, zx, za, cc, aa, hh, ac, oo, part, far, near,
    tail, sums, sm_ref, small_ref, gain_ref, send, recv, local,
):
    p = Place()
    w = Wires(p, send, recv, local)
    t, c, z = p.t, p.c, p.z
    odd = pl.ds(1024, 128)
    small_ref[...] = jnp.zeros((16, 512), f32)
    small_ref[0:4, :] = conv_w[...]
    small_ref[4:5, :] = conv_b[...].reshape(1, 512)
    small_ref[5:7, :] = gate_bias[...]
    raw = decay[...].reshape(1, 512)
    small_ref[7:8, :] = jnp.maximum(raw, 0.0) + log1p_series(jnp.exp(-jnp.abs(raw)))
    small_ref[8:9, :] = jax.nn.sigmoid(raw)
    gain_ref[...] = gain_1d[...].reshape(1, 1536)
    p.enter()

    spread_in = Spread(
        w,
        [lambda q: wx.at[:, cols(q)], lambda q: wy.at[:, cols(q)], lambda q: gates.at[:, q]],
        [
            lambda q: win.at[0, q, c, :, cols(z)],
            lambda q: win.at[1, q, c, :, cols(z)],
            lambda q: gg.at[:, z, q, c],
        ],
    )
    spread_out = Spread(w, [lambda q: wo.at[:, cols(q)]], [lambda q: wout.at[q, c, :, cols(z)]])

    def wide(weight, home, odd_home):
        return (
            Spread(w, [lambda q: weight.at[:, cols(q, 256)]], [home]),
            OneSpread(w, weight.at[:, odd], odd_home),
        )

    spreads = [
        wide(wg, lambda q: wg_out.at[q, c, :, cols(z, 256)], lambda q: wg_out.at[q, c, :, odd]),
        wide(wu, lambda q: wu_out.at[q, c, :, cols(z, 256)], lambda q: wu_out.at[q, c, :, odd]),
        wide(wd, lambda q: a2d.at[q, :, pl.ds(0, 256)], lambda q: a2d.at[q, :, pl.ds(256, 128)]),
    ]

    def wide_line(full):
        return LineGather(
            w, [(lambda b, q: full.at[:, q, :, cols(b, 256)], False), (lambda b, q: full.at[:, q, :, odd], True)]
        )

    line_in = LineGather(
        w, [(lambda b, q: win.at[:, :, q, :, cols(b)], False), (lambda b, q: gg.at[:, b, :, q], False)]
    )
    line_out = LineGather(w, [(lambda b, q: wout.at[:, q, :, cols(b)], False)])
    line_g, line_u = wide_line(wg_out), wide_line(wu_out)

    spread_in.start()
    small_slots = [w.slot() for _ in range(3)]
    for k in (1, 2, 3):
        w.copy(
            small_ref.at[:, cols(t)], sm_ref.at[:, cols(z)], small_slots[k - 1], p.line(p.around(k))
        ).start()
    sm_ref[:, cols(z)] = small_ref[:, cols(t)]

    @pl.loop(0, 16)
    def _(i):
        v = x_ref[rows16(i), :].astype(f32)
        n1[t, rows16(i), :] = (v * norm_rows(v) * gain_ref[...]).astype(bf16)

    gather = PlaneGather(w, n1)
    gather.start()
    spread_in.wait()
    line_in.first()
    turn(n1, n1t, t)
    line_in.step(2)
    gather.forward()
    spread_out.start()
    for part_spread in spreads[0] + spreads[1]:
        part_spread.start()
    turn(n1, n1t, p.tx)
    turn(n1, n1t, p.ty)
    line_in.step(3)
    spread_out.wait()
    line_out.first()
    line_in.step(4)
    line_in.finish()
    kept = [w.here(win, win_out), w.here(gg, gg_out)]
    gather.finish()
    gather_cot = PlaneGather(w, cot_out)
    gather_cot.start(cot)

    @pl.loop(0, 4)
    def _(j):
        xb[j, pl.ds(8, 256), :] = mm(n1[j], win[0].reshape(1536, 512))

    halo = w.slot()

    @pl.when(z < 3)
    def _():
        w.copy(xb.at[:, pl.ds(256, 8)], xb.at[:, pl.ds(0, 8)], halo, p.line(z + 1)).start()

    @pl.when(z == 0)
    def _():
        xb[:, 0:8, :] = jnp.zeros((4, 8, 512), f32)

    line_out.step(2)
    turn(n1, n1t, p.td)
    kept.append(w.here(n1t, n1t_out))
    for part_spread in spreads[0]:
        part_spread.wait()
    line_g.first()
    for k in (1, 2, 3):
        w.landed(sm_ref.at[:, cols(p.around(4 - k))], small_slots[k - 1])

    @pl.loop(0, 4)
    def _(j):
        zy[j] = mm(n1[j], win[1].reshape(1536, 512))

    line_out.step(3)
    kept.append(w.here(zy, zy_out))

    @pl.when(z > 0)
    def _():
        w.landed(xb.at[:, pl.ds(0, 8)], halo)

    row = lax.broadcasted_iota(jnp.int32, (8, 512), 0)
    zero = jnp.zeros((8, 512), f32)

    def convolve(j):
        @pl.loop(0, 16)
        def _(i):
            v = xb[j, rows16(i, 24), :]
            total = sm_ref[4:5, :] + sm_ref[0:1, :] * v[8:24]
            for k in (1, 2, 3):
                total = total + sm_ref[k : k + 1, :] * v[8 - k : 24 - k]
            cc[j, rows16(i), :] = total.astype(bf16)

        for b in range(4):
            lanes = pl.ds(b * 128, 128)
            left = cc[j, :, lanes]
            zx[j, :, lanes] = mm(left, gg[0, b].reshape(128, 128)) + sm_ref[5:6, lanes]
            za[j, :, lanes] = mm(left, gg[1, b].reshape(128, 128)) + sm_ref[6:7, lanes]

    def scan(j):
        def advance(i, carry):
            state, product = carry
            pre_x, pre_a = zx[j, rows16(i), :], za[j, rows16(i), :]
            rate, entry = jax.nn.sigmoid(pre_a), jax.nn.sigmoid(pre_x)
            zx[j, rows16(i), :] = entry
            za[j, rows16(i), :] = rate
            log_a = -8.0 * rate * sm_ref[7:8, :]
            decay = jnp.exp(log_a)
            mult = jnp.sqrt(one_minus_square(2.0 * log_a, decay))
            index = lax.broadcasted_iota(jnp.int32, (16, 512), 0) + i * 16 + z * 256
            mult = jnp.where(index == 0, 1.0, mult)
            inflow = mult * entry * cc[j, rows16(i), :].astype(f32)
            aa[j, rows16(i), :] = decay
            for half in (0, 8):
                dv, uv = decay[half : half + 8], inflow[half : half + 8]
                for st in (1, 2, 4):
                    ok = row >= st
                    uv = uv + jnp.where(ok, dv * pltpu.roll(uv, st, 0), 0.0)
                    dv = jnp.where(ok, dv * pltpu.roll(dv, st, 0), dv)
                hv, pv = uv + dv * state, dv * product
                hh[j, pl.ds(pl.multiple_of(i * 16 + half + 8, 8), 8), :] = hv
                ac[j, pl.ds(pl.multiple_of(i * 16 + half, 8), 8), :] = pv
                state = jnp.broadcast_to(hv[7:8, :], (8, 512))
                product = jnp.broadcast_to(pv[7:8, :], (8, 512))
            return state, product

        state, product = lax.fori_loop(0, 16, advance, (zero, zero + 1.0))
        tail[j] = fold(state, product)

    tail_slots = w.block(12)

    def tell(n, j):
        for away in (1, 2, 3):

            @pl.when(z + away <= 3)
            def _():
                w.copy(tail.at[j], sums.at[z, j], tail_slots + 3 * n + away - 1, p.line(z + away)).start()

    def settle(n, j):
        for away in (1, 2, 3):

            @pl.when(z >= away)
            def _():
                w.landed(sums.at[z - away, j], tail_slots + 3 * n + away - 1)

        enter = zero
        for src in range(3):
            tile = sums[src, j]
            enter = jnp.where(z > src, unfold(tile, 0) + unfold(tile, 4) * enter, enter)
        hh[j, 0:8, :] = enter
        first = jnp.concatenate([enter, enter], axis=0)

        @pl.loop(0, 16)
        def _(i):
            at = pl.ds(pl.multiple_of(i * 16 + 8, 8), 16)
            hv = hh[j, at, :] + ac[j, rows16(i), :] * first
            hh[j, at, :] = hv
            oo[j, rows16(i), :] = (hv * gelu_value(zy[j, rows16(i), :])).astype(bf16)

    def project(j):
        for n in range(2):
            part[j, :, n * 768 : (n + 1) * 768] = mm_nt(
                oo[j], wout[2 * n : 2 * n + 2].reshape(768, 512)
            ).astype(bf16)

    summed = PlaneSum(w, part, far, near)
    kept_out = w.held_here(wout, wout_out)

    @pl.loop(0, 5)
    def _(k):
        @pl.when(k < 4)
        def _():
            j = p.member(3 - k)
            convolve(j)
            scan(j)
            tell(k, j)

        @pl.when(k == 0)
        def _():
            line_out.step(4)
            line_g.step(2)
            for part_spread in spreads[1]:
                part_spread.wait()
            line_u.first()

        @pl.when(k == 1)
        def _():
            line_out.finish()
            kept_out.start()

        @pl.when(k == 2)
        def _():
            line_g.step(3)
            line_u.step(2)

        @pl.when(k == 3)
        def _():
            gather_cot.forward()

        @pl.when(k > 0)
        def _():
            j = p.member(4 - k)
            settle(k - 1, j)
            project(j)

        @pl.when(k == 1)
        def _():
            summed.diagonal()

        @pl.when(k == 3)
        def _():
            summed.arrive()
            summed.to_y()
            summed.to_x()

    for part_spread in spreads[2]:
        part_spread.start()
    kept += [w.here(xb, xb_out), w.here(cc, c_out), w.here(zx, zx_out), w.here(za, za_out)]
    kept += [kept_out, w.here(hh, h_out), w.here(oo, o_out)]
    next_slot = w.slot()

    @pl.when(z > 0)
    def _():
        w.copy(aa.at[:, pl.ds(0, 8)], aa.at[:, pl.ds(256, 8)], next_slot, p.line(z - 1)).start()

    @pl.when(z == 3)
    def _():
        aa[:, 256:264, :] = jnp.zeros((4, 8, 512), f32)

    line_g.step(4)
    line_u.step(3)

    @pl.when(z < 3)
    def _():
        w.landed(aa.at[:, pl.ds(256, 8)], next_slot)

    kept.append(w.here(aa, a_out))
    line_g.finish()
    gather_cot.finish()
    summed.finish()

    def last(i, carry):
        at = rows16(i)
        branch = part[t, at, :].astype(f32) + near[0, at, :].astype(f32) + near[1, at, :].astype(f32)
        stream = x_ref[at, :].astype(f32) + branch
        x1_ref[at, :] = stream
        s2, b2 = stream * stream, branch * branch
        return carry[0] + s2[0:8] + s2[8:16], carry[1] + b2[0:8] + b2[8:16]

    zw = jnp.zeros((8, 1536), f32)
    s2, b2 = lax.fori_loop(0, 16, last, (zw, zw))
    stat_ref[...] = zw
    stat_ref[0:1, :] = jnp.sum(s2, axis=0, keepdims=True)
    stat_ref[1:2, :] = jnp.sum(b2, axis=0, keepdims=True)
    sm_out[...] = sm_ref[...]
    line_u.step(4)
    line_u.finish()
    for part_spread in spreads[2]:
        part_spread.wait()
    for made in kept:
        made.wait()
    spread_in.drain()
    spread_out.drain()
    for pair in spreads:
        for part_spread in pair:
            part_spread.drain()
    for k in (1, 2, 3):
        w.sent(small_ref.at[:, cols(t)], small_slots[k - 1])
    gather.drain()
    gather_cot.drain()
    line_in.drain()
    line_out.drain()
    line_g.drain()
    line_u.drain()

    @pl.when(z < 3)
    def _():
        w.sent(xb.at[:, pl.ds(256, 8)], halo)

    for n in range(4):
        for away in (1, 2, 3):

            @pl.when(z + away <= 3)
            def _():
                w.sent(tail.at[n], tail_slots + 3 * n + away - 1)

    @pl.when(z > 0)
    def _():
        w.sent(aa.at[:, pl.ds(0, 8)], next_slot)

    summed.drain()


def shape(dims, dtype):
    return jax.ShapeDtypeStruct(dims, dtype)


def call(kernel, number, args, spaces, outs, out_spaces, scratch, wires, locals_, name):
    v = pl.BlockSpec(memory_space=pltpu.VMEM)
    a = pl.BlockSpec(memory_space=pl.ANY)
    kinds = {"v": v, "a": a}
    return pl.pallas_call(
        kernel,
        out_shape=outs,
        in_specs=[kinds[k] for k in spaces],
        out_specs=[kinds[k] for k in out_spaces],
        scratch_shapes=list(scratch)
        + [
            pltpu.SemaphoreType.DMA((wires,)),
            pltpu.SemaphoreType.DMA((wires,)),
            pltpu.SemaphoreType.DMA((locals_,)),
        ],
        compiler_params=pltpu.CompilerParams(
            collective_id=number, has_side_effects=True, vmem_limit_bytes=VMEM_BYTES
        ),
        name=name,
    )(*args)


def forward_recurrence(*args):
    V = pltpu.VMEM
    outs = [
        shape((256, 1536), f32), shape((8, 1536), f32), shape((16, 512), f32),
        shape((1536, 1024), bf16), shape((2, 4, 2, 192, 512), bf16), shape((4, 2, 192, 512), bf16),
        shape((4, 2, 192, 1152), bf16), shape((4, 2, 192, 1152), bf16), shape((4, 192, 384), bf16),
        shape((4, 256, 1536), bf16), shape((2, 4, 4, 2, 16, 128), bf16),
        shape((4, 264, 512), f32), shape((4, 256, 512), f32), shape((4, 256, 512), f32),
        shape((4, 256, 512), f32), shape((4, 256, 512), bf16), shape((4, 264, 512), f32),
        shape((4, 264, 512), f32), shape((4, 256, 512), bf16),
    ]
    scratch = [
        V((2, 4, 2, 192, 512), bf16), V((4, 2, 192, 512), bf16), V((2, 4, 4, 2, 16, 128), bf16),
        V((4, 256, 1536), bf16), V((1536, 1024), bf16), V((4, 264, 512), f32), V((4, 256, 512), f32),
        V((4, 256, 512), f32), V((4, 256, 512), f32), V((4, 256, 512), bf16),
        V((4, 264, 512), f32), V((4, 264, 512), f32), V((4, 256, 512), f32),
        V((4, 256, 512), bf16), V((4, 256, 1536), bf16), V((2, 128, 1536), bf16),
        V((2, 256, 1536), bf16),
        V((4, 8, 128), f32), V((4, 4, 8, 128), f32), V((16, 512), f32), V((16, 512), f32), V((1, 1536), f32),
    ]
    return call(
        recurrence_forward, 0, args, "v" * 6 + "a" * 8,
        outs, "vvv" + "a" * 16, scratch, 160, 32, "recurrence_forward",
    )


def half_line(w, piece, landing, odd_piece=None, odd_landing=None):
    odd = None if odd_piece is None else (odd_piece, lambda n: odd_landing.at[n])
    return LineSum(w, [(piece, lambda s, k: landing.at[s * 3 + k - 1])], odd)


def feed_forward(
    x1_ref, gain_1d, cot_ref, cot_in, wg_in, wu_in, a2d,
    dx1_ref, y_ref, stat_ref, half_out, piece_out,
    wgu, wd, n2, n2t, ct, ctt, gu, hid, dgu, part, far, near,
    gdown, cb, landing, landing_odd, gain_ref, send, recv, local,
):
    p = Place()
    w = Wires(p, send, recv, local)
    t, c, z = p.t, p.c, p.z
    gain_ref[...] = gain_1d[...].reshape(1, 1536)
    p.enter()
    odd = pl.ds(1024, 128)

    first = w.here(a2d.at[:, :, pl.ds(0, 256)], wd.at[:, c, :, cols(z, 256)])
    first_odd = w.held_here(a2d.at[:, :, pl.ds(256, 128)], wd.at[:, c, :, odd])

    @pl.when(t == z)
    def _():
        first_odd.start()

    load_gate, load_up = w.here(wg_in, wgu.at[0]), w.here(wu_in, wgu.at[1])
    load_cot = [w.here(cot_in.at[j], ct.at[j]) for j in p.peers]

    @pl.loop(0, 16)
    def _(i):
        at = rows16(i)
        v = x1_ref[at, :]
        n2[t, at, :] = (v * norm_rows(v) * gain_ref[...]).astype(bf16)
        ct[t, at, :] = cot_ref[at, :]

    gather = PlaneGather(w, n2)
    gather.start()
    first.wait()

    @pl.when(t == z)
    def _():
        first_odd.wait()

    line_d = LineGather(
        w, [(lambda b, q: wd.at[:, q, :, cols(b, 256)], False), (lambda b, q: wd.at[:, q, :, odd], True)]
    )
    line_d.first()
    load_gate.wait()
    load_up.wait()

    @pl.loop(0, 4)
    def _(k):
        @pl.when(k == 1)
        def _():
            for made in load_cot:
                made.wait()

            @pl.loop(0, 4)
            def _(n):
                turn(ct, ctt, n)

            line_d.step(2)
            gather.forward()
            line_d.step(3)

        @pl.when(k == 3)
        def _():
            gather.finish()

        j = p.member(k)

        @pl.loop(0, 2)
        def _(m):
            gu[m, j] = mm(n2[j], wgu[m].reshape(1536, 1152))

        @pl.loop(0, 16)
        def _(i):
            at = rows16(i)
            value, slope = gelu_pair(gu[0, j, at, :])
            u = gu[1, j, at, :]
            hid[j, at, :] = (value * u).astype(bf16)
            gu[0, j, at, :] = u * slope
            gu[1, j, at, :] = value

        @pl.when(k < 3)
        def _():
            turn(n2, n2t, j)

    line_d.step(4)
    line_d.finish()

    def weight_grad(left, right, out, first, count):
        @pl.loop(first, first + count)
        def _(i):
            out[i] = mm(left[cols(i, 384), :], right[...].reshape(1024, 1152)).astype(bf16).reshape(2, 192, 1152)

    def half_unit(home, u, n):
        return half_line(
            w,
            lambda j: home.at[pl.ds(2 * u, 2), c, :, cols(j, 256)],
            landing.at[n],
            home.at[pl.ds(2 * u, 2), c, :, odd],
            landing_odd.at[n],
        )

    units = [half_unit(gdown, 0, 0), half_unit(gdown, 1, 1), half_unit(wgu.at[0], 0, 2)]
    cores = [
        CoreSum(w, lambda q, u=u: gdown.at[pl.ds(2 * u, 2), q], cb.at[0, pl.ds(2 * u, 2)]) for u in range(2)
    ]
    cores_gu = [CoreSum(w, lambda q, m=m: wgu.at[m, :, q], cb.at[1 - m]) for m in range(2)]
    summed = PlaneSum(w, part, far, near)
    near_m = n2.at[pl.ds(0, 2)]
    branch = PlaneSum(w, ct, far, near_m)

    def mid(j):
        for n in range(2):
            ct[j, :, n * 768 : (n + 1) * 768] = mm_nt(
                hid[j], wd[2 * n : 2 * n + 2].reshape(768, 1152)
            ).astype(bf16)

    @pl.loop(0, 4)
    def _(k):
        j = p.member(3 - k)
        dh = mm(ct[j], wd[...].reshape(1536, 1152))
        for m in range(2):
            dgu[m, j] = (dh * gu[m, j]).astype(bf16)

        for n in range(2):
            span = pl.ds(2 * n, 2)
            part[j, :, n * 768 : (n + 1) * 768] = (
                mm_nt(dgu[0, j], wgu[0, span].reshape(768, 1152)) + mm_nt(dgu[1, j], wgu[1, span].reshape(768, 1152))
            ).astype(bf16)

        @pl.when(k == 0)
        def _():
            summed.diagonal()
            turn(n2, n2t, p.td)

        @pl.when(k == 1)
        def _():
            cores[0].finish()
            units[0].first()

        @pl.when(k == 2)
        def _():
            summed.arrive()
            summed.to_y()
            summed.to_x()
            cores[1].finish()
            units[1].first()

        @pl.when(k < 2)
        def _():
            weight_grad(ctt, hid, gdown, 2 * k, 2)

        @pl.when(k == 0)
        def _():
            cores[0].start()

        @pl.when(k == 1)
        def _():
            cores[1].start()

    units[0].step(2)

    @pl.loop(0, 2)
    def _(m):
        weight_grad(n2t, dgu.at[m], wgu.at[m], 0, 4)

        @pl.when(m == 0)
        def _():
            cores_gu[0].start()
            units[0].step(3)

        @pl.when(m == 1)
        def _():
            cores_gu[0].finish()
            cores_gu[1].start()
            units[2].first()

        for i in range(2):
            mid(p.member(3 - 2 * m - i))

    units[0].step(4)
    units[1].step(2)
    summed.finish()
    gather.drain()
    branch.diagonal()

    def dx(i, carry):
        at = rows16(i)
        v = x1_ref[at, :]
        s = norm_rows(v)
        dn = part[t, at, :].astype(f32) + near[0, at, :].astype(f32) + near[1, at, :].astype(f32)
        q = gain_ref[...] * dn
        dx1_ref[at, :] = (
            cot_ref[at, :].astype(f32) + s * q - v * (s * s * s * jnp.mean(q * v, axis=1, keepdims=True))
        )
        g2 = dn * v * s
        return carry + g2[0:8] + g2[8:16]

    zw = jnp.zeros((8, 1536), f32)
    g2 = lax.fori_loop(0, 16, dx, zw)
    stat_ref[...] = zw
    stat_ref[4:5, :] = jnp.sum(g2, axis=0, keepdims=True)
    units[1].step(3)
    cores_gu[1].finish()
    kept = [w.here(wgu.at[1, :, c], half_out.at[1])]
    branch.arrive()
    branch.to_y()
    branch.to_x()
    units[1].step(4)
    for src, dst in ((cols(z, 256), pl.ds(0, 256)), (odd, pl.ds(256, 128))):
        kept.append(w.here(gdown.at[:, c, :, src], piece_out.at[:, :, dst]))
    units[2].step(2)
    units[2].step(3)
    units[2].step(4)
    kept.append(w.here(wgu.at[0, :, c], half_out.at[0]))
    branch.finish()

    def last(i, carry):
        at = rows16(i)
        m = ct[t, at, :].astype(f32) + n2[0, at, :].astype(f32) + n2[1, at, :].astype(f32)
        y = x1_ref[at, :] + m
        y_ref[at, :] = y.astype(bf16)
        m2, y2 = m * m, y * y
        return carry[0] + m2[0:8] + m2[8:16], carry[1] + y2[0:8] + y2[8:16]

    m2, y2 = lax.fori_loop(0, 16, last, (zw, zw))
    stat_ref[2:3, :] = jnp.sum(m2, axis=0, keepdims=True)
    stat_ref[3:4, :] = jnp.sum(y2, axis=0, keepdims=True)
    for made in kept:
        made.wait()
    line_d.drain()
    summed.drain()
    branch.drain()
    for unit in units + cores + cores_gu:
        unit.drain()


def recurrence_backward(
    x_ref, gain_1d, dx1_ref, sm_ref, stat1, stat2,
    win_in, wout_in, n1t_in, xb_in, zy_in, zx_in, za_in, c_in, a_in, h_in, o_in, gg_in,
    half_in, piece_in,
    gi_ref, v1_ref, v2_ref, v3_ref, gin_out, gout_out, gff_out, gd_out, ggate_out,
    win, wout, n1t, dr, xb, zy, zx, za, cc, aa, hh, oo, gg, hgu, tmp, bc, dzy, dzx, dza,
    far, near, gin, gout, ggr, cbi, cbo, cbg, land_i, land_o, land_g, land_f, land_fo,
    tail, sums, acc8, early_own, late_own, acc8_l, acc8_c, acc8_p, early_l, early_c, early_p, late_l, late_c, late_p,
    gain_ref, acc, send, recv, local,
):
    p = Place()
    w = Wires(p, send, recv, local)
    t, c, z = p.t, p.c, p.z
    gain_ref[...] = gain_1d[...].reshape(1, 1536)
    p.enter()
    odd = pl.ds(1024, 128)

    load_half = w.here(half_in, hgu)
    load_out = w.here(wout_in, wout)
    early = [w.here(a, b) for a, b in ((zy_in, zy), (h_in, hh), (a_in, aa))]
    later = [
        w.here(a, b)
        for a, b in (
            (o_in, oo), (zx_in, zx), (za_in, za), (c_in, cc), (gg_in, gg), (n1t_in, n1t), (xb_in, xb), (win_in, win),
        )
    ]

    @pl.loop(0, 16)
    def _(i):
        dr[t, rows16(i), :] = dx1_ref[rows16(i), :].astype(bf16)

    gather = PlaneGather(w, dr)
    gather.start()
    units = [
        half_line(
            w,
            lambda j, m=m, u=u: hgu.at[m, pl.ds(2 * u, 2), :, cols(j, 256)],
            land_f.at[n],
            hgu.at[m, pl.ds(2 * u, 2), :, odd],
            land_fo.at[n],
        )
        for n, (m, u) in enumerate(((0, 1), (1, 0), (1, 1)))
    ]
    line_o = half_line(w, lambda j: gout.at[:, c, :, cols(j)], land_o)
    line_y = half_line(w, lambda j: gin.at[1, :, c, :, cols(j)], land_i.at[1])
    line_x = LineSum(
        w,
        [
            (lambda j: gin.at[0, :, c, :, cols(j)], lambda s, k: land_i.at[0, s * 3 + k - 1]),
            (lambda j: ggr.at[:, j, :, c], lambda s, k: land_g.at[s * 3 + k - 1]),
        ],
    )

    load_half.wait()
    for unit in units:
        unit.first()
    load_out.wait()
    for made in early:
        made.wait()

    row = lax.broadcasted_iota(jnp.int32, (8, 512), 0)
    zero = jnp.zeros((8, 512), f32)

    def scan_rows(j):
        tmp[...] = mm(dr[j], wout[...].reshape(1536, 512))

        def step(k, carry):
            i = 15 - k
            state, product = carry
            at = rows16(i)
            value, slope = gelu_pair(zy[j, at, :])
            do = tmp[at, :]
            h = hh[j, pl.ds(pl.multiple_of(i * 16 + 8, 8), 16), :]
            dzy[j, at, :] = (do * h * slope).astype(bf16)
            flow = do * value
            follow = aa[j, rows16(i, 24), :][1:17]
            for half in (8, 0):
                uv, dv = flow[half : half + 8], follow[half : half + 8]
                for st in (1, 2, 4):
                    ok = row < 8 - st
                    uv = uv + jnp.where(ok, dv * pltpu.roll(uv, 8 - st, 0), 0.0)
                    dv = jnp.where(ok, dv * pltpu.roll(dv, 8 - st, 0), dv)
                gv, pv = uv + dv * state, dv * product
                here = pl.ds(pl.multiple_of(i * 16 + half, 8), 8)
                zy[j, here, :] = gv
                bc[j, here, :] = pv
                state = jnp.broadcast_to(gv[0:1, :], (8, 512))
                product = jnp.broadcast_to(pv[0:1, :], (8, 512))
            return state, product

        state, product = lax.fori_loop(0, 16, step, (zero, zero + 1.0))
        tail[j] = fold(state, product)

    tail_slots = w.block(12)
    down = Spread(
        w, [lambda q: piece_in.at[q, :, pl.ds(0, 256)]], [lambda q: gd_out.at[:, cols(q, 256)]]
    )
    down_odd = OddScatter(w, lambda q: piece_in.at[q, :, pl.ds(256, 128)], gd_out.at[:, odd])

    @pl.loop(0, 4)
    def _(k):
        @pl.when(k == 1)
        def _():
            units[0].step(2)
            gather.forward()
            units[0].step(3)

        @pl.when(k == 3)
        def _():
            gather.finish()
            down.start()
            down_odd.start()
            units[0].step(4)
            units[1].step(2)

        j = p.member(k)
        scan_rows(j)
        for away in (1, 2, 3):

            @pl.when(z >= away)
            def _():
                w.copy(tail.at[j], sums.at[z, j], tail_slots + 3 * k + away - 1, p.line(z - away)).start()

    units[1].step(3)
    for made in later:
        made.wait()

    @pl.loop(0, 4)
    def _(i):
        gout[i] = (
            mm_tn(dr[:, :, cols(i, 384)].reshape(1024, 384), oo[...].reshape(1024, 512))
            .astype(bf16)
            .reshape(2, 192, 512)
        )

    core_o = CoreSum(w, lambda q: gout.at[:, q], cbo)
    core_o.start()

    def in_grad(m, right):
        @pl.loop(0, 4)
        def _(i):
            gin[m, i] = mm(n1t[cols(i, 384), :], right[...].reshape(1024, 512)).astype(bf16).reshape(2, 192, 512)

    in_grad(1, dzy)
    core_y = CoreSum(w, lambda q: gin.at[1, :, q], cbi.at[1])
    core_y.start()
    def through(j, carry):
        after = zero
        for src in (3, 2, 1):
            tile = sums[src, j]
            after = jnp.where(z < src, unfold(tile, 0) + unfold(tile, 4) * after, after)
        after = jnp.concatenate([after, after], axis=0)

        def step(i, carry):
            sum_x, sum_a, sum_d = carry
            at = rows16(i)
            g = zy[j, at, :] + bc[j, at, :] * after
            before = hh[j, rows16(i, 24), :][7:23]
            entry, rate, value = zx[j, at, :], za[j, at, :], cc[j, at, :].astype(f32)
            log_a = -8.0 * rate * sm_ref[7:8, :]
            decay = aa[j, at, :]
            index = lax.broadcasted_iota(jnp.int32, (16, 512), 0) + i * 16 + z * 256
            start = index == 0
            mult = jnp.where(start, 1.0, jnp.sqrt(one_minus_square(2.0 * log_a, decay)))
            gm = g * mult
            d_entry = gm * value
            bc[j, at, :] = gm * entry
            low_x = (d_entry * entry * (1.0 - entry)).astype(bf16)
            dzx[j, at, :] = low_x
            d_mult = g * entry * value
            d_log = g * before * decay - jnp.where(start, 0.0, d_mult * decay * decay / mult)
            low_a = (d_log * (-8.0 * sm_ref[7:8, :]) * rate * (1.0 - rate)).astype(bf16)
            dza[j, at, :] = low_a
            wide_x, wide_a, d_decay = low_x.astype(f32), low_a.astype(f32), d_log * rate
            return (
                sum_x + wide_x[0:8] + wide_x[8:16],
                sum_a + wide_a[0:8] + wide_a[8:16],
                sum_d + d_decay[0:8] + d_decay[8:16],
            )

        carry = lax.fori_loop(0, 16, step, carry)
        for b in range(4):
            lanes = pl.ds(b * 128, 128)
            bc[j, pl.ds(0, 256), lanes] += mm_nt(
                dzx[j, :, lanes], gg[0, b].reshape(128, 128)
            ) + mm_nt(dza[j, :, lanes], gg[1, b].reshape(128, 128))
        return carry

    def taps(j, carry):
        def step(i, carry):
            at = rows16(i)
            v = bc[j, rows16(i, 24), :]
            xv = xb[j, rows16(i, 24), :]
            total = sm_ref[0:1, :] * v[0:16]
            for k in (1, 2, 3):
                total = total + sm_ref[k : k + 1, :] * v[k : k + 16]
            oo[j, at, :] = total.astype(bf16)
            now = v[0:16]
            new = []
            for k in range(4):
                product = now * xv[8 - k : 24 - k]
                new.append(carry[k] + product[0:8] + product[8:16])
            new.append(carry[4] + now[0:8] + now[8:16])
            return tuple(new)

        return lax.fori_loop(0, 16, step, carry)

    halo_slots = w.block(4)

    def tell(n, j):
        @pl.when(z > 0)
        def _():
            w.copy(
                bc.at[j, pl.ds(0, 8)], bc.at[j, pl.ds(256, 8)], halo_slots + n, p.line(z - 1)
            ).start()

    def hear(n, j):
        @pl.when(z < 3)
        def _():
            w.landed(bc.at[j, pl.ds(256, 8)], halo_slots + n)

    @pl.when(z == 3)
    def _():
        bc[:, 256:264, :] = jnp.zeros((4, 8, 512), f32)

    def gate_grads(i, right):
        for b in range(4):
            lanes = pl.ds(b * 128, 128)
            ggr[i, b] = (
                mm_tn(cc[:, :, lanes].reshape(1024, 128), right[:, :, lanes].reshape(1024, 128))
                .astype(bf16)
                .reshape(4, 2, 16, 128)
            )

    gather.drain()
    summed = PlaneSum(w, dr, far, near)
    core_x = CoreSum(w, lambda q: gin.at[0, :, q], cbi.at[0])
    core_g = CoreSum(w, lambda q: ggr.at[:, :, :, q], cbg)
    spreads = [
        Spread(
            w,
            [lambda q: hgu.at[:, q, :, cols(z, 256)]],
            [lambda q: gff_out.at[:, :, cols(q, 256)]],
        ),
        Spread(
            w,
            [lambda q: gout.at[q, c, :, cols(z)], lambda q: gin.at[1, q, c, :, cols(z)]],
            [lambda q: gout_out.at[:, cols(q)], lambda q: gin_out.at[1, :, cols(q)]],
        ),
        Spread(
            w,
            [lambda q: gin.at[0, q, c, :, cols(z)], lambda q: ggr.at[:, z, q, c]],
            [lambda q: gin_out.at[0, :, cols(q)], lambda q: ggate_out.at[:, q]],
        ),
    ]
    odds = [
        OddScatter(w, lambda q: hgu.at[:, q, :, odd], gff_out.at[:, :, odd]),
    ]

    zw = jnp.zeros((8, 1536), f32)
    stats = stat1[...] + stat2[...]
    early_own[...] = jnp.zeros((16, 128), f32)
    stack_rows(stats[4:5, :], early_own)
    for n in range(4):
        early_own[12 + n : 13 + n, :] = jnp.broadcast_to(jnp.sum(stats[n : n + 1, :], axis=1, keepdims=True), (1, 128))
    late_own[...] = jnp.zeros((16, 128), f32)
    small_early = SmallSum(
        w, [(acc8, acc8_l, acc8_c, acc8_p), (early_own, early_l, early_c, early_p)], [True, False]
    )
    small_late = SmallSum(w, [(late_own, late_l, late_c, late_p)], [False])
    acc[...] = jnp.zeros((8, 8, 512), f32)

    @pl.loop(0, 5)
    def _(k):
        @pl.when(k == 1)
        def _():
            units[1].step(4)
            units[2].step(2)

        @pl.when(k == 4)
        def _():
            gate_grads(0, dzx)
            gate_grads(1, dza)

        @pl.when(k < 4)
        def _():
            j = p.member(3 - k)
            for away in (1, 2, 3):

                @pl.when(z + away <= 3)
                def _():
                    w.landed(sums.at[z + away, j], tail_slots + 3 * (3 - k) + away - 1)

            for n, value in enumerate(through(j, (zero,) * 3)):
                acc[n] += value
            tell(k, j)

        @pl.when(k > 0)
        def _():
            j = p.member(4 - k)
            hear(k - 1, j)
            for n, value in enumerate(taps(j, (zero,) * 5)):
                acc[3 + n] += value
            for n in range(2):
                span = pl.ds(2 * n, 2)
                dr[j, :, n * 768 : (n + 1) * 768] = (
                    mm_nt(oo[j], win[0, span].reshape(768, 512)) + mm_nt(dzy[j], win[1, span].reshape(768, 512))
                ).astype(bf16)

        @pl.when(k == 0)
        def _():
            core_o.finish()
            line_o.first()
            core_y.finish()
            line_y.first()

        @pl.when(k == 1)
        def _():
            summed.diagonal()
            units[2].step(3)

        @pl.when(k == 2)
        def _():
            units[2].step(4)
            spreads[0].start()
            odds[0].start()
            line_o.step(2)

        @pl.when(k == 3)
        def _():
            summed.arrive()
            summed.to_y()
            summed.to_x()
            line_o.step(3)

    line_o.step(4)
    in_grad(0, oo)
    core_x.start()
    core_g.start()
    line_y.step(2)
    acc8[5:6, :] = jnp.sum(acc[0], axis=0, keepdims=True)
    acc8[6:7, :] = jnp.sum(acc[1], axis=0, keepdims=True)
    acc8[7:8, :] = -8.0 * sm_ref[8:9, :] * jnp.sum(acc[2], axis=0, keepdims=True)
    for k in range(5):
        acc8[k : k + 1, :] = jnp.sum(acc[3 + k], axis=0, keepdims=True)
    small_early.line()
    core_x.finish()
    core_g.finish()
    line_x.first()
    line_y.step(3)
    line_y.step(4)
    spreads[1].start()
    line_x.step(2)
    small_early.core()
    summed.finish()

    def last(i, carry):
        at = rows16(i)
        v = x_ref[at, :].astype(f32)
        s = norm_rows(v)
        dn = dr[t, at, :].astype(f32) + near[0, at, :].astype(f32) + near[1, at, :].astype(f32)
        q = gain_ref[...] * dn
        gi_ref[at, :] = (
            dx1_ref[at, :] + s * q - v * (s * s * s * jnp.mean(q * v, axis=1, keepdims=True))
        ).astype(bf16)
        g1 = dn * v * s
        return carry + g1[0:8] + g1[8:16]

    g1 = lax.fori_loop(0, 16, last, zw)
    line_x.step(3)
    stack_rows(jnp.sum(g1, axis=0, keepdims=True), late_own)
    small_late.line()
    small_early.plane()
    line_x.step(4)
    spreads[2].start()
    small_late.core()
    small_late.plane()
    v2_ref[...], v1_ref[...] = small_early.result()
    (v3_ref[...],) = small_late.result()

    for made in spreads + [down]:
        made.wait()
        made.drain()
    for made in odds + [down_odd]:
        made.finish()
    small_early.drain()
    small_late.drain()
    summed.drain()
    for made in units + [line_o, line_y, line_x, core_o, core_y, core_x, core_g]:
        made.drain()

    for n in range(4):
        for away in (1, 2, 3):

            @pl.when(z >= away)
            def _():
                w.sent(tail.at[n], tail_slots + 3 * n + away - 1)

    for n in range(4):

        @pl.when(z > 0)
        def _():
            w.sent(bc.at[n, pl.ds(0, 8)], halo_slots + n)


def feed_forward_call(*args):
    V = pltpu.VMEM
    outs = [
        shape((256, 1536), f32), shape((256, 1536), bf16), shape((8, 1536), f32),
        shape((2, 4, 192, 1152), bf16), shape((4, 192, 384), bf16),
    ]
    weights = V((4, 2, 192, 1152), bf16)
    tokens, turned = V((4, 256, 1536), bf16), V((1536, 1024), bf16)
    scratch = [
        V((2, 4, 2, 192, 1152), bf16), weights, tokens, turned, tokens, turned, V((2, 4, 256, 1152), f32),
        V((4, 256, 1152), bf16), V((2, 4, 256, 1152), bf16), tokens, V((2, 128, 1536), bf16),
        V((2, 256, 1536), bf16), weights, V((2, 4, 192, 1152), bf16),
        V((3, 6, 2, 192, 256), bf16), V((3, 3, 2, 192, 128), bf16), V((1, 1536), f32),
    ]
    return call(feed_forward, 1, args, "vvvaaaa", outs, "vvvaa", scratch, 128, 24, "feed_forward")


def backward_recurrence(*args):
    V = pltpu.VMEM
    outs = [
        shape((256, 1536), bf16), shape((16, 128), f32), shape((4, 8, 512), f32), shape((16, 128), f32),
        shape((2, 192, 512), bf16), shape((192, 512), bf16), shape((2, 192, 1152), bf16), shape((192, 1152), bf16),
        shape((2, 4, 16, 128), bf16),
    ]
    tokens, turned = V((4, 256, 1536), bf16), V((1536, 1024), bf16)
    wide, padded, low = V((4, 256, 512), f32), V((4, 264, 512), f32), V((4, 256, 512), bf16)
    scratch = [
        V((2, 4, 2, 192, 512), bf16), V((4, 2, 192, 512), bf16), turned, tokens, padded, wide, wide, wide, low,
        padded, padded, low, V((2, 4, 4, 2, 16, 128), bf16), V((2, 4, 192, 1152), bf16), V((256, 512), f32),
        padded, low, low, low,
        V((2, 128, 1536), bf16), V((2, 256, 1536), bf16),
        V((2, 4, 2, 192, 512), bf16), V((4, 2, 192, 512), bf16), V((2, 4, 4, 2, 16, 128), bf16),
        V((2, 4, 192, 512), bf16), V((4, 192, 512), bf16), V((2, 4, 4, 16, 128), bf16),
        V((2, 6, 4, 192, 128), bf16), V((6, 4, 192, 128), bf16), V((6, 2, 4, 16, 128), bf16),
        V((3, 6, 2, 192, 256), bf16), V((3, 3, 2, 192, 128), bf16),
        V((4, 8, 128), f32), V((4, 4, 8, 128), f32), V((8, 512), f32),
        V((16, 128), f32), V((16, 128), f32), V((4, 8, 512), f32), V((3, 8, 512), f32), V((4, 8, 512), f32),
        V((4, 16, 128), f32), V((3, 16, 128), f32), V((4, 16, 128), f32),
        V((4, 16, 128), f32), V((3, 16, 128), f32), V((4, 16, 128), f32),
        V((1, 1536), f32), V((8, 8, 512), f32),
    ]
    return call(
        recurrence_backward, 2, args, "vvvvvv" + "a" * 14,
        outs, "vvvvaaaaa", scratch, 192, 24, "recurrence_backward",
    )


def finish(count, gin, gout, gff, gd, ggate, y, gi, v1, v2, v3,
           wx, wy, wo, wg, wu, wd, gg, y_out, gi_out, g1, g2, cw, cb, bias, decay, rms, rows, wide):
    wx[...] = gin[0].astype(f32)
    wy[...] = gin[1].astype(f32)
    wo[...] = gout[...].astype(f32)
    wg[...] = gff[0].astype(f32)
    wu[...] = gff[1].astype(f32)
    wd[...] = gd[...].astype(f32)
    y_out[...] = y[...]
    gi_out[...] = gi[...]

    @pl.when(pl.program_id(0) == 0)
    def _():
        gg[...] = ggate[...].astype(f32)
        for n in range(12):
            wide[0:1, n * 128 : (n + 1) * 128] = v3[n : n + 1, :]
            wide[1:2, n * 128 : (n + 1) * 128] = v1[n : n + 1, :]
        g1[...] = wide[0:1, :].reshape(1536)
        g2[...] = wide[1:2, :].reshape(1536)
        for t in range(4):
            for z in range(4):
                rows[:, z * 512 + t * 128 : z * 512 + (t + 1) * 128] = v2[t, :, z * 128 : (z + 1) * 128]
        cw[...] = rows[0:4, :]
        cb[...] = rows[4:5, :].reshape(2048)
        bias[...] = rows[5:7, :]
        decay[...] = rows[7:8, :].reshape(2048)
        root = jnp.sqrt(v1[12:16, :] / count)
        for i in range(4):
            rms[i] = root[i, 0]


def finish_call(count, gin, gout, gff, gd, ggate, y, gi, v1, v2, v3):
    steps = 4

    def sliced(a):
        axis = a.ndim - 2
        block = tuple(n // steps if i == axis else n for i, n in enumerate(a.shape))
        return pl.BlockSpec(block, lambda i: tuple(i if n == axis else 0 for n in range(a.ndim)))

    def whole(a):
        return pl.BlockSpec(a.shape, lambda i: (0,) * len(a.shape))

    one, two = shape((192, 512), f32), shape((192, 1152), f32)
    big = [one, one, one, two, two, two]
    small = [
        shape((1536,), f32), shape((1536,), f32), shape((4, 2048), f32), shape((2048,), f32),
        shape((2, 2048), f32), shape((2048,), f32),
    ]
    gates = shape(ggate.shape, f32)
    tokens = shape(y.shape, bf16)
    return pl.pallas_call(
        functools.partial(finish, count),
        out_shape=big + [gates, tokens, tokens] + small + [shape((4,), f32)],
        grid=(steps,),
        in_specs=[sliced(a) for a in (gin, gout, gff, gd)] + [whole(ggate)] + [sliced(a) for a in (y, gi)] + [whole(v1), whole(v2), whole(v3)],
        out_specs=[sliced(a) for a in big] + [whole(gates), sliced(tokens), sliced(tokens)]
        + [whole(a) for a in small] + [pl.BlockSpec(memory_space=pltpu.SMEM)],
        scratch_shapes=[pltpu.VMEM((8, 2048), f32), pltpu.VMEM((8, 1536), f32)],
        name="finish",
    )(gin, gout, gff, gd, ggate, y, gi, v1, v2, v3)


def fast_local(
    inputs, norm1_gain, w_in_x, w_in_y, conv_w, conv_b, gates, gate_bias, decay_param, w_out,
    norm2_gain, w_gate, w_up, w_down, cotangent,
):
    (x1, stat1, sm, n1t, win, wout, wg, wu, a2d, cot, gg, xb, zy, zx, za, cc, aa, hh, oo) = forward_recurrence(
        inputs, norm1_gain, conv_w, conv_b, gate_bias, decay_param, w_in_x, w_in_y, w_out, gates,
        w_gate, w_up, w_down, cotangent,
    )
    dx1, y, stat2, halves, piece = feed_forward_call(x1, norm2_gain, cotangent, cot, wg, wu, a2d)
    gi, v1, v2, v3, gin, gout, gff, gd, ggate = backward_recurrence(
        inputs, norm1_gain, dx1, sm, stat1, stat2, win, wout, n1t, xb, zy, zx, za, cc, aa, hh, oo, gg,
        halves, piece,
    )
    count = inputs.shape[0] * lax.axis_size("dp") * lax.axis_size("tensor") * inputs.shape[1]
    (gwx, gwy, gwo, gwg, gwu, gwd, ggates, output, grad_inputs, g1, g2, gcw, gcb, gbias, gdecay, rms) = finish_call(
        count, gin, gout, gff, gd, ggate, y, gi, v1, v2, v3
    )
    return (
        output, grad_inputs, g1, gwx, gwy, gcw, gcb, ggates, gbias, gdecay, gwo, g2, gwg, gwu, gwd, rms,
    )


def solution(mesh):
    fits = mesh.shape["dp"] == 8 and mesh.shape["tensor"] == 4
    return jax.shard_map(
        fast_local if fits else local,
        mesh=mesh,
        in_specs=(
            P(("dp", "tensor"), None),
            P(),
            P("dp", "tensor"),
            P("dp", "tensor"),
            P(None, "tensor"),
            P("tensor"),
            P(None, "tensor", "dp", None),
            P(None, "tensor"),
            P("tensor"),
            P("dp", "tensor"),
            P(),
            P("dp", "tensor"),
            P("dp", "tensor"),
            P("dp", "tensor"),
            P(("dp", "tensor"), None),
        ),
        out_specs=(
            P(("dp", "tensor"), None),
            P(("dp", "tensor"), None),
            P(),
            P("dp", "tensor"),
            P("dp", "tensor"),
            P(),
            P(),
            P(None, "tensor", "dp", None),
            P(),
            P(),
            P("dp", "tensor"),
            P(),
            P("dp", "tensor"),
            P("dp", "tensor"),
            P("dp", "tensor"),
            P(),
        ),
        check_vma=False,
    )
```

```python
import functools

import jax
import jax.numpy as jnp
from jax import lax
from jax.experimental import pallas as pl
from jax.experimental.pallas import tpu as pltpu
from jax.sharding import PartitionSpec as P

CONV = 4
SEQ_LEN = 1024


epsilon = 1e-06


def gelu_tanh(value):
    return jax.nn.gelu(value, approximate=True)


def combine(earlier, later):
    return (earlier[0] * later[0], later[0] * earlier[1] + later[1])


def norm_back(value, scale, gain, grad):
    scaled = gain * grad
    return scale * scaled - value * scale * scale * scale * jnp.mean(
        scaled * value, axis=1, keepdims=True
    )


def row_product(left, right):
    return lax.dot_general(
        left, right, (((0,), (0,)), ((), ())), preferred_element_type=jnp.float32
    )


def back_product(left, right):
    return lax.dot_general(
        left, right, (((1,), (1,)), ((), ())), preferred_element_type=jnp.float32
    )


def local(
    inputs,
    norm1_gain,
    w_in_x,
    w_in_y,
    conv_w,
    conv_b,
    gates,
    gate_bias,
    decay_param,
    w_out,
    norm2_gain,
    w_gate,
    w_up,
    w_down,
    cotangent,
):
    row_count = inputs.shape[0]
    model_width = inputs.shape[1]
    tensor_count = lax.axis_size("tensor")
    group_rows = row_count * tensor_count
    seq_count = group_rows // SEQ_LEN
    rec_x, rec_y, rec_o, gate_mats = (
        lax.all_gather(w_in_x, "dp", axis=0, tiled=True),
        lax.all_gather(w_in_y, "dp", axis=0, tiled=True),
        lax.all_gather(w_out, "dp", axis=0, tiled=True),
        lax.all_gather(gates, "dp", axis=2, tiled=True),
    )
    channels = rec_x.shape[1]
    blocks_here = gate_mats.shape[1]
    block_width = gate_mats.shape[3]
    residual = inputs.astype(jnp.float32)
    scale_one = lax.rsqrt(jnp.mean(residual * residual, axis=1, keepdims=True) + epsilon)
    n_one = (residual * scale_one * norm1_gain).astype(jnp.bfloat16)
    full_one = lax.all_gather(n_one, "tensor", axis=0, tiled=True)
    x_branch = jnp.dot(full_one, rec_x, preferred_element_type=jnp.float32)
    y_pre = jnp.dot(full_one, rec_y, preferred_element_type=jnp.float32)
    seq_x = x_branch.reshape(seq_count, SEQ_LEN, channels)
    padded = jnp.pad(seq_x, ((0, 0), (CONV - 1, 0), (0, 0)))
    conv_sum = conv_b + jnp.zeros_like(seq_x)
    for k in range(CONV):
        conv_sum = conv_sum + conv_w[k] * padded[:, CONV - 1 - k : CONV - 1 - k + SEQ_LEN]
    conv_low = conv_sum.reshape(group_rows, channels).astype(jnp.bfloat16)
    conv_value = conv_low.astype(jnp.float32)
    blocked = conv_low.reshape(group_rows, blocks_here, block_width)
    z_input = (
        jnp.einsum(
            "gbi,bij->gbj", blocked, gate_mats[0], preferred_element_type=jnp.float32
        ).reshape(group_rows, channels)
        + gate_bias[0]
    )
    z_decay = (
        jnp.einsum(
            "gbi,bij->gbj", blocked, gate_mats[1], preferred_element_type=jnp.float32
        ).reshape(group_rows, channels)
        + gate_bias[1]
    )
    seq_start = (jnp.arange(group_rows) % SEQ_LEN == 0)[:, None]

    def coefficients(input_pre, decay_pre, conv_part, decay_raw):
        log_decay = -8.0 * jax.nn.sigmoid(decay_pre) * jax.nn.softplus(decay_raw)
        mult = jnp.where(seq_start, 1.0, jnp.sqrt(-jnp.expm1(2.0 * log_decay)))
        return (jnp.exp(log_decay), mult * jax.nn.sigmoid(input_pre) * conv_part)

    (decays, inflow), pull_coeff = jax.vjp(coefficients, z_input, z_decay, conv_value, decay_param)
    seq_decay = decays.reshape(seq_count, SEQ_LEN, channels)
    _, seq_states = lax.associative_scan(
        combine, (seq_decay, inflow.reshape(seq_count, SEQ_LEN, channels)), axis=1
    )
    states = seq_states.reshape(group_rows, channels)
    y_gate = gelu_tanh(y_pre)
    mixed_out = (states * y_gate).astype(jnp.bfloat16)
    branch = lax.psum_scatter(
        back_product(mixed_out, rec_o), "tensor", scatter_dimension=0, tiled=True
    )
    stream = residual + branch
    mlp_g, mlp_u, mlp_d = (
        lax.all_gather(w_gate, "dp", axis=0, tiled=True),
        lax.all_gather(w_up, "dp", axis=0, tiled=True),
        lax.all_gather(w_down, "dp", axis=0, tiled=True),
    )
    scale_two = lax.rsqrt(jnp.mean(stream * stream, axis=1, keepdims=True) + epsilon)
    n_two = (stream * scale_two * norm2_gain).astype(jnp.bfloat16)
    full_two = lax.all_gather(n_two, "tensor", axis=0, tiled=True)
    gate_pre = jnp.dot(full_two, mlp_g, preferred_element_type=jnp.float32)
    up_pre = jnp.dot(full_two, mlp_u, preferred_element_type=jnp.float32)
    hidden = (gelu_tanh(gate_pre) * up_pre).astype(jnp.bfloat16)
    ffn_out = lax.psum_scatter(
        back_product(hidden, mlp_d), "tensor", scatter_dimension=0, tiled=True
    )
    result = stream + ffn_out
    output = result.astype(jnp.bfloat16)
    squares = jnp.stack(
        [
            jnp.sum(stream * stream),
            jnp.sum(branch * branch),
            jnp.sum(ffn_out * ffn_out),
            jnp.sum(result * result),
        ]
    )
    upstream = cotangent.astype(jnp.float32)
    full_cot = lax.all_gather(cotangent, "tensor", axis=0, tiled=True)
    d_hidden = jnp.dot(full_cot, mlp_d, preferred_element_type=jnp.float32)
    grad_down = row_product(full_cot, hidden)
    _, pull_mlp = jax.vjp(
        lambda gate_value, up_value: gelu_tanh(gate_value) * up_value, gate_pre, up_pre
    )
    d_gate, d_up = pull_mlp(d_hidden)
    d_gate_low = d_gate.astype(jnp.bfloat16)
    d_up_low = d_up.astype(jnp.bfloat16)
    grad_gate_w = row_product(full_two, d_gate_low)
    grad_up_w = row_product(full_two, d_up_low)
    d_two = lax.psum_scatter(
        back_product(d_gate_low, mlp_g) + back_product(d_up_low, mlp_u),
        "tensor",
        scatter_dimension=0,
        tiled=True,
    )
    grad_gain_two = jnp.sum(d_two * stream * scale_two, axis=0)
    d_stream = upstream + norm_back(stream, scale_two, norm2_gain, d_two)
    mlp_summed = (grad_gate_w, grad_up_w, grad_down)
    full_branch = lax.all_gather(d_stream.astype(jnp.bfloat16), "tensor", axis=0, tiled=True)
    d_mixed = jnp.dot(full_branch, rec_o, preferred_element_type=jnp.float32)
    grad_out_w = row_product(full_branch, mixed_out)
    d_states = d_mixed * y_gate
    _, pull_gelu = jax.vjp(gelu_tanh, y_pre)
    d_y_low = pull_gelu(d_mixed * states)[0].astype(jnp.bfloat16)
    next_decay = jnp.concatenate([seq_decay[:, 1:], jnp.zeros_like(seq_decay[:, :1])], axis=1)
    _, carried = lax.associative_scan(
        combine, (next_decay, d_states.reshape(seq_count, SEQ_LEN, channels)), reverse=True, axis=1
    )
    prev_states = jnp.concatenate([jnp.zeros_like(seq_states[:, :1]), seq_states[:, :-1]], axis=1)
    d_decays = (carried * prev_states).reshape(group_rows, channels)
    d_input_pre, d_decay_pre, d_conv_direct, grad_decay = pull_coeff(
        (d_decays, carried.reshape(group_rows, channels))
    )
    d_input_low = d_input_pre.astype(jnp.bfloat16)
    d_decay_low = d_decay_pre.astype(jnp.bfloat16)
    grad_bias = jnp.stack(
        [
            jnp.sum(d_input_low, axis=0, dtype=jnp.float32),
            jnp.sum(d_decay_low, axis=0, dtype=jnp.float32),
        ]
    )
    input_blocks = d_input_low.reshape(group_rows, blocks_here, block_width)
    decay_blocks = d_decay_low.reshape(group_rows, blocks_here, block_width)
    grad_gate_mats = jnp.stack(
        [
            jnp.einsum("gbi,gbj->bij", blocked, input_blocks, preferred_element_type=jnp.float32),
            jnp.einsum("gbi,gbj->bij", blocked, decay_blocks, preferred_element_type=jnp.float32),
        ]
    )
    d_conv = d_conv_direct + jnp.einsum(
        "gbj,bij->gbi", input_blocks, gate_mats[0], preferred_element_type=jnp.float32
    ).reshape(group_rows, channels)
    d_conv = d_conv + jnp.einsum(
        "gbj,bij->gbi", decay_blocks, gate_mats[1], preferred_element_type=jnp.float32
    ).reshape(group_rows, channels)
    seq_dconv = d_conv.reshape(seq_count, SEQ_LEN, channels)
    grad_conv_b = jnp.sum(seq_dconv, axis=(0, 1))
    padded_back = jnp.pad(seq_dconv, ((0, 0), (0, CONV - 1), (0, 0)))
    tap_grads = []
    d_x_seq = jnp.zeros_like(seq_dconv)
    for k in range(CONV):
        tap_grads.append(
            jnp.sum(seq_dconv * padded[:, CONV - 1 - k : CONV - 1 - k + SEQ_LEN], axis=(0, 1))
        )
        d_x_seq = d_x_seq + conv_w[k] * padded_back[:, k : k + SEQ_LEN]
    grad_conv_w = jnp.stack(tap_grads)
    d_x_low = d_x_seq.reshape(group_rows, channels).astype(jnp.bfloat16)
    grad_in_x_w = row_product(full_one, d_x_low)
    grad_in_y_w = row_product(full_one, d_y_low)
    d_one = lax.psum_scatter(
        back_product(d_x_low, rec_x) + back_product(d_y_low, rec_y),
        "tensor",
        scatter_dimension=0,
        tiled=True,
    )
    grad_gain_one = jnp.sum(d_one * residual * scale_one, axis=0)
    grad_inputs = (d_stream + norm_back(residual, scale_one, norm1_gain, d_one)).astype(
        jnp.bfloat16
    )
    small_grads = jnp.concatenate(
        [grad_conv_w, grad_conv_b[None], grad_bias, grad_decay[None]], axis=0
    )
    spread_grads = lax.dynamic_update_slice(
        jnp.zeros((small_grads.shape[0], channels * tensor_count), jnp.float32),
        small_grads,
        (0, lax.axis_index("tensor") * channels),
    )
    gain_total, small_total, square_total = lax.psum(
        (jnp.stack([grad_gain_one, grad_gain_two]), spread_grads, squares), ("dp", "tensor")
    )
    stream_rms = jnp.sqrt(
        square_total / (row_count * lax.axis_size("dp") * tensor_count * model_width)
    )
    summed_all = (
        lax.psum_scatter(grad_in_x_w, "dp", scatter_dimension=0, tiled=True),
        lax.psum_scatter(grad_in_y_w, "dp", scatter_dimension=0, tiled=True),
        lax.psum_scatter(grad_out_w, "dp", scatter_dimension=0, tiled=True),
        lax.psum_scatter(grad_gate_mats, "dp", scatter_dimension=2, tiled=True),
        lax.psum_scatter(mlp_summed[0], "dp", scatter_dimension=0, tiled=True),
        lax.psum_scatter(mlp_summed[1], "dp", scatter_dimension=0, tiled=True),
        lax.psum_scatter(mlp_summed[2], "dp", scatter_dimension=0, tiled=True),
    )
    rec_summed = summed_all[:4]
    grad_gate_sum, grad_up_sum, grad_down_sum = (summed_all[4], summed_all[5], summed_all[6])
    return (
        output,
        grad_inputs,
        gain_total[0],
        rec_summed[0],
        rec_summed[1],
        small_total[0:CONV],
        small_total[CONV],
        rec_summed[3],
        small_total[CONV + 1 : CONV + 3],
        small_total[CONV + 3],
        rec_summed[2],
        gain_total[1],
        grad_gate_sum,
        grad_up_sum,
        grad_down_sum,
        stream_rms,
    )


MESH = pl.DeviceIdType.MESH
bf16 = jnp.bfloat16
f32 = jnp.float32
VMEM_BYTES = 67043328


def mm(a, b):
    return jnp.dot(a, b, preferred_element_type=f32)


def mm_nt(a, b):
    return lax.dot_general(a, b, (((1,), (1,)), ((), ())), preferred_element_type=f32)


def mm_tn(a, b):
    return lax.dot_general(a, b, (((0,), (0,)), ((), ())), preferred_element_type=f32)


def gelu_value(x):
    return 0.5 * x * (1.0 + jnp.tanh(0.7978845608028654 * x * (1.0 + 0.044715 * (x * x))))


def gelu_pair(x):
    x2 = x * x
    th = jnp.tanh(0.7978845608028654 * x * (1.0 + 0.044715 * x2))
    cdf = 0.5 * (1.0 + th)
    slope = 0.5 * x * (1.0 - th * th) * (0.7978845608028654 * (1.0 + 0.134145 * x2))
    return x * cdf, cdf + slope


def one_minus_square(x, decay):
    series = x * (
        1.0
        + x * (0.5 + x * (1 / 6 + x * (1 / 24 + x * (1 / 120 + x * (1 / 720 + x * (1 / 5040))))))
    )
    return jnp.where(x > -0.35, -series, 1.0 - decay * decay)


class Place:
    def __init__(self):
        self.d = lax.axis_index("dp")
        self.z = lax.axis_index("tensor")
        self.t = lax.div(self.d, 2)
        self.c = lax.rem(self.d, 2)
        self.tx = self.t + 1 - 2 * lax.rem(self.t, 2)
        self.ty = self.t + 2 - 4 * lax.div(self.t, 2)
        self.td = 3 - self.t
        self.peers = (self.tx, self.ty, self.td)

    def member(self, r):
        x, y = lax.rem(self.t, 2), lax.div(self.t, 2)
        b, e = lax.rem(r, 2), lax.div(r, 2)
        return x + b - 2 * x * b + 2 * (y + e - 2 * y * e)

    def plane(self, t):
        return (2 * t + self.c, self.z)

    def line(self, z):
        return (self.d, z)

    def partner(self):
        return (2 * self.t + 1 - self.c, self.z)

    def around(self, k):
        return lax.rem(self.z + k, 4)

    def enter(self):
        barrier = pltpu.get_barrier_semaphore()
        targets = [self.plane(t) for t in self.peers] + [self.partner()]
        targets += [self.line(self.around(k)) for k in (1, 2, 3)]
        for target in targets:
            pl.semaphore_signal(barrier, inc=1, device_id=target, device_id_type=MESH)
        pl.semaphore_wait(barrier, len(targets))


class Wires:
    def __init__(self, place, send, recv, local):
        self.place, self.send, self.recv, self.local = place, send, recv, local
        self.used, self.used_local = 0, 0

    def slot(self):
        self.used += 1
        assert self.used <= self.send.shape[0]
        return self.used - 1

    def block(self, count):
        self.used += count
        assert self.used <= self.send.shape[0]
        return self.used - count

    def copy(self, src, dst, slot, device):
        return pltpu.make_async_remote_copy(
            src_ref=src,
            dst_ref=dst,
            send_sem=self.send.at[slot],
            recv_sem=self.recv.at[slot],
            device_id=device,
            device_id_type=MESH,
        )

    def landed(self, ref, slot):
        self.copy(ref, ref, slot, self.place.partner()).wait_recv()

    def sent(self, ref, slot):
        self.copy(ref, ref, slot, self.place.partner()).wait_send()

    def held_here(self, src, dst):
        self.used_local += 1
        assert self.used_local <= self.local.shape[0]
        return pltpu.make_async_copy(src, dst, self.local.at[self.used_local - 1])

    def here(self, src, dst):
        made = self.held_here(src, dst)
        made.start()
        return made


class Spread:
    def __init__(self, w, parts, homes):
        self.w, self.parts, self.homes = w, parts, homes
        self.slots = [[w.slot() for _ in range(3)] for _ in parts]
        self.first = w.used_local
        w.used_local += len(parts)

    def _kept(self, act):
        t = self.w.place.t
        for n, (part, home) in enumerate(zip(self.parts, self.homes)):
            act(pltpu.make_async_copy(part(t), home(t), self.w.local.at[self.first + n]))

    def start(self):
        p = self.w.place
        for part, home, slots in zip(self.parts, self.homes, self.slots):
            for peer, slot in zip(p.peers, slots):
                self.w.copy(part(peer), home(p.t), slot, p.plane(peer)).start()
        self._kept(lambda made: made.start())

    def wait(self):
        p = self.w.place
        self._kept(lambda made: made.wait())
        for home, slots in zip(self.homes, self.slots):
            for peer, slot in zip(p.peers, slots):
                self.w.landed(home(peer), slot)

    def drain(self):
        p = self.w.place
        for part, slots in zip(self.parts, self.slots):
            for peer, slot in zip(p.peers, slots):
                self.w.sent(part(peer), slot)


class OneSpread:
    def __init__(self, w, part, home):
        self.w, self.part, self.home = w, part, home
        self.slots = [w.slot() for _ in range(3)]
        self.kept = w.held_here(part, home(w.place.t))

    def start(self):
        p = self.w.place

        @pl.when(p.t == p.z)
        def _():
            self.kept.start()

        for peer, slot in zip(p.peers, self.slots):

            @pl.when(peer == p.z)
            def _():
                self.w.copy(self.part, self.home(p.t), slot, p.plane(peer)).start()

    def wait(self):
        p = self.w.place

        @pl.when(p.t == p.z)
        def _():
            self.kept.wait()
            for peer, slot in zip(p.peers, self.slots):
                self.w.landed(self.home(peer), slot)

    def drain(self):
        p = self.w.place
        for peer, slot in zip(p.peers, self.slots):

            @pl.when(peer == p.z)
            def _():
                self.w.sent(self.part, slot)


class LineGather:
    def __init__(self, w, regions):
        self.w, self.regions = w, regions
        self.slots = [
            {key: w.slot() for key in ["o", "r1", "r2", "r3", "l1", "l2", "l3"]
             + ["or1", "or2", "or3", "ol1", "ol2", "ol3"]}
            for _ in regions
        ]

    def _each(self, b, act, *conditions):
        p = self.w.place
        for (view, odd), slots in zip(self.regions, self.slots):
            terms = list(conditions) + ([b == p.t] if odd else [])
            if not terms:
                act(view, slots)
                continue
            ok = terms[0]
            for term in terms[1:]:
                ok = jnp.logical_and(ok, term)

            @pl.when(ok)
            def _():
                act(view, slots)

    def _start(self, view, b, slot, device):
        p = self.w.place
        self.w.copy(view(b, p.c), view(b, p.c), slot, device).start()

    def first(self):
        p = self.w.place
        z = p.z
        self._each(z, lambda v, s: self._start(v, z, s["r1"], p.line(z + 1)), z < 3)
        self._each(z, lambda v, s: self._start(v, z, s["l1"], p.line(z - 1)), z > 0)
        self._each(z, lambda v, s: self._start(v, z, s["o"], p.partner()))

    def step(self, k):
        p = self.w.place
        z = p.z
        for sign, left in ((1, "r"), (-1, "l")):
            b = z - sign * (k - 1)
            exists = b >= 0 if sign > 0 else b <= 3

            def take(v, s):
                self.w.landed(v(b, p.c), s[f"{left}{k - 1}"])
                if k < 4:

                    @pl.when(z < 3 if sign > 0 else z > 0)
                    def _():
                        self._start(v, b, s[f"{left}{k}"], p.line(z + sign))

                self._start(v, b, s[f"o{left}{k - 1}"], p.partner())

            self._each(b, take, exists)

    def finish(self):
        p = self.w.place
        z = p.z
        other = 1 - p.c
        self._each(z, lambda v, s: self.w.landed(v(z, other), s["o"]))
        for k in (1, 2, 3):
            for sign, left in ((1, "r"), (-1, "l")):
                b = z - sign * k
                exists = b >= 0 if sign > 0 else b <= 3
                self._each(b, lambda v, s: self.w.landed(v(b, other), s[f"o{left}{k}"]), exists)

    def drain(self):
        p = self.w.place
        z = p.z
        self._each(z, lambda v, s: self.w.sent(v(z, p.c), s["o"]))
        for k in (1, 2, 3):
            for sign, left in ((1, "r"), (-1, "l")):
                b = z - sign * k
                exists = b >= 0 if sign > 0 else b <= 3
                self._each(b, lambda v, s: self.w.sent(v(b, p.c), s[f"o{left}{k}"]), exists)
                b2 = z - sign * (k - 1)
                exists2 = b2 >= 0 if sign > 0 else b2 <= 3
                more = z < 3 if sign > 0 else z > 0
                self._each(b2, lambda v, s: self.w.sent(v(b2, p.c), s[f"{left}{k}"]), exists2, more)


class PlaneGather:
    def __init__(self, w, buf):
        self.w, self.buf = w, buf
        self.half = buf.shape[1] // 2
        self.s = {key: w.slot() for key in ("x", "y", "fx", "fy")}

    def _low(self, t):
        return self.buf.at[t, pl.ds(0, self.half)]

    def _high(self, t):
        return self.buf.at[t, pl.ds(self.half, self.half)]

    def start(self, own=None):
        p, w = self.w.place, self.w
        self.own = self.buf.at[p.t] if own is None else own
        w.copy(self.own, self.buf.at[p.t], self.s["x"], p.plane(p.tx)).start()
        w.copy(self.own, self.buf.at[p.t], self.s["y"], p.plane(p.ty)).start()

    def forward(self):
        p, w = self.w.place, self.w
        w.landed(self.buf.at[p.tx], self.s["x"])
        w.copy(self._high(p.tx), self._high(p.tx), self.s["fy"], p.plane(p.ty)).start()
        w.landed(self.buf.at[p.ty], self.s["y"])
        w.copy(self._low(p.ty), self._low(p.ty), self.s["fx"], p.plane(p.tx)).start()

    def finish(self):
        p, w = self.w.place, self.w
        w.landed(self._low(p.td), self.s["fx"])
        w.landed(self._high(p.td), self.s["fy"])

    def drain(self):
        p, w = self.w.place, self.w
        w.sent(self.own, self.s["x"])
        w.sent(self.own, self.s["y"])
        w.sent(self._high(p.tx), self.s["fy"])
        w.sent(self._low(p.ty), self.s["fx"])


class PlaneSum:
    def __init__(self, w, part, far, near):
        self.w, self.part, self.far, self.near = w, part, far, near
        self.half = part.shape[1] // 2
        self.s = {key: w.slot() for key in ("dx", "dy", "x", "y")}

    def diagonal(self):
        p, w, h = self.w.place, self.w, self.half
        self.a = self.part.at[p.td, pl.ds(0, h)]
        self.b = self.part.at[p.td, pl.ds(h, h)]
        w.copy(self.a, self.far.at[0], self.s["dx"], p.plane(p.tx)).start()
        w.copy(self.b, self.far.at[1], self.s["dy"], p.plane(p.ty)).start()

    def _add(self, t, which):
        h = self.half

        @pl.loop(0, h // 32)
        def _(i):
            rows = pl.ds(pl.multiple_of(i * 32, 32), 32)
            mine = pl.ds(pl.multiple_of(which * h + i * 32, 32), 32)
            total = self.part[t, mine, :].astype(f32) + self.far[which, rows, :].astype(f32)
            self.part[t, mine, :] = total.astype(bf16)

    def arrive(self):
        p = self.w.place
        self.w.landed(self.far.at[0], self.s["dx"])
        self._add(p.ty, 0)
        self.w.landed(self.far.at[1], self.s["dy"])
        self._add(p.tx, 1)

    def to_y(self):
        p, w = self.w.place, self.w
        w.copy(self.part.at[p.ty], self.near.at[1], self.s["y"], p.plane(p.ty)).start()

    def to_x(self):
        p, w = self.w.place, self.w
        w.copy(self.part.at[p.tx], self.near.at[0], self.s["x"], p.plane(p.tx)).start()

    def finish(self):
        self.w.landed(self.near.at[0], self.s["x"])
        self.w.landed(self.near.at[1], self.s["y"])

    def drain(self):
        p, w = self.w.place, self.w
        w.sent(self.a, self.s["dx"])
        w.sent(self.b, self.s["dy"])
        w.sent(self.part.at[p.ty], self.s["y"])
        w.sent(self.part.at[p.tx], self.s["x"])


def add_into(dst, *sources):
    lead, rows = dst.shape[:-2], dst.shape[-2]
    size = 64 if rows % 64 == 0 else rows
    count = rows // size
    total = count
    for n in lead:
        total *= n

    @pl.loop(0, total)
    def _(i):
        at = []
        rest = lax.div(i, count)
        for n in reversed(lead):
            at.insert(0, lax.rem(rest, n))
            rest = lax.div(rest, n)
        at.append(pl.ds(pl.multiple_of(lax.rem(i, count) * size, size), size))
        at = tuple(at)
        value = dst.at[at][...].astype(f32)
        for src in sources:
            value = value + src.at[at][...].astype(f32)
        dst.at[at][...] = value.astype(bf16)


class CoreSum:
    def __init__(self, w, half, landing):
        self.w, self.half, self.landing = w, half, landing
        self.slot = w.slot()

    def start(self):
        p = self.w.place
        self.w.copy(self.half(1 - p.c), self.landing, self.slot, p.partner()).start()

    def finish(self):
        self.w.landed(self.landing, self.slot)
        add_into(self.half(self.w.place.c), self.landing)

    def drain(self):
        self.w.sent(self.half(1 - self.w.place.c), self.slot)


class LineSum:
    def __init__(self, w, parts, odd=None):
        self.w, self.parts, self.odd = w, parts, odd
        self.slots = [[w.slot() for _ in range(6)] for _ in parts]
        if odd is not None:
            self.odd_slots = w.block(3)

    def _each(self, act, ok):
        @pl.when(ok)
        def _():
            for (piece, landing), slots in zip(self.parts, self.slots):
                act(piece, landing, slots)

    def _send(self, k, act, which):
        z = self.w.place.z
        for side, sign in ((0, 1), (1, -1)):
            j = z + sign * (4 - k)
            end = z == 0 if sign > 0 else z == 3
            inner = jnp.logical_and(z > 0, z < 3)
            there = j <= 3 if sign > 0 else j >= 0
            valid = end if which == "end" else jnp.logical_and(inner, there)
            self._each(lambda piece, landing, s: act(piece, landing, s[side * 3 + k - 1], side, k, j, sign), valid)

    def _out(self, piece, landing, slot, side, k, j, sign):
        p = self.w.place
        self.w.copy(piece(j), landing(side, k), slot, p.line(p.z + sign)).start()

    def first(self):
        p = self.w.place
        for k in (1, 2, 3):
            self._send(k, self._out, "end")
        if self.odd is not None:
            piece, landing = self.odd

            @pl.when(p.z != p.t)
            def _():
                k = lax.rem(p.t - p.z + 4, 4) - 1
                self.w.copy(piece, landing(k), self.odd_slots + k, p.line(p.t)).start()

    def _take(self, k):
        z = self.w.place.z
        for side, sign in ((0, 1), (1, -1)):
            j = z - sign + sign * (4 - k)
            valid = jnp.logical_and(j <= 3, z >= 1) if sign > 0 else jnp.logical_and(j >= 0, z <= 2)

            def act(piece, landing, s):
                self.w.landed(landing(side, k), s[side * 3 + k - 1])
                add_into(piece(j), landing(side, k))

            self._each(act, valid)

    def step(self, k):
        self._take(k - 1)
        if k < 4:
            self._send(k, self._out, "inner")
        elif self.odd is not None:
            p = self.w.place
            piece, landing = self.odd

            @pl.when(p.z == p.t)
            def _():
                for n in range(3):
                    self.w.landed(landing(n), self.odd_slots + n)
                add_into(piece, landing(0), landing(1), landing(2))

    def drain(self):
        p = self.w.place
        for k in (1, 2, 3):
            for which in ("end", "inner"):
                self._send(k, lambda piece, landing, slot, side, kk, j, sign: self.w.sent(piece(j), slot), which)
        if self.odd is not None:

            @pl.when(p.z != p.t)
            def _():
                self.w.sent(self.odd[0], self.odd_slots + lax.rem(p.t - p.z + 4, 4) - 1)


class SmallSum:
    def __init__(self, w, places, keep):
        self.w, self.places, self.keep = w, places, keep
        self.slots = [w.block(7) for _ in places]

    def line(self):
        p, w = self.w.place, self.w
        for (own, line, core, plane), s in zip(self.places, self.slots):
            line[p.z] = own[...]
            for k in (1, 2, 3):
                w.copy(own, line.at[p.z], s + k - 1, p.line(p.around(k))).start()

    def core(self):
        p, w = self.w.place, self.w
        for (own, line, core, plane), s in zip(self.places, self.slots):
            for k in (1, 2, 3):
                w.landed(line.at[p.around(4 - k)], s + k - 1)
            core[0] = line[0] + line[1] + line[2] + line[3]
            w.copy(core.at[0], core.at[1], s + 3, p.partner()).start()

    def plane(self):
        p, w = self.w.place, self.w
        for (own, line, core, plane), s in zip(self.places, self.slots):
            w.landed(core.at[1], s + 3)
            core[2] = core[0] + core[1]
            plane[p.t] = core[2]
            for n, peer in enumerate(p.peers):
                w.copy(core.at[2], plane.at[p.t], s + 4 + n, p.plane(peer)).start()

    def result(self):
        p, w = self.w.place, self.w
        values = []
        for (own, line, core, plane), s, keep in zip(self.places, self.slots, self.keep):
            for n, peer in enumerate(p.peers):
                w.landed(plane.at[peer], s + 4 + n)
            values.append(plane[...] if keep else plane[0] + plane[1] + plane[2] + plane[3])
        return values

    def drain(self):
        w = self.w
        for (own, line, core, plane), s in zip(self.places, self.slots):
            for k in (1, 2, 3):
                w.sent(own, s + k - 1)
                w.sent(core.at[2], s + 3 + k)
            w.sent(core.at[0], s + 3)


def stack_rows(v, out):
    for n in range(12):
        out[n : n + 1, :] = v[:, n * 128 : (n + 1) * 128]


class OddScatter:
    def __init__(self, w, part, home):
        self.w, self.part, self.home = w, part, home
        self.slots = [w.slot() for _ in range(3)]
        self.kept = w.held_here(part(w.place.t), home)

    def start(self):
        p = self.w.place

        @pl.when(p.t == p.z)
        def _():
            self.kept.start()
            for peer, slot in zip(p.peers, self.slots):
                self.w.copy(self.part(peer), self.home, slot, p.plane(peer)).start()

    def finish(self):
        p = self.w.place
        for peer, slot in zip(p.peers, self.slots):

            @pl.when(peer == p.z)
            def _():
                self.w.landed(self.home, slot)

        @pl.when(p.t == p.z)
        def _():
            self.kept.wait()
            for peer, slot in zip(p.peers, self.slots):
                self.w.sent(self.part(peer), slot)


def rows16(i, size=16):
    return pl.ds(pl.multiple_of(i * 16, 16), size)


def cols(b, width=128):
    return pl.ds(pl.multiple_of(b * width, width), width)


def norm_rows(v):
    return lax.rsqrt(jnp.mean(v * v, axis=1, keepdims=True) + epsilon)


def log1p_series(y):
    s = y / (2.0 + y)
    q = s * s
    total = 1.0 / 17
    for n in (15, 13, 11, 9, 7, 5, 3, 1):
        total = total * q + 1.0 / n
    return 2.0 * s * total


def turn(src, dst, j):
    @pl.loop(0, 12)
    def _(i):
        dst[cols(i), cols(j, 256)] = src[j, :, cols(i)].T


def fold(state, product):
    rows = [v[0:1, b * 128 : (b + 1) * 128] for v in (state, product) for b in range(4)]
    return jnp.concatenate(rows, axis=0)


def unfold(tile, first):
    return jnp.concatenate([jnp.broadcast_to(tile[first + b : first + b + 1, :], (8, 128)) for b in range(4)], axis=1)


def recurrence_forward(
    x_ref, gain_1d, conv_w, conv_b, gate_bias, decay, wx, wy, wo, gates, wg, wu, wd, cot,
    x1_ref, stat_ref, sm_out,
    n1t_out, win_out, wout_out, wg_out, wu_out, a2d, cot_out, gg_out,
    xb_out, zy_out, zx_out, za_out, c_out, a_out, h_out, o_out,
    win, wout, gg, n1, n1t, xb, zy, zx, za, cc, aa, hh, ac, oo, part, far, near,
    tail, sums, sm_ref, small_ref, gain_ref, send, recv, local,
):
    p = Place()
    w = Wires(p, send, recv, local)
    t, c, z = p.t, p.c, p.z
    odd = pl.ds(1024, 128)
    small_ref[...] = jnp.zeros((16, 512), f32)
    small_ref[0:4, :] = conv_w[...]
    small_ref[4:5, :] = conv_b[...].reshape(1, 512)
    small_ref[5:7, :] = gate_bias[...]
    raw = decay[...].reshape(1, 512)
    small_ref[7:8, :] = jnp.maximum(raw, 0.0) + log1p_series(jnp.exp(-jnp.abs(raw)))
    small_ref[8:9, :] = jax.nn.sigmoid(raw)
    gain_ref[...] = gain_1d[...].reshape(1, 1536)
    p.enter()

    spread_in = Spread(
        w,
        [lambda q: wx.at[:, cols(q)], lambda q: wy.at[:, cols(q)], lambda q: gates.at[:, q]],
        [
            lambda q: win.at[0, q, c, :, cols(z)],
            lambda q: win.at[1, q, c, :, cols(z)],
            lambda q: gg.at[:, z, q, c],
        ],
    )
    spread_out = Spread(w, [lambda q: wo.at[:, cols(q)]], [lambda q: wout.at[q, c, :, cols(z)]])

    def wide(weight, home, odd_home):
        return (
            Spread(w, [lambda q: weight.at[:, cols(q, 256)]], [home]),
            OneSpread(w, weight.at[:, odd], odd_home),
        )

    spreads = [
        wide(wg, lambda q: wg_out.at[q, c, :, cols(z, 256)], lambda q: wg_out.at[q, c, :, odd]),
        wide(wu, lambda q: wu_out.at[q, c, :, cols(z, 256)], lambda q: wu_out.at[q, c, :, odd]),
        wide(wd, lambda q: a2d.at[q, :, pl.ds(0, 256)], lambda q: a2d.at[q, :, pl.ds(256, 128)]),
    ]

    def wide_line(full):
        return LineGather(
            w, [(lambda b, q: full.at[:, q, :, cols(b, 256)], False), (lambda b, q: full.at[:, q, :, odd], True)]
        )

    line_in = LineGather(
        w, [(lambda b, q: win.at[:, :, q, :, cols(b)], False), (lambda b, q: gg.at[:, b, :, q], False)]
    )
    line_out = LineGather(w, [(lambda b, q: wout.at[:, q, :, cols(b)], False)])
    line_g, line_u = wide_line(wg_out), wide_line(wu_out)

    spread_in.start()
    small_slots = [w.slot() for _ in range(3)]
    for k in (1, 2, 3):
        w.copy(
            small_ref.at[:, cols(t)], sm_ref.at[:, cols(z)], small_slots[k - 1], p.line(p.around(k))
        ).start()
    sm_ref[:, cols(z)] = small_ref[:, cols(t)]

    @pl.loop(0, 16)
    def _(i):
        v = x_ref[rows16(i), :].astype(f32)
        n1[t, rows16(i), :] = (v * norm_rows(v) * gain_ref[...]).astype(bf16)

    gather = PlaneGather(w, n1)
    gather.start()
    spread_in.wait()
    line_in.first()
    turn(n1, n1t, t)
    line_in.step(2)
    gather.forward()
    spread_out.start()
    for part_spread in spreads[0] + spreads[1]:
        part_spread.start()
    turn(n1, n1t, p.tx)
    turn(n1, n1t, p.ty)
    line_in.step(3)
    spread_out.wait()
    line_out.first()
    line_in.step(4)
    line_in.finish()
    kept = [w.here(win, win_out), w.here(gg, gg_out)]
    gather.finish()
    gather_cot = PlaneGather(w, cot_out)
    gather_cot.start(cot)

    @pl.loop(0, 4)
    def _(j):
        xb[j, pl.ds(8, 256), :] = mm(n1[j], win[0].reshape(1536, 512))

    halo = w.slot()

    @pl.when(z < 3)
    def _():
        w.copy(xb.at[:, pl.ds(256, 8)], xb.at[:, pl.ds(0, 8)], halo, p.line(z + 1)).start()

    @pl.when(z == 0)
    def _():
        xb[:, 0:8, :] = jnp.zeros((4, 8, 512), f32)

    line_out.step(2)
    turn(n1, n1t, p.td)
    kept.append(w.here(n1t, n1t_out))
    for part_spread in spreads[0]:
        part_spread.wait()
    line_g.first()
    for k in (1, 2, 3):
        w.landed(sm_ref.at[:, cols(p.around(4 - k))], small_slots[k - 1])

    @pl.loop(0, 4)
    def _(j):
        zy[j] = mm(n1[j], win[1].reshape(1536, 512))

    line_out.step(3)
    kept.append(w.here(zy, zy_out))

    @pl.when(z > 0)
    def _():
        w.landed(xb.at[:, pl.ds(0, 8)], halo)

    row = lax.broadcasted_iota(jnp.int32, (8, 512), 0)
    zero = jnp.zeros((8, 512), f32)

    def convolve(j):
        @pl.loop(0, 16)
        def _(i):
            v = xb[j, rows16(i, 24), :]
            total = sm_ref[4:5, :] + sm_ref[0:1, :] * v[8:24]
            for k in (1, 2, 3):
                total = total + sm_ref[k : k + 1, :] * v[8 - k : 24 - k]
            cc[j, rows16(i), :] = total.astype(bf16)

        for b in range(4):
            lanes = pl.ds(b * 128, 128)
            left = cc[j, :, lanes]
            zx[j, :, lanes] = mm(left, gg[0, b].reshape(128, 128)) + sm_ref[5:6, lanes]
            za[j, :, lanes] = mm(left, gg[1, b].reshape(128, 128)) + sm_ref[6:7, lanes]

    def scan(j):
        def advance(i, carry):
            state, product = carry
            pre_x, pre_a = zx[j, rows16(i), :], za[j, rows16(i), :]
            rate, entry = jax.nn.sigmoid(pre_a), jax.nn.sigmoid(pre_x)
            zx[j, rows16(i), :] = entry
            za[j, rows16(i), :] = rate
            log_a = -8.0 * rate * sm_ref[7:8, :]
            decay = jnp.exp(log_a)
            mult = jnp.sqrt(one_minus_square(2.0 * log_a, decay))
            index = lax.broadcasted_iota(jnp.int32, (16, 512), 0) + i * 16 + z * 256
            mult = jnp.where(index == 0, 1.0, mult)
            inflow = mult * entry * cc[j, rows16(i), :].astype(f32)
            aa[j, rows16(i), :] = decay
            for half in (0, 8):
                dv, uv = decay[half : half + 8], inflow[half : half + 8]
                for st in (1, 2, 4):
                    ok = row >= st
                    uv = uv + jnp.where(ok, dv * pltpu.roll(uv, st, 0), 0.0)
                    dv = jnp.where(ok, dv * pltpu.roll(dv, st, 0), dv)
                hv, pv = uv + dv * state, dv * product
                hh[j, pl.ds(pl.multiple_of(i * 16 + half + 8, 8), 8), :] = hv
                ac[j, pl.ds(pl.multiple_of(i * 16 + half, 8), 8), :] = pv
                state = jnp.broadcast_to(hv[7:8, :], (8, 512))
                product = jnp.broadcast_to(pv[7:8, :], (8, 512))
            return state, product

        state, product = lax.fori_loop(0, 16, advance, (zero, zero + 1.0))
        tail[j] = fold(state, product)

    tail_slots = w.block(12)

    def tell(n, j):
        for away in (1, 2, 3):

            @pl.when(z + away <= 3)
            def _():
                w.copy(tail.at[j], sums.at[z, j], tail_slots + 3 * n + away - 1, p.line(z + away)).start()

    def settle(n, j):
        for away in (1, 2, 3):

            @pl.when(z >= away)
            def _():
                w.landed(sums.at[z - away, j], tail_slots + 3 * n + away - 1)

        enter = zero
        for src in range(3):
            tile = sums[src, j]
            enter = jnp.where(z > src, unfold(tile, 0) + unfold(tile, 4) * enter, enter)
        hh[j, 0:8, :] = enter
        first = jnp.concatenate([enter, enter], axis=0)

        @pl.loop(0, 16)
        def _(i):
            at = pl.ds(pl.multiple_of(i * 16 + 8, 8), 16)
            hv = hh[j, at, :] + ac[j, rows16(i), :] * first
            hh[j, at, :] = hv
            oo[j, rows16(i), :] = (hv * gelu_value(zy[j, rows16(i), :])).astype(bf16)

    def project(j):
        for n in range(2):
            part[j, :, n * 768 : (n + 1) * 768] = mm_nt(
                oo[j], wout[2 * n : 2 * n + 2].reshape(768, 512)
            ).astype(bf16)

    summed = PlaneSum(w, part, far, near)
    kept_out = w.held_here(wout, wout_out)

    @pl.loop(0, 5)
    def _(k):
        @pl.when(k < 4)
        def _():
            j = p.member(3 - k)
            convolve(j)
            scan(j)
            tell(k, j)

        @pl.when(k == 0)
        def _():
            line_out.step(4)
            line_g.step(2)
            for part_spread in spreads[1]:
                part_spread.wait()
            line_u.first()

        @pl.when(k == 1)
        def _():
            line_out.finish()
            kept_out.start()

        @pl.when(k == 2)
        def _():
            line_g.step(3)
            line_u.step(2)

        @pl.when(k == 3)
        def _():
            gather_cot.forward()

        @pl.when(k > 0)
        def _():
            j = p.member(4 - k)
            settle(k - 1, j)
            project(j)

        @pl.when(k == 1)
        def _():
            summed.diagonal()

        @pl.when(k == 3)
        def _():
            summed.arrive()
            summed.to_y()
            summed.to_x()

    for part_spread in spreads[2]:
        part_spread.start()
    kept += [w.here(xb, xb_out), w.here(cc, c_out), w.here(zx, zx_out), w.here(za, za_out)]
    kept += [kept_out, w.here(hh, h_out), w.here(oo, o_out)]
    next_slot = w.slot()

    @pl.when(z > 0)
    def _():
        w.copy(aa.at[:, pl.ds(0, 8)], aa.at[:, pl.ds(256, 8)], next_slot, p.line(z - 1)).start()

    @pl.when(z == 3)
    def _():
        aa[:, 256:264, :] = jnp.zeros((4, 8, 512), f32)

    line_g.step(4)
    line_u.step(3)

    @pl.when(z < 3)
    def _():
        w.landed(aa.at[:, pl.ds(256, 8)], next_slot)

    kept.append(w.here(aa, a_out))
    line_g.finish()
    gather_cot.finish()
    summed.finish()

    def last(i, carry):
        at = rows16(i)
        branch = part[t, at, :].astype(f32) + near[0, at, :].astype(f32) + near[1, at, :].astype(f32)
        stream = x_ref[at, :].astype(f32) + branch
        x1_ref[at, :] = stream
        s2, b2 = stream * stream, branch * branch
        return carry[0] + s2[0:8] + s2[8:16], carry[1] + b2[0:8] + b2[8:16]

    zw = jnp.zeros((8, 1536), f32)
    s2, b2 = lax.fori_loop(0, 16, last, (zw, zw))
    stat_ref[...] = zw
    stat_ref[0:1, :] = jnp.sum(s2, axis=0, keepdims=True)
    stat_ref[1:2, :] = jnp.sum(b2, axis=0, keepdims=True)
    sm_out[...] = sm_ref[...]
    line_u.step(4)
    line_u.finish()
    for part_spread in spreads[2]:
        part_spread.wait()
    for made in kept:
        made.wait()
    spread_in.drain()
    spread_out.drain()
    for pair in spreads:
        for part_spread in pair:
            part_spread.drain()
    for k in (1, 2, 3):
        w.sent(small_ref.at[:, cols(t)], small_slots[k - 1])
    gather.drain()
    gather_cot.drain()
    line_in.drain()
    line_out.drain()
    line_g.drain()
    line_u.drain()

    @pl.when(z < 3)
    def _():
        w.sent(xb.at[:, pl.ds(256, 8)], halo)

    for n in range(4):
        for away in (1, 2, 3):

            @pl.when(z + away <= 3)
            def _():
                w.sent(tail.at[n], tail_slots + 3 * n + away - 1)

    @pl.when(z > 0)
    def _():
        w.sent(aa.at[:, pl.ds(0, 8)], next_slot)

    summed.drain()


def shape(dims, dtype):
    return jax.ShapeDtypeStruct(dims, dtype)


def call(kernel, number, args, spaces, outs, out_spaces, scratch, wires, locals_, name):
    v = pl.BlockSpec(memory_space=pltpu.VMEM)
    a = pl.BlockSpec(memory_space=pl.ANY)
    kinds = {"v": v, "a": a}
    return pl.pallas_call(
        kernel,
        out_shape=outs,
        in_specs=[kinds[k] for k in spaces],
        out_specs=[kinds[k] for k in out_spaces],
        scratch_shapes=list(scratch)
        + [
            pltpu.SemaphoreType.DMA((wires,)),
            pltpu.SemaphoreType.DMA((wires,)),
            pltpu.SemaphoreType.DMA((locals_,)),
        ],
        compiler_params=pltpu.CompilerParams(
            collective_id=number, has_side_effects=True, vmem_limit_bytes=VMEM_BYTES
        ),
        name=name,
    )(*args)


def forward_recurrence(*args):
    V = pltpu.VMEM
    outs = [
        shape((256, 1536), f32), shape((8, 1536), f32), shape((16, 512), f32),
        shape((1536, 1024), bf16), shape((2, 4, 2, 192, 512), bf16), shape((4, 2, 192, 512), bf16),
        shape((4, 2, 192, 1152), bf16), shape((4, 2, 192, 1152), bf16), shape((4, 192, 384), bf16),
        shape((4, 256, 1536), bf16), shape((2, 4, 4, 2, 16, 128), bf16),
        shape((4, 264, 512), f32), shape((4, 256, 512), f32), shape((4, 256, 512), f32),
        shape((4, 256, 512), f32), shape((4, 256, 512), bf16), shape((4, 264, 512), f32),
        shape((4, 264, 512), f32), shape((4, 256, 512), bf16),
    ]
    scratch = [
        V((2, 4, 2, 192, 512), bf16), V((4, 2, 192, 512), bf16), V((2, 4, 4, 2, 16, 128), bf16),
        V((4, 256, 1536), bf16), V((1536, 1024), bf16), V((4, 264, 512), f32), V((4, 256, 512), f32),
        V((4, 256, 512), f32), V((4, 256, 512), f32), V((4, 256, 512), bf16),
        V((4, 264, 512), f32), V((4, 264, 512), f32), V((4, 256, 512), f32),
        V((4, 256, 512), bf16), V((4, 256, 1536), bf16), V((2, 128, 1536), bf16),
        V((2, 256, 1536), bf16),
        V((4, 8, 128), f32), V((4, 4, 8, 128), f32), V((16, 512), f32), V((16, 512), f32), V((1, 1536), f32),
    ]
    return call(
        recurrence_forward, 0, args, "v" * 6 + "a" * 8,
        outs, "vvv" + "a" * 16, scratch, 160, 32, "recurrence_forward",
    )


def half_line(w, piece, landing, odd_piece=None, odd_landing=None):
    odd = None if odd_piece is None else (odd_piece, lambda n: odd_landing.at[n])
    return LineSum(w, [(piece, lambda s, k: landing.at[s * 3 + k - 1])], odd)


def feed_forward(
    x1_ref, gain_1d, cot_ref, cot_in, wg_in, wu_in, a2d,
    dx1_ref, y_ref, stat_ref, half_out, piece_out,
    wgu, wd, n2, n2t, ct, ctt, gu, hid, dgu, part, far, near,
    gdown, cb, landing, landing_odd, gain_ref, send, recv, local,
):
    p = Place()
    w = Wires(p, send, recv, local)
    t, c, z = p.t, p.c, p.z
    gain_ref[...] = gain_1d[...].reshape(1, 1536)
    p.enter()
    odd = pl.ds(1024, 128)

    first = w.here(a2d.at[:, :, pl.ds(0, 256)], wd.at[:, c, :, cols(z, 256)])
    first_odd = w.held_here(a2d.at[:, :, pl.ds(256, 128)], wd.at[:, c, :, odd])

    @pl.when(t == z)
    def _():
        first_odd.start()

    load_gate, load_up = w.here(wg_in, wgu.at[0]), w.here(wu_in, wgu.at[1])
    load_cot = [w.here(cot_in.at[j], ct.at[j]) for j in p.peers]

    @pl.loop(0, 16)
    def _(i):
        at = rows16(i)
        v = x1_ref[at, :]
        n2[t, at, :] = (v * norm_rows(v) * gain_ref[...]).astype(bf16)
        ct[t, at, :] = cot_ref[at, :]

    gather = PlaneGather(w, n2)
    gather.start()
    first.wait()

    @pl.when(t == z)
    def _():
        first_odd.wait()

    line_d = LineGather(
        w, [(lambda b, q: wd.at[:, q, :, cols(b, 256)], False), (lambda b, q: wd.at[:, q, :, odd], True)]
    )
    line_d.first()
    load_gate.wait()
    load_up.wait()

    @pl.loop(0, 4)
    def _(k):
        @pl.when(k == 1)
        def _():
            for made in load_cot:
                made.wait()

            @pl.loop(0, 4)
            def _(n):
                turn(ct, ctt, n)

            line_d.step(2)
            gather.forward()
            line_d.step(3)

        @pl.when(k == 3)
        def _():
            gather.finish()

        j = p.member(k)

        @pl.loop(0, 2)
        def _(m):
            gu[m, j] = mm(n2[j], wgu[m].reshape(1536, 1152))

        @pl.loop(0, 16)
        def _(i):
            at = rows16(i)
            value, slope = gelu_pair(gu[0, j, at, :])
            u = gu[1, j, at, :]
            hid[j, at, :] = (value * u).astype(bf16)
            gu[0, j, at, :] = u * slope
            gu[1, j, at, :] = value

        @pl.when(k < 3)
        def _():
            turn(n2, n2t, j)

    line_d.step(4)
    line_d.finish()

    def weight_grad(left, right, out, first, count):
        @pl.loop(first, first + count)
        def _(i):
            out[i] = mm(left[cols(i, 384), :], right[...].reshape(1024, 1152)).astype(bf16).reshape(2, 192, 1152)

    def half_unit(home, u, n):
        return half_line(
            w,
            lambda j: home.at[pl.ds(2 * u, 2), c, :, cols(j, 256)],
            landing.at[n],
            home.at[pl.ds(2 * u, 2), c, :, odd],
            landing_odd.at[n],
        )

    units = [half_unit(gdown, 0, 0), half_unit(gdown, 1, 1), half_unit(wgu.at[0], 0, 2)]
    cores = [
        CoreSum(w, lambda q, u=u: gdown.at[pl.ds(2 * u, 2), q], cb.at[0, pl.ds(2 * u, 2)]) for u in range(2)
    ]
    cores_gu = [CoreSum(w, lambda q, m=m: wgu.at[m, :, q], cb.at[1 - m]) for m in range(2)]
    summed = PlaneSum(w, part, far, near)
    near_m = n2.at[pl.ds(0, 2)]
    branch = PlaneSum(w, ct, far, near_m)

    def mid(j):
        for n in range(2):
            ct[j, :, n * 768 : (n + 1) * 768] = mm_nt(
                hid[j], wd[2 * n : 2 * n + 2].reshape(768, 1152)
            ).astype(bf16)

    @pl.loop(0, 4)
    def _(k):
        j = p.member(3 - k)
        dh = mm(ct[j], wd[...].reshape(1536, 1152))
        for m in range(2):
            dgu[m, j] = (dh * gu[m, j]).astype(bf16)

        for n in range(2):
            span = pl.ds(2 * n, 2)
            part[j, :, n * 768 : (n + 1) * 768] = (
                mm_nt(dgu[0, j], wgu[0, span].reshape(768, 1152)) + mm_nt(dgu[1, j], wgu[1, span].reshape(768, 1152))
            ).astype(bf16)

        @pl.when(k == 0)
        def _():
            summed.diagonal()
            turn(n2, n2t, p.td)

        @pl.when(k == 1)
        def _():
            cores[0].finish()
            units[0].first()

        @pl.when(k == 2)
        def _():
            summed.arrive()
            summed.to_y()
            summed.to_x()
            cores[1].finish()
            units[1].first()

        @pl.when(k < 2)
        def _():
            weight_grad(ctt, hid, gdown, 2 * k, 2)

        @pl.when(k == 0)
        def _():
            cores[0].start()

        @pl.when(k == 1)
        def _():
            cores[1].start()

    units[0].step(2)

    @pl.loop(0, 2)
    def _(m):
        weight_grad(n2t, dgu.at[m], wgu.at[m], 0, 4)

        @pl.when(m == 0)
        def _():
            cores_gu[0].start()
            units[0].step(3)

        @pl.when(m == 1)
        def _():
            cores_gu[0].finish()
            cores_gu[1].start()
            units[2].first()

        for i in range(2):
            mid(p.member(3 - 2 * m - i))

    units[0].step(4)
    units[1].step(2)
    summed.finish()
    gather.drain()
    branch.diagonal()

    def dx(i, carry):
        at = rows16(i)
        v = x1_ref[at, :]
        s = norm_rows(v)
        dn = part[t, at, :].astype(f32) + near[0, at, :].astype(f32) + near[1, at, :].astype(f32)
        q = gain_ref[...] * dn
        dx1_ref[at, :] = (
            cot_ref[at, :].astype(f32) + s * q - v * (s * s * s * jnp.mean(q * v, axis=1, keepdims=True))
        )
        g2 = dn * v * s
        return carry + g2[0:8] + g2[8:16]

    zw = jnp.zeros((8, 1536), f32)
    g2 = lax.fori_loop(0, 16, dx, zw)
    stat_ref[...] = zw
    stat_ref[4:5, :] = jnp.sum(g2, axis=0, keepdims=True)
    units[1].step(3)
    cores_gu[1].finish()
    kept = [w.here(wgu.at[1, :, c], half_out.at[1])]
    branch.arrive()
    branch.to_y()
    branch.to_x()
    units[1].step(4)
    for src, dst in ((cols(z, 256), pl.ds(0, 256)), (odd, pl.ds(256, 128))):
        kept.append(w.here(gdown.at[:, c, :, src], piece_out.at[:, :, dst]))
    units[2].step(2)
    units[2].step(3)
    units[2].step(4)
    kept.append(w.here(wgu.at[0, :, c], half_out.at[0]))
    branch.finish()

    def last(i, carry):
        at = rows16(i)
        m = ct[t, at, :].astype(f32) + n2[0, at, :].astype(f32) + n2[1, at, :].astype(f32)
        y = x1_ref[at, :] + m
        y_ref[at, :] = y.astype(bf16)
        m2, y2 = m * m, y * y
        return carry[0] + m2[0:8] + m2[8:16], carry[1] + y2[0:8] + y2[8:16]

    m2, y2 = lax.fori_loop(0, 16, last, (zw, zw))
    stat_ref[2:3, :] = jnp.sum(m2, axis=0, keepdims=True)
    stat_ref[3:4, :] = jnp.sum(y2, axis=0, keepdims=True)
    for made in kept:
        made.wait()
    line_d.drain()
    summed.drain()
    branch.drain()
    for unit in units + cores + cores_gu:
        unit.drain()


def recurrence_backward(
    x_ref, gain_1d, dx1_ref, sm_ref, stat1, stat2,
    win_in, wout_in, n1t_in, xb_in, zy_in, zx_in, za_in, c_in, a_in, h_in, o_in, gg_in,
    half_in, piece_in,
    gi_ref, v1_ref, v2_ref, v3_ref, gin_out, gout_out, gff_out, gd_out, ggate_out,
    win, wout, n1t, dr, xb, zy, zx, za, cc, aa, hh, oo, gg, hgu, tmp, bc, dzy, dzx, dza,
    far, near, gin, gout, ggr, cbi, cbo, cbg, land_i, land_o, land_g, land_f, land_fo,
    tail, sums, acc8, early_own, late_own, acc8_l, acc8_c, acc8_p, early_l, early_c, early_p, late_l, late_c, late_p,
    gain_ref, acc, send, recv, local,
):
    p = Place()
    w = Wires(p, send, recv, local)
    t, c, z = p.t, p.c, p.z
    gain_ref[...] = gain_1d[...].reshape(1, 1536)
    p.enter()
    odd = pl.ds(1024, 128)

    load_half = w.here(half_in, hgu)
    load_out = w.here(wout_in, wout)
    early = [w.here(a, b) for a, b in ((zy_in, zy), (h_in, hh), (a_in, aa))]
    later = [
        w.here(a, b)
        for a, b in (
            (o_in, oo), (zx_in, zx), (za_in, za), (c_in, cc), (gg_in, gg), (n1t_in, n1t), (xb_in, xb), (win_in, win),
        )
    ]

    @pl.loop(0, 16)
    def _(i):
        dr[t, rows16(i), :] = dx1_ref[rows16(i), :].astype(bf16)

    gather = PlaneGather(w, dr)
    gather.start()
    units = [
        half_line(
            w,
            lambda j, m=m, u=u: hgu.at[m, pl.ds(2 * u, 2), :, cols(j, 256)],
            land_f.at[n],
            hgu.at[m, pl.ds(2 * u, 2), :, odd],
            land_fo.at[n],
        )
        for n, (m, u) in enumerate(((0, 1), (1, 0), (1, 1)))
    ]
    line_o = half_line(w, lambda j: gout.at[:, c, :, cols(j)], land_o)
    line_y = half_line(w, lambda j: gin.at[1, :, c, :, cols(j)], land_i.at[1])
    line_x = LineSum(
        w,
        [
            (lambda j: gin.at[0, :, c, :, cols(j)], lambda s, k: land_i.at[0, s * 3 + k - 1]),
            (lambda j: ggr.at[:, j, :, c], lambda s, k: land_g.at[s * 3 + k - 1]),
        ],
    )

    load_half.wait()
    for unit in units:
        unit.first()
    load_out.wait()
    for made in early:
        made.wait()

    row = lax.broadcasted_iota(jnp.int32, (8, 512), 0)
    zero = jnp.zeros((8, 512), f32)

    def scan_rows(j):
        tmp[...] = mm(dr[j], wout[...].reshape(1536, 512))

        def step(k, carry):
            i = 15 - k
            state, product = carry
            at = rows16(i)
            value, slope = gelu_pair(zy[j, at, :])
            do = tmp[at, :]
            h = hh[j, pl.ds(pl.multiple_of(i * 16 + 8, 8), 16), :]
            dzy[j, at, :] = (do * h * slope).astype(bf16)
            flow = do * value
            follow = aa[j, rows16(i, 24), :][1:17]
            for half in (8, 0):
                uv, dv = flow[half : half + 8], follow[half : half + 8]
                for st in (1, 2, 4):
                    ok = row < 8 - st
                    uv = uv + jnp.where(ok, dv * pltpu.roll(uv, 8 - st, 0), 0.0)
                    dv = jnp.where(ok, dv * pltpu.roll(dv, 8 - st, 0), dv)
                gv, pv = uv + dv * state, dv * product
                here = pl.ds(pl.multiple_of(i * 16 + half, 8), 8)
                zy[j, here, :] = gv
                bc[j, here, :] = pv
                state = jnp.broadcast_to(gv[0:1, :], (8, 512))
                product = jnp.broadcast_to(pv[0:1, :], (8, 512))
            return state, product

        state, product = lax.fori_loop(0, 16, step, (zero, zero + 1.0))
        tail[j] = fold(state, product)

    tail_slots = w.block(12)
    down = Spread(
        w, [lambda q: piece_in.at[q, :, pl.ds(0, 256)]], [lambda q: gd_out.at[:, cols(q, 256)]]
    )
    down_odd = OddScatter(w, lambda q: piece_in.at[q, :, pl.ds(256, 128)], gd_out.at[:, odd])

    @pl.loop(0, 4)
    def _(k):
        @pl.when(k == 1)
        def _():
            units[0].step(2)
            gather.forward()
            units[0].step(3)


        @pl.when(k == 3)
        def _():
            gather.finish()
            down.start()
            down_odd.start()

        j = p.member(k)
        scan_rows(j)
        for away in (1, 2, 3):

            @pl.when(z >= away)
            def _():
                w.copy(tail.at[j], sums.at[z, j], tail_slots + 3 * k + away - 1, p.line(z - away)).start()

    units[0].step(4)
    units[1].step(2)
    for made in later:
        made.wait()

    @pl.loop(0, 4)
    def _(i):
        gout[i] = (
            mm_tn(dr[:, :, cols(i, 384)].reshape(1024, 384), oo[...].reshape(1024, 512))
            .astype(bf16)
            .reshape(2, 192, 512)
        )

    core_o = CoreSum(w, lambda q: gout.at[:, q], cbo)
    core_o.start()
    units[1].step(3)

    def in_grad(m, right):
        @pl.loop(0, 4)
        def _(i):
            gin[m, i] = mm(n1t[cols(i, 384), :], right[...].reshape(1024, 512)).astype(bf16).reshape(2, 192, 512)

    in_grad(1, dzy)
    core_y = CoreSum(w, lambda q: gin.at[1, :, q], cbi.at[1])
    core_y.start()
    core_o.finish()
    line_o.first()
    def through(j, carry):
        after = zero
        for src in (3, 2, 1):
            tile = sums[src, j]
            after = jnp.where(z < src, unfold(tile, 0) + unfold(tile, 4) * after, after)
        after = jnp.concatenate([after, after], axis=0)

        def step(i, carry):
            sum_x, sum_a, sum_d = carry
            at = rows16(i)
            g = zy[j, at, :] + bc[j, at, :] * after
            before = hh[j, rows16(i, 24), :][7:23]
            entry, rate, value = zx[j, at, :], za[j, at, :], cc[j, at, :].astype(f32)
            log_a = -8.0 * rate * sm_ref[7:8, :]
            decay = aa[j, at, :]
            index = lax.broadcasted_iota(jnp.int32, (16, 512), 0) + i * 16 + z * 256
            start = index == 0
            mult = jnp.where(start, 1.0, jnp.sqrt(one_minus_square(2.0 * log_a, decay)))
            gm = g * mult
            d_entry = gm * value
            bc[j, at, :] = gm * entry
            low_x = (d_entry * entry * (1.0 - entry)).astype(bf16)
            dzx[j, at, :] = low_x
            d_mult = g * entry * value
            d_log = g * before * decay - jnp.where(start, 0.0, d_mult * decay * decay / mult)
            low_a = (d_log * (-8.0 * sm_ref[7:8, :]) * rate * (1.0 - rate)).astype(bf16)
            dza[j, at, :] = low_a
            wide_x, wide_a, d_decay = low_x.astype(f32), low_a.astype(f32), d_log * rate
            return (
                sum_x + wide_x[0:8] + wide_x[8:16],
                sum_a + wide_a[0:8] + wide_a[8:16],
                sum_d + d_decay[0:8] + d_decay[8:16],
            )

        carry = lax.fori_loop(0, 16, step, carry)
        for b in range(4):
            lanes = pl.ds(b * 128, 128)
            bc[j, pl.ds(0, 256), lanes] += mm_nt(
                dzx[j, :, lanes], gg[0, b].reshape(128, 128)
            ) + mm_nt(dza[j, :, lanes], gg[1, b].reshape(128, 128))
        return carry

    def taps(j, carry):
        def step(i, carry):
            at = rows16(i)
            v = bc[j, rows16(i, 24), :]
            xv = xb[j, rows16(i, 24), :]
            total = sm_ref[0:1, :] * v[0:16]
            for k in (1, 2, 3):
                total = total + sm_ref[k : k + 1, :] * v[k : k + 16]
            oo[j, at, :] = total.astype(bf16)
            now = v[0:16]
            new = []
            for k in range(4):
                product = now * xv[8 - k : 24 - k]
                new.append(carry[k] + product[0:8] + product[8:16])
            new.append(carry[4] + now[0:8] + now[8:16])
            return tuple(new)

        return lax.fori_loop(0, 16, step, carry)

    halo_slots = w.block(4)

    def tell(n, j):
        @pl.when(z > 0)
        def _():
            w.copy(
                bc.at[j, pl.ds(0, 8)], bc.at[j, pl.ds(256, 8)], halo_slots + n, p.line(z - 1)
            ).start()

    def hear(n, j):
        @pl.when(z < 3)
        def _():
            w.landed(bc.at[j, pl.ds(256, 8)], halo_slots + n)

    @pl.when(z == 3)
    def _():
        bc[:, 256:264, :] = jnp.zeros((4, 8, 512), f32)

    def gate_grads(i, right):
        for b in range(4):
            lanes = pl.ds(b * 128, 128)
            ggr[i, b] = (
                mm_tn(cc[:, :, lanes].reshape(1024, 128), right[:, :, lanes].reshape(1024, 128))
                .astype(bf16)
                .reshape(4, 2, 16, 128)
            )

    gather.drain()
    summed = PlaneSum(w, dr, far, near)
    core_x = CoreSum(w, lambda q: gin.at[0, :, q], cbi.at[0])
    core_g = CoreSum(w, lambda q: ggr.at[:, :, :, q], cbg)
    spreads = [
        Spread(
            w,
            [lambda q: hgu.at[:, q, :, cols(z, 256)]],
            [lambda q: gff_out.at[:, :, cols(q, 256)]],
        ),
        Spread(
            w,
            [lambda q: gout.at[q, c, :, cols(z)], lambda q: gin.at[1, q, c, :, cols(z)]],
            [lambda q: gout_out.at[:, cols(q)], lambda q: gin_out.at[1, :, cols(q)]],
        ),
        Spread(
            w,
            [lambda q: gin.at[0, q, c, :, cols(z)], lambda q: ggr.at[:, z, q, c]],
            [lambda q: gin_out.at[0, :, cols(q)], lambda q: ggate_out.at[:, q]],
        ),
    ]
    odds = [
        OddScatter(w, lambda q: hgu.at[:, q, :, odd], gff_out.at[:, :, odd]),
    ]

    zw = jnp.zeros((8, 1536), f32)
    stats = stat1[...] + stat2[...]
    early_own[...] = jnp.zeros((16, 128), f32)
    stack_rows(stats[4:5, :], early_own)
    for n in range(4):
        early_own[12 + n : 13 + n, :] = jnp.broadcast_to(jnp.sum(stats[n : n + 1, :], axis=1, keepdims=True), (1, 128))
    late_own[...] = jnp.zeros((16, 128), f32)
    small_early = SmallSum(
        w, [(acc8, acc8_l, acc8_c, acc8_p), (early_own, early_l, early_c, early_p)], [True, False]
    )
    small_late = SmallSum(w, [(late_own, late_l, late_c, late_p)], [False])
    acc[...] = jnp.zeros((8, 8, 512), f32)

    @pl.loop(0, 5)
    def _(k):

        @pl.when(k == 4)
        def _():
            gate_grads(0, dzx)
            gate_grads(1, dza)

        @pl.when(k < 4)
        def _():
            j = p.member(3 - k)
            for away in (1, 2, 3):

                @pl.when(z + away <= 3)
                def _():
                    w.landed(sums.at[z + away, j], tail_slots + 3 * (3 - k) + away - 1)

            for n, value in enumerate(through(j, (zero,) * 3)):
                acc[n] += value
            tell(k, j)

        @pl.when(k > 0)
        def _():
            j = p.member(4 - k)
            hear(k - 1, j)
            for n, value in enumerate(taps(j, (zero,) * 5)):
                acc[3 + n] += value
            for n in range(2):
                span = pl.ds(2 * n, 2)
                dr[j, :, n * 768 : (n + 1) * 768] = (
                    mm_nt(oo[j], win[0, span].reshape(768, 512)) + mm_nt(dzy[j], win[1, span].reshape(768, 512))
                ).astype(bf16)

        @pl.when(k == 0)
        def _():
            core_y.finish()
            line_y.first()
            units[1].step(4)
            units[2].step(2)

        @pl.when(k == 1)
        def _():
            summed.diagonal()
            units[2].step(3)

        @pl.when(k == 2)
        def _():
            units[2].step(4)
            line_o.step(2)

        @pl.when(k == 3)
        def _():
            summed.arrive()
            summed.to_y()
            summed.to_x()
            line_o.step(3)

        @pl.when(k == 4)
        def _():
            line_o.step(4)
            line_y.step(2)

    in_grad(0, oo)
    core_x.start()
    core_g.start()
    line_y.step(3)
    acc8[5:6, :] = jnp.sum(acc[0], axis=0, keepdims=True)
    acc8[6:7, :] = jnp.sum(acc[1], axis=0, keepdims=True)
    acc8[7:8, :] = -8.0 * sm_ref[8:9, :] * jnp.sum(acc[2], axis=0, keepdims=True)
    for k in range(5):
        acc8[k : k + 1, :] = jnp.sum(acc[3 + k], axis=0, keepdims=True)
    small_early.line()
    core_x.finish()
    core_g.finish()
    line_x.first()
    line_y.step(4)
    small_early.core()
    summed.finish()
    spreads[0].start()
    odds[0].start()
    spreads[1].start()
    line_x.step(2)

    def last(i, carry):
        at = rows16(i)
        v = x_ref[at, :].astype(f32)
        s = norm_rows(v)
        dn = dr[t, at, :].astype(f32) + near[0, at, :].astype(f32) + near[1, at, :].astype(f32)
        q = gain_ref[...] * dn
        gi_ref[at, :] = (
            dx1_ref[at, :] + s * q - v * (s * s * s * jnp.mean(q * v, axis=1, keepdims=True))
        ).astype(bf16)
        g1 = dn * v * s
        return carry + g1[0:8] + g1[8:16]

    g1 = lax.fori_loop(0, 16, last, zw)
    line_x.step(3)
    stack_rows(jnp.sum(g1, axis=0, keepdims=True), late_own)
    small_late.line()
    small_early.plane()
    line_x.step(4)
    spreads[2].start()
    small_late.core()
    small_late.plane()
    v2_ref[...], v1_ref[...] = small_early.result()
    (v3_ref[...],) = small_late.result()

    for made in spreads + [down]:
        made.wait()
        made.drain()
    for made in odds + [down_odd]:
        made.finish()
    small_early.drain()
    small_late.drain()
    summed.drain()
    for made in units + [line_o, line_y, line_x, core_o, core_y, core_x, core_g]:
        made.drain()

    for n in range(4):
        for away in (1, 2, 3):

            @pl.when(z >= away)
            def _():
                w.sent(tail.at[n], tail_slots + 3 * n + away - 1)

    for n in range(4):

        @pl.when(z > 0)
        def _():
            w.sent(bc.at[n, pl.ds(0, 8)], halo_slots + n)


def feed_forward_call(*args):
    V = pltpu.VMEM
    outs = [
        shape((256, 1536), f32), shape((256, 1536), bf16), shape((8, 1536), f32),
        shape((2, 4, 192, 1152), bf16), shape((4, 192, 384), bf16),
    ]
    weights = V((4, 2, 192, 1152), bf16)
    tokens, turned = V((4, 256, 1536), bf16), V((1536, 1024), bf16)
    scratch = [
        V((2, 4, 2, 192, 1152), bf16), weights, tokens, turned, tokens, turned, V((2, 4, 256, 1152), f32),
        V((4, 256, 1152), bf16), V((2, 4, 256, 1152), bf16), tokens, V((2, 128, 1536), bf16),
        V((2, 256, 1536), bf16), weights, V((2, 4, 192, 1152), bf16),
        V((3, 6, 2, 192, 256), bf16), V((3, 3, 2, 192, 128), bf16), V((1, 1536), f32),
    ]
    return call(feed_forward, 1, args, "vvvaaaa", outs, "vvvaa", scratch, 128, 24, "feed_forward")


def backward_recurrence(*args):
    V = pltpu.VMEM
    outs = [
        shape((256, 1536), bf16), shape((16, 128), f32), shape((4, 8, 512), f32), shape((16, 128), f32),
        shape((2, 192, 512), bf16), shape((192, 512), bf16), shape((2, 192, 1152), bf16), shape((192, 1152), bf16),
        shape((2, 4, 16, 128), bf16),
    ]
    tokens, turned = V((4, 256, 1536), bf16), V((1536, 1024), bf16)
    wide, padded, low = V((4, 256, 512), f32), V((4, 264, 512), f32), V((4, 256, 512), bf16)
    scratch = [
        V((2, 4, 2, 192, 512), bf16), V((4, 2, 192, 512), bf16), turned, tokens, padded, wide, wide, wide, low,
        padded, padded, low, V((2, 4, 4, 2, 16, 128), bf16), V((2, 4, 192, 1152), bf16), V((256, 512), f32),
        padded, low, low, low,
        V((2, 128, 1536), bf16), V((2, 256, 1536), bf16),
        V((2, 4, 2, 192, 512), bf16), V((4, 2, 192, 512), bf16), V((2, 4, 4, 2, 16, 128), bf16),
        V((2, 4, 192, 512), bf16), V((4, 192, 512), bf16), V((2, 4, 4, 16, 128), bf16),
        V((2, 6, 4, 192, 128), bf16), V((6, 4, 192, 128), bf16), V((6, 2, 4, 16, 128), bf16),
        V((3, 6, 2, 192, 256), bf16), V((3, 3, 2, 192, 128), bf16),
        V((4, 8, 128), f32), V((4, 4, 8, 128), f32), V((8, 512), f32),
        V((16, 128), f32), V((16, 128), f32), V((4, 8, 512), f32), V((3, 8, 512), f32), V((4, 8, 512), f32),
        V((4, 16, 128), f32), V((3, 16, 128), f32), V((4, 16, 128), f32),
        V((4, 16, 128), f32), V((3, 16, 128), f32), V((4, 16, 128), f32),
        V((1, 1536), f32), V((8, 8, 512), f32),
    ]
    return call(
        recurrence_backward, 2, args, "vvvvvv" + "a" * 14,
        outs, "vvvvaaaaa", scratch, 192, 24, "recurrence_backward",
    )


def finish(count, gin, gout, gff, gd, ggate, y, gi, v1, v2, v3,
           wx, wy, wo, wg, wu, wd, gg, y_out, gi_out, g1, g2, cw, cb, bias, decay, rms, rows, wide):
    wx[...] = gin[0].astype(f32)
    wy[...] = gin[1].astype(f32)
    wo[...] = gout[...].astype(f32)
    wg[...] = gff[0].astype(f32)
    wu[...] = gff[1].astype(f32)
    wd[...] = gd[...].astype(f32)
    y_out[...] = y[...]
    gi_out[...] = gi[...]

    @pl.when(pl.program_id(0) == 0)
    def _():
        gg[...] = ggate[...].astype(f32)
        for n in range(12):
            wide[0:1, n * 128 : (n + 1) * 128] = v3[n : n + 1, :]
            wide[1:2, n * 128 : (n + 1) * 128] = v1[n : n + 1, :]
        g1[...] = wide[0:1, :].reshape(1536)
        g2[...] = wide[1:2, :].reshape(1536)
        for t in range(4):
            for z in range(4):
                rows[:, z * 512 + t * 128 : z * 512 + (t + 1) * 128] = v2[t, :, z * 128 : (z + 1) * 128]
        cw[...] = rows[0:4, :]
        cb[...] = rows[4:5, :].reshape(2048)
        bias[...] = rows[5:7, :]
        decay[...] = rows[7:8, :].reshape(2048)
        root = jnp.sqrt(v1[12:16, :] / count)
        for i in range(4):
            rms[i] = root[i, 0]


def finish_call(count, gin, gout, gff, gd, ggate, y, gi, v1, v2, v3):
    steps = 4

    def sliced(a):
        axis = a.ndim - 2
        block = tuple(n // steps if i == axis else n for i, n in enumerate(a.shape))
        return pl.BlockSpec(block, lambda i: tuple(i if n == axis else 0 for n in range(a.ndim)))

    def whole(a):
        return pl.BlockSpec(a.shape, lambda i: (0,) * len(a.shape))

    one, two = shape((192, 512), f32), shape((192, 1152), f32)
    big = [one, one, one, two, two, two]
    small = [
        shape((1536,), f32), shape((1536,), f32), shape((4, 2048), f32), shape((2048,), f32),
        shape((2, 2048), f32), shape((2048,), f32),
    ]
    gates = shape(ggate.shape, f32)
    tokens = shape(y.shape, bf16)
    return pl.pallas_call(
        functools.partial(finish, count),
        out_shape=big + [gates, tokens, tokens] + small + [shape((4,), f32)],
        grid=(steps,),
        in_specs=[sliced(a) for a in (gin, gout, gff, gd)] + [whole(ggate)] + [sliced(a) for a in (y, gi)] + [whole(v1), whole(v2), whole(v3)],
        out_specs=[sliced(a) for a in big] + [whole(gates), sliced(tokens), sliced(tokens)]
        + [whole(a) for a in small] + [pl.BlockSpec(memory_space=pltpu.SMEM)],
        scratch_shapes=[pltpu.VMEM((8, 2048), f32), pltpu.VMEM((8, 1536), f32)],
        name="finish",
    )(gin, gout, gff, gd, ggate, y, gi, v1, v2, v3)


def fast_local(
    inputs, norm1_gain, w_in_x, w_in_y, conv_w, conv_b, gates, gate_bias, decay_param, w_out,
    norm2_gain, w_gate, w_up, w_down, cotangent,
):
    (x1, stat1, sm, n1t, win, wout, wg, wu, a2d, cot, gg, xb, zy, zx, za, cc, aa, hh, oo) = forward_recurrence(
        inputs, norm1_gain, conv_w, conv_b, gate_bias, decay_param, w_in_x, w_in_y, w_out, gates,
        w_gate, w_up, w_down, cotangent,
    )
    dx1, y, stat2, halves, piece = feed_forward_call(x1, norm2_gain, cotangent, cot, wg, wu, a2d)
    gi, v1, v2, v3, gin, gout, gff, gd, ggate = backward_recurrence(
        inputs, norm1_gain, dx1, sm, stat1, stat2, win, wout, n1t, xb, zy, zx, za, cc, aa, hh, oo, gg,
        halves, piece,
    )
    count = inputs.shape[0] * lax.axis_size("dp") * lax.axis_size("tensor") * inputs.shape[1]
    (gwx, gwy, gwo, gwg, gwu, gwd, ggates, output, grad_inputs, g1, g2, gcw, gcb, gbias, gdecay, rms) = finish_call(
        count, gin, gout, gff, gd, ggate, y, gi, v1, v2, v3
    )
    return (
        output, grad_inputs, g1, gwx, gwy, gcw, gcb, ggates, gbias, gdecay, gwo, g2, gwg, gwu, gwd, rms,
    )


def solution(mesh):
    fits = mesh.shape["dp"] == 8 and mesh.shape["tensor"] == 4
    return jax.shard_map(
        fast_local if fits else local,
        mesh=mesh,
        in_specs=(
            P(("dp", "tensor"), None),
            P(),
            P("dp", "tensor"),
            P("dp", "tensor"),
            P(None, "tensor"),
            P("tensor"),
            P(None, "tensor", "dp", None),
            P(None, "tensor"),
            P("tensor"),
            P("dp", "tensor"),
            P(),
            P("dp", "tensor"),
            P("dp", "tensor"),
            P("dp", "tensor"),
            P(("dp", "tensor"), None),
        ),
        out_specs=(
            P(("dp", "tensor"), None),
            P(("dp", "tensor"), None),
            P(),
            P("dp", "tensor"),
            P("dp", "tensor"),
            P(),
            P(),
            P(None, "tensor", "dp", None),
            P(),
            P(),
            P("dp", "tensor"),
            P(),
            P("dp", "tensor"),
            P("dp", "tensor"),
            P("dp", "tensor"),
            P(),
        ),
        check_vma=False,
    )
```

```python
import functools

import jax
import jax.numpy as jnp
from jax import lax
from jax.experimental import pallas as pl
from jax.experimental.pallas import tpu as pltpu
from jax.sharding import PartitionSpec as P

CONV = 4
SEQ_LEN = 1024


epsilon = 1e-06


def gelu_tanh(value):
    return jax.nn.gelu(value, approximate=True)


def combine(earlier, later):
    return (earlier[0] * later[0], later[0] * earlier[1] + later[1])


def norm_back(value, scale, gain, grad):
    scaled = gain * grad
    return scale * scaled - value * scale * scale * scale * jnp.mean(
        scaled * value, axis=1, keepdims=True
    )


def row_product(left, right):
    return lax.dot_general(
        left, right, (((0,), (0,)), ((), ())), preferred_element_type=jnp.float32
    )


def back_product(left, right):
    return lax.dot_general(
        left, right, (((1,), (1,)), ((), ())), preferred_element_type=jnp.float32
    )


def local(
    inputs,
    norm1_gain,
    w_in_x,
    w_in_y,
    conv_w,
    conv_b,
    gates,
    gate_bias,
    decay_param,
    w_out,
    norm2_gain,
    w_gate,
    w_up,
    w_down,
    cotangent,
):
    row_count = inputs.shape[0]
    model_width = inputs.shape[1]
    tensor_count = lax.axis_size("tensor")
    group_rows = row_count * tensor_count
    seq_count = group_rows // SEQ_LEN
    rec_x, rec_y, rec_o, gate_mats = (
        lax.all_gather(w_in_x, "dp", axis=0, tiled=True),
        lax.all_gather(w_in_y, "dp", axis=0, tiled=True),
        lax.all_gather(w_out, "dp", axis=0, tiled=True),
        lax.all_gather(gates, "dp", axis=2, tiled=True),
    )
    channels = rec_x.shape[1]
    blocks_here = gate_mats.shape[1]
    block_width = gate_mats.shape[3]
    residual = inputs.astype(jnp.float32)
    scale_one = lax.rsqrt(jnp.mean(residual * residual, axis=1, keepdims=True) + epsilon)
    n_one = (residual * scale_one * norm1_gain).astype(jnp.bfloat16)
    full_one = lax.all_gather(n_one, "tensor", axis=0, tiled=True)
    x_branch = jnp.dot(full_one, rec_x, preferred_element_type=jnp.float32)
    y_pre = jnp.dot(full_one, rec_y, preferred_element_type=jnp.float32)
    seq_x = x_branch.reshape(seq_count, SEQ_LEN, channels)
    padded = jnp.pad(seq_x, ((0, 0), (CONV - 1, 0), (0, 0)))
    conv_sum = conv_b + jnp.zeros_like(seq_x)
    for k in range(CONV):
        conv_sum = conv_sum + conv_w[k] * padded[:, CONV - 1 - k : CONV - 1 - k + SEQ_LEN]
    conv_low = conv_sum.reshape(group_rows, channels).astype(jnp.bfloat16)
    conv_value = conv_low.astype(jnp.float32)
    blocked = conv_low.reshape(group_rows, blocks_here, block_width)
    z_input = (
        jnp.einsum(
            "gbi,bij->gbj", blocked, gate_mats[0], preferred_element_type=jnp.float32
        ).reshape(group_rows, channels)
        + gate_bias[0]
    )
    z_decay = (
        jnp.einsum(
            "gbi,bij->gbj", blocked, gate_mats[1], preferred_element_type=jnp.float32
        ).reshape(group_rows, channels)
        + gate_bias[1]
    )
    seq_start = (jnp.arange(group_rows) % SEQ_LEN == 0)[:, None]

    def coefficients(input_pre, decay_pre, conv_part, decay_raw):
        log_decay = -8.0 * jax.nn.sigmoid(decay_pre) * jax.nn.softplus(decay_raw)
        mult = jnp.where(seq_start, 1.0, jnp.sqrt(-jnp.expm1(2.0 * log_decay)))
        return (jnp.exp(log_decay), mult * jax.nn.sigmoid(input_pre) * conv_part)

    (decays, inflow), pull_coeff = jax.vjp(coefficients, z_input, z_decay, conv_value, decay_param)
    seq_decay = decays.reshape(seq_count, SEQ_LEN, channels)
    _, seq_states = lax.associative_scan(
        combine, (seq_decay, inflow.reshape(seq_count, SEQ_LEN, channels)), axis=1
    )
    states = seq_states.reshape(group_rows, channels)
    y_gate = gelu_tanh(y_pre)
    mixed_out = (states * y_gate).astype(jnp.bfloat16)
    branch = lax.psum_scatter(
        back_product(mixed_out, rec_o), "tensor", scatter_dimension=0, tiled=True
    )
    stream = residual + branch
    mlp_g, mlp_u, mlp_d = (
        lax.all_gather(w_gate, "dp", axis=0, tiled=True),
        lax.all_gather(w_up, "dp", axis=0, tiled=True),
        lax.all_gather(w_down, "dp", axis=0, tiled=True),
    )
    scale_two = lax.rsqrt(jnp.mean(stream * stream, axis=1, keepdims=True) + epsilon)
    n_two = (stream * scale_two * norm2_gain).astype(jnp.bfloat16)
    full_two = lax.all_gather(n_two, "tensor", axis=0, tiled=True)
    gate_pre = jnp.dot(full_two, mlp_g, preferred_element_type=jnp.float32)
    up_pre = jnp.dot(full_two, mlp_u, preferred_element_type=jnp.float32)
    hidden = (gelu_tanh(gate_pre) * up_pre).astype(jnp.bfloat16)
    ffn_out = lax.psum_scatter(
        back_product(hidden, mlp_d), "tensor", scatter_dimension=0, tiled=True
    )
    result = stream + ffn_out
    output = result.astype(jnp.bfloat16)
    squares = jnp.stack(
        [
            jnp.sum(stream * stream),
            jnp.sum(branch * branch),
            jnp.sum(ffn_out * ffn_out),
            jnp.sum(result * result),
        ]
    )
    upstream = cotangent.astype(jnp.float32)
    full_cot = lax.all_gather(cotangent, "tensor", axis=0, tiled=True)
    d_hidden = jnp.dot(full_cot, mlp_d, preferred_element_type=jnp.float32)
    grad_down = row_product(full_cot, hidden)
    _, pull_mlp = jax.vjp(
        lambda gate_value, up_value: gelu_tanh(gate_value) * up_value, gate_pre, up_pre
    )
    d_gate, d_up = pull_mlp(d_hidden)
    d_gate_low = d_gate.astype(jnp.bfloat16)
    d_up_low = d_up.astype(jnp.bfloat16)
    grad_gate_w = row_product(full_two, d_gate_low)
    grad_up_w = row_product(full_two, d_up_low)
    d_two = lax.psum_scatter(
        back_product(d_gate_low, mlp_g) + back_product(d_up_low, mlp_u),
        "tensor",
        scatter_dimension=0,
        tiled=True,
    )
    grad_gain_two = jnp.sum(d_two * stream * scale_two, axis=0)
    d_stream = upstream + norm_back(stream, scale_two, norm2_gain, d_two)
    mlp_summed = (grad_gate_w, grad_up_w, grad_down)
    full_branch = lax.all_gather(d_stream.astype(jnp.bfloat16), "tensor", axis=0, tiled=True)
    d_mixed = jnp.dot(full_branch, rec_o, preferred_element_type=jnp.float32)
    grad_out_w = row_product(full_branch, mixed_out)
    d_states = d_mixed * y_gate
    _, pull_gelu = jax.vjp(gelu_tanh, y_pre)
    d_y_low = pull_gelu(d_mixed * states)[0].astype(jnp.bfloat16)
    next_decay = jnp.concatenate([seq_decay[:, 1:], jnp.zeros_like(seq_decay[:, :1])], axis=1)
    _, carried = lax.associative_scan(
        combine, (next_decay, d_states.reshape(seq_count, SEQ_LEN, channels)), reverse=True, axis=1
    )
    prev_states = jnp.concatenate([jnp.zeros_like(seq_states[:, :1]), seq_states[:, :-1]], axis=1)
    d_decays = (carried * prev_states).reshape(group_rows, channels)
    d_input_pre, d_decay_pre, d_conv_direct, grad_decay = pull_coeff(
        (d_decays, carried.reshape(group_rows, channels))
    )
    d_input_low = d_input_pre.astype(jnp.bfloat16)
    d_decay_low = d_decay_pre.astype(jnp.bfloat16)
    grad_bias = jnp.stack(
        [
            jnp.sum(d_input_low, axis=0, dtype=jnp.float32),
            jnp.sum(d_decay_low, axis=0, dtype=jnp.float32),
        ]
    )
    input_blocks = d_input_low.reshape(group_rows, blocks_here, block_width)
    decay_blocks = d_decay_low.reshape(group_rows, blocks_here, block_width)
    grad_gate_mats = jnp.stack(
        [
            jnp.einsum("gbi,gbj->bij", blocked, input_blocks, preferred_element_type=jnp.float32),
            jnp.einsum("gbi,gbj->bij", blocked, decay_blocks, preferred_element_type=jnp.float32),
        ]
    )
    d_conv = d_conv_direct + jnp.einsum(
        "gbj,bij->gbi", input_blocks, gate_mats[0], preferred_element_type=jnp.float32
    ).reshape(group_rows, channels)
    d_conv = d_conv + jnp.einsum(
        "gbj,bij->gbi", decay_blocks, gate_mats[1], preferred_element_type=jnp.float32
    ).reshape(group_rows, channels)
    seq_dconv = d_conv.reshape(seq_count, SEQ_LEN, channels)
    grad_conv_b = jnp.sum(seq_dconv, axis=(0, 1))
    padded_back = jnp.pad(seq_dconv, ((0, 0), (0, CONV - 1), (0, 0)))
    tap_grads = []
    d_x_seq = jnp.zeros_like(seq_dconv)
    for k in range(CONV):
        tap_grads.append(
            jnp.sum(seq_dconv * padded[:, CONV - 1 - k : CONV - 1 - k + SEQ_LEN], axis=(0, 1))
        )
        d_x_seq = d_x_seq + conv_w[k] * padded_back[:, k : k + SEQ_LEN]
    grad_conv_w = jnp.stack(tap_grads)
    d_x_low = d_x_seq.reshape(group_rows, channels).astype(jnp.bfloat16)
    grad_in_x_w = row_product(full_one, d_x_low)
    grad_in_y_w = row_product(full_one, d_y_low)
    d_one = lax.psum_scatter(
        back_product(d_x_low, rec_x) + back_product(d_y_low, rec_y),
        "tensor",
        scatter_dimension=0,
        tiled=True,
    )
    grad_gain_one = jnp.sum(d_one * residual * scale_one, axis=0)
    grad_inputs = (d_stream + norm_back(residual, scale_one, norm1_gain, d_one)).astype(
        jnp.bfloat16
    )
    small_grads = jnp.concatenate(
        [grad_conv_w, grad_conv_b[None], grad_bias, grad_decay[None]], axis=0
    )
    spread_grads = lax.dynamic_update_slice(
        jnp.zeros((small_grads.shape[0], channels * tensor_count), jnp.float32),
        small_grads,
        (0, lax.axis_index("tensor") * channels),
    )
    gain_total, small_total, square_total = lax.psum(
        (jnp.stack([grad_gain_one, grad_gain_two]), spread_grads, squares), ("dp", "tensor")
    )
    stream_rms = jnp.sqrt(
        square_total / (row_count * lax.axis_size("dp") * tensor_count * model_width)
    )
    summed_all = (
        lax.psum_scatter(grad_in_x_w, "dp", scatter_dimension=0, tiled=True),
        lax.psum_scatter(grad_in_y_w, "dp", scatter_dimension=0, tiled=True),
        lax.psum_scatter(grad_out_w, "dp", scatter_dimension=0, tiled=True),
        lax.psum_scatter(grad_gate_mats, "dp", scatter_dimension=2, tiled=True),
        lax.psum_scatter(mlp_summed[0], "dp", scatter_dimension=0, tiled=True),
        lax.psum_scatter(mlp_summed[1], "dp", scatter_dimension=0, tiled=True),
        lax.psum_scatter(mlp_summed[2], "dp", scatter_dimension=0, tiled=True),
    )
    rec_summed = summed_all[:4]
    grad_gate_sum, grad_up_sum, grad_down_sum = (summed_all[4], summed_all[5], summed_all[6])
    return (
        output,
        grad_inputs,
        gain_total[0],
        rec_summed[0],
        rec_summed[1],
        small_total[0:CONV],
        small_total[CONV],
        rec_summed[3],
        small_total[CONV + 1 : CONV + 3],
        small_total[CONV + 3],
        rec_summed[2],
        gain_total[1],
        grad_gate_sum,
        grad_up_sum,
        grad_down_sum,
        stream_rms,
    )


MESH = pl.DeviceIdType.MESH
bf16 = jnp.bfloat16
f32 = jnp.float32
VMEM_BYTES = 67043328


def mm(a, b):
    return jnp.dot(a, b, preferred_element_type=f32)


def mm_nt(a, b):
    return lax.dot_general(a, b, (((1,), (1,)), ((), ())), preferred_element_type=f32)


def mm_tn(a, b):
    return lax.dot_general(a, b, (((0,), (0,)), ((), ())), preferred_element_type=f32)


def gelu_value(x):
    return 0.5 * x * (1.0 + jnp.tanh(0.7978845608028654 * x * (1.0 + 0.044715 * (x * x))))


def gelu_pair(x):
    x2 = x * x
    th = jnp.tanh(0.7978845608028654 * x * (1.0 + 0.044715 * x2))
    cdf = 0.5 * (1.0 + th)
    slope = 0.5 * x * (1.0 - th * th) * (0.7978845608028654 * (1.0 + 0.134145 * x2))
    return x * cdf, cdf + slope


def one_minus_square(x, decay):
    series = x * (
        1.0
        + x * (0.5 + x * (1 / 6 + x * (1 / 24 + x * (1 / 120 + x * (1 / 720 + x * (1 / 5040))))))
    )
    return jnp.where(x > -0.35, -series, 1.0 - decay * decay)


class Place:
    def __init__(self):
        self.d = lax.axis_index("dp")
        self.z = lax.axis_index("tensor")
        self.t = lax.div(self.d, 2)
        self.c = lax.rem(self.d, 2)
        self.tx = self.t + 1 - 2 * lax.rem(self.t, 2)
        self.ty = self.t + 2 - 4 * lax.div(self.t, 2)
        self.td = 3 - self.t
        self.peers = (self.tx, self.ty, self.td)

    def member(self, r):
        x, y = lax.rem(self.t, 2), lax.div(self.t, 2)
        b, e = lax.rem(r, 2), lax.div(r, 2)
        return x + b - 2 * x * b + 2 * (y + e - 2 * y * e)

    def plane(self, t):
        return (2 * t + self.c, self.z)

    def line(self, z):
        return (self.d, z)

    def partner(self):
        return (2 * self.t + 1 - self.c, self.z)

    def around(self, k):
        return lax.rem(self.z + k, 4)

    def enter(self):
        barrier = pltpu.get_barrier_semaphore()
        targets = [self.plane(t) for t in self.peers] + [self.partner()]
        targets += [self.line(self.around(k)) for k in (1, 2, 3)]
        for target in targets:
            pl.semaphore_signal(barrier, inc=1, device_id=target, device_id_type=MESH)
        pl.semaphore_wait(barrier, len(targets))


class Wires:
    def __init__(self, place, send, recv, local):
        self.place, self.send, self.recv, self.local = place, send, recv, local
        self.used, self.used_local = 0, 0

    def slot(self):
        self.used += 1
        assert self.used <= self.send.shape[0]
        return self.used - 1

    def block(self, count):
        self.used += count
        assert self.used <= self.send.shape[0]
        return self.used - count

    def copy(self, src, dst, slot, device):
        return pltpu.make_async_remote_copy(
            src_ref=src,
            dst_ref=dst,
            send_sem=self.send.at[slot],
            recv_sem=self.recv.at[slot],
            device_id=device,
            device_id_type=MESH,
        )

    def landed(self, ref, slot):
        self.copy(ref, ref, slot, self.place.partner()).wait_recv()

    def sent(self, ref, slot):
        self.copy(ref, ref, slot, self.place.partner()).wait_send()

    def held_here(self, src, dst):
        self.used_local += 1
        assert self.used_local <= self.local.shape[0]
        return pltpu.make_async_copy(src, dst, self.local.at[self.used_local - 1])

    def here(self, src, dst):
        made = self.held_here(src, dst)
        made.start()
        return made


class Spread:
    def __init__(self, w, parts, homes):
        self.w, self.parts, self.homes = w, parts, homes
        self.slots = [[w.slot() for _ in range(3)] for _ in parts]
        self.first = w.used_local
        w.used_local += len(parts)

    def _kept(self, act):
        t = self.w.place.t
        for n, (part, home) in enumerate(zip(self.parts, self.homes)):
            act(pltpu.make_async_copy(part(t), home(t), self.w.local.at[self.first + n]))

    def start(self):
        p = self.w.place
        for part, home, slots in zip(self.parts, self.homes, self.slots):
            for peer, slot in zip(p.peers, slots):
                self.w.copy(part(peer), home(p.t), slot, p.plane(peer)).start()
        self._kept(lambda made: made.start())

    def wait(self):
        p = self.w.place
        self._kept(lambda made: made.wait())
        for home, slots in zip(self.homes, self.slots):
            for peer, slot in zip(p.peers, slots):
                self.w.landed(home(peer), slot)

    def drain(self):
        p = self.w.place
        for part, slots in zip(self.parts, self.slots):
            for peer, slot in zip(p.peers, slots):
                self.w.sent(part(peer), slot)


class OneSpread:
    def __init__(self, w, part, home):
        self.w, self.part, self.home = w, part, home
        self.slots = [w.slot() for _ in range(3)]
        self.kept = w.held_here(part, home(w.place.t))

    def start(self):
        p = self.w.place

        @pl.when(p.t == p.z)
        def _():
            self.kept.start()

        for peer, slot in zip(p.peers, self.slots):

            @pl.when(peer == p.z)
            def _():
                self.w.copy(self.part, self.home(p.t), slot, p.plane(peer)).start()

    def wait(self):
        p = self.w.place

        @pl.when(p.t == p.z)
        def _():
            self.kept.wait()
            for peer, slot in zip(p.peers, self.slots):
                self.w.landed(self.home(peer), slot)

    def drain(self):
        p = self.w.place
        for peer, slot in zip(p.peers, self.slots):

            @pl.when(peer == p.z)
            def _():
                self.w.sent(self.part, slot)


class LineGather:
    def __init__(self, w, regions):
        self.w, self.regions = w, regions
        self.slots = [
            {key: w.slot() for key in ["o", "r1", "r2", "r3", "l1", "l2", "l3"]
             + ["or1", "or2", "or3", "ol1", "ol2", "ol3"]}
            for _ in regions
        ]

    def _each(self, b, act, *conditions):
        p = self.w.place
        for (view, odd), slots in zip(self.regions, self.slots):
            terms = list(conditions) + ([b == p.t] if odd else [])
            if not terms:
                act(view, slots)
                continue
            ok = terms[0]
            for term in terms[1:]:
                ok = jnp.logical_and(ok, term)

            @pl.when(ok)
            def _():
                act(view, slots)

    def _start(self, view, b, slot, device):
        p = self.w.place
        self.w.copy(view(b, p.c), view(b, p.c), slot, device).start()

    def first(self):
        p = self.w.place
        z = p.z
        self._each(z, lambda v, s: self._start(v, z, s["r1"], p.line(z + 1)), z < 3)
        self._each(z, lambda v, s: self._start(v, z, s["l1"], p.line(z - 1)), z > 0)
        self._each(z, lambda v, s: self._start(v, z, s["o"], p.partner()))

    def step(self, k):
        p = self.w.place
        z = p.z
        for sign, left in ((1, "r"), (-1, "l")):
            b = z - sign * (k - 1)
            exists = b >= 0 if sign > 0 else b <= 3

            def take(v, s):
                self.w.landed(v(b, p.c), s[f"{left}{k - 1}"])
                if k < 4:

                    @pl.when(z < 3 if sign > 0 else z > 0)
                    def _():
                        self._start(v, b, s[f"{left}{k}"], p.line(z + sign))

                self._start(v, b, s[f"o{left}{k - 1}"], p.partner())

            self._each(b, take, exists)

    def finish(self):
        p = self.w.place
        z = p.z
        other = 1 - p.c
        self._each(z, lambda v, s: self.w.landed(v(z, other), s["o"]))
        for k in (1, 2, 3):
            for sign, left in ((1, "r"), (-1, "l")):
                b = z - sign * k
                exists = b >= 0 if sign > 0 else b <= 3
                self._each(b, lambda v, s: self.w.landed(v(b, other), s[f"o{left}{k}"]), exists)

    def drain(self):
        p = self.w.place
        z = p.z
        self._each(z, lambda v, s: self.w.sent(v(z, p.c), s["o"]))
        for k in (1, 2, 3):
            for sign, left in ((1, "r"), (-1, "l")):
                b = z - sign * k
                exists = b >= 0 if sign > 0 else b <= 3
                self._each(b, lambda v, s: self.w.sent(v(b, p.c), s[f"o{left}{k}"]), exists)
                b2 = z - sign * (k - 1)
                exists2 = b2 >= 0 if sign > 0 else b2 <= 3
                more = z < 3 if sign > 0 else z > 0
                self._each(b2, lambda v, s: self.w.sent(v(b2, p.c), s[f"{left}{k}"]), exists2, more)


class PlaneGather:
    def __init__(self, w, buf):
        self.w, self.buf = w, buf
        self.half = buf.shape[1] // 2
        self.s = {key: w.slot() for key in ("x", "y", "fx", "fy")}

    def _low(self, t):
        return self.buf.at[t, pl.ds(0, self.half)]

    def _high(self, t):
        return self.buf.at[t, pl.ds(self.half, self.half)]

    def start(self, own=None):
        p, w = self.w.place, self.w
        self.own = self.buf.at[p.t] if own is None else own
        w.copy(self.own, self.buf.at[p.t], self.s["x"], p.plane(p.tx)).start()
        w.copy(self.own, self.buf.at[p.t], self.s["y"], p.plane(p.ty)).start()

    def forward(self):
        p, w = self.w.place, self.w
        w.landed(self.buf.at[p.tx], self.s["x"])
        w.copy(self._high(p.tx), self._high(p.tx), self.s["fy"], p.plane(p.ty)).start()
        w.landed(self.buf.at[p.ty], self.s["y"])
        w.copy(self._low(p.ty), self._low(p.ty), self.s["fx"], p.plane(p.tx)).start()

    def finish(self):
        p, w = self.w.place, self.w
        w.landed(self._low(p.td), self.s["fx"])
        w.landed(self._high(p.td), self.s["fy"])

    def drain(self):
        p, w = self.w.place, self.w
        w.sent(self.own, self.s["x"])
        w.sent(self.own, self.s["y"])
        w.sent(self._high(p.tx), self.s["fy"])
        w.sent(self._low(p.ty), self.s["fx"])


class PlaneSum:
    def __init__(self, w, part, far, near):
        self.w, self.part, self.far, self.near = w, part, far, near
        self.half = part.shape[1] // 2
        self.s = {key: w.slot() for key in ("dx", "dy", "x", "y")}

    def diagonal(self):
        p, w, h = self.w.place, self.w, self.half
        self.a = self.part.at[p.td, pl.ds(0, h)]
        self.b = self.part.at[p.td, pl.ds(h, h)]
        w.copy(self.a, self.far.at[0], self.s["dx"], p.plane(p.tx)).start()
        w.copy(self.b, self.far.at[1], self.s["dy"], p.plane(p.ty)).start()

    def _add(self, t, which):
        h = self.half

        @pl.loop(0, h // 32)
        def _(i):
            rows = pl.ds(pl.multiple_of(i * 32, 32), 32)
            mine = pl.ds(pl.multiple_of(which * h + i * 32, 32), 32)
            total = self.part[t, mine, :].astype(f32) + self.far[which, rows, :].astype(f32)
            self.part[t, mine, :] = total.astype(bf16)

    def arrive(self):
        p = self.w.place
        self.w.landed(self.far.at[0], self.s["dx"])
        self._add(p.ty, 0)
        self.w.landed(self.far.at[1], self.s["dy"])
        self._add(p.tx, 1)

    def to_y(self):
        p, w = self.w.place, self.w
        w.copy(self.part.at[p.ty], self.near.at[1], self.s["y"], p.plane(p.ty)).start()

    def to_x(self):
        p, w = self.w.place, self.w
        w.copy(self.part.at[p.tx], self.near.at[0], self.s["x"], p.plane(p.tx)).start()

    def finish(self):
        self.w.landed(self.near.at[0], self.s["x"])
        self.w.landed(self.near.at[1], self.s["y"])

    def drain(self):
        p, w = self.w.place, self.w
        w.sent(self.a, self.s["dx"])
        w.sent(self.b, self.s["dy"])
        w.sent(self.part.at[p.ty], self.s["y"])
        w.sent(self.part.at[p.tx], self.s["x"])


def add_into(dst, *sources):
    lead, rows = dst.shape[:-2], dst.shape[-2]
    size = 64 if rows % 64 == 0 else rows
    count = rows // size
    total = count
    for n in lead:
        total *= n

    @pl.loop(0, total)
    def _(i):
        at = []
        rest = lax.div(i, count)
        for n in reversed(lead):
            at.insert(0, lax.rem(rest, n))
            rest = lax.div(rest, n)
        at.append(pl.ds(pl.multiple_of(lax.rem(i, count) * size, size), size))
        at = tuple(at)
        value = dst.at[at][...].astype(f32)
        for src in sources:
            value = value + src.at[at][...].astype(f32)
        dst.at[at][...] = value.astype(bf16)


class CoreSum:
    def __init__(self, w, half, landing):
        self.w, self.half, self.landing = w, half, landing
        self.slot = w.slot()

    def start(self):
        p = self.w.place
        self.w.copy(self.half(1 - p.c), self.landing, self.slot, p.partner()).start()

    def finish(self):
        self.w.landed(self.landing, self.slot)
        add_into(self.half(self.w.place.c), self.landing)

    def drain(self):
        self.w.sent(self.half(1 - self.w.place.c), self.slot)


class LineSum:
    def __init__(self, w, parts, odd=None):
        self.w, self.parts, self.odd = w, parts, odd
        self.slots = [[w.slot() for _ in range(6)] for _ in parts]
        if odd is not None:
            self.odd_slots = w.block(3)

    def _each(self, act, ok):
        @pl.when(ok)
        def _():
            for (piece, landing), slots in zip(self.parts, self.slots):
                act(piece, landing, slots)

    def _send(self, k, act, which):
        z = self.w.place.z
        for side, sign in ((0, 1), (1, -1)):
            j = z + sign * (4 - k)
            end = z == 0 if sign > 0 else z == 3
            inner = jnp.logical_and(z > 0, z < 3)
            there = j <= 3 if sign > 0 else j >= 0
            valid = end if which == "end" else jnp.logical_and(inner, there)
            self._each(lambda piece, landing, s: act(piece, landing, s[side * 3 + k - 1], side, k, j, sign), valid)

    def _out(self, piece, landing, slot, side, k, j, sign):
        p = self.w.place
        self.w.copy(piece(j), landing(side, k), slot, p.line(p.z + sign)).start()

    def first(self):
        p = self.w.place
        for k in (1, 2, 3):
            self._send(k, self._out, "end")
        if self.odd is not None:
            piece, landing = self.odd

            @pl.when(p.z != p.t)
            def _():
                k = lax.rem(p.t - p.z + 4, 4) - 1
                self.w.copy(piece, landing(k), self.odd_slots + k, p.line(p.t)).start()

    def _take(self, k):
        z = self.w.place.z
        for side, sign in ((0, 1), (1, -1)):
            j = z - sign + sign * (4 - k)
            valid = jnp.logical_and(j <= 3, z >= 1) if sign > 0 else jnp.logical_and(j >= 0, z <= 2)

            def act(piece, landing, s):
                self.w.landed(landing(side, k), s[side * 3 + k - 1])
                add_into(piece(j), landing(side, k))

            self._each(act, valid)

    def step(self, k):
        self._take(k - 1)
        if k < 4:
            self._send(k, self._out, "inner")
        elif self.odd is not None:
            p = self.w.place
            piece, landing = self.odd

            @pl.when(p.z == p.t)
            def _():
                for n in range(3):
                    self.w.landed(landing(n), self.odd_slots + n)
                add_into(piece, landing(0), landing(1), landing(2))

    def drain(self):
        p = self.w.place
        for k in (1, 2, 3):
            for which in ("end", "inner"):
                self._send(k, lambda piece, landing, slot, side, kk, j, sign: self.w.sent(piece(j), slot), which)
        if self.odd is not None:

            @pl.when(p.z != p.t)
            def _():
                self.w.sent(self.odd[0], self.odd_slots + lax.rem(p.t - p.z + 4, 4) - 1)


class SmallSum:
    def __init__(self, w, places, keep):
        self.w, self.places, self.keep = w, places, keep
        self.slots = [w.block(7) for _ in places]

    def line(self):
        p, w = self.w.place, self.w
        for (own, line, core, plane), s in zip(self.places, self.slots):
            line[p.z] = own[...]
            for k in (1, 2, 3):
                w.copy(own, line.at[p.z], s + k - 1, p.line(p.around(k))).start()

    def core(self):
        p, w = self.w.place, self.w
        for (own, line, core, plane), s in zip(self.places, self.slots):
            for k in (1, 2, 3):
                w.landed(line.at[p.around(4 - k)], s + k - 1)
            core[0] = line[0] + line[1] + line[2] + line[3]
            w.copy(core.at[0], core.at[1], s + 3, p.partner()).start()

    def plane(self):
        p, w = self.w.place, self.w
        for (own, line, core, plane), s in zip(self.places, self.slots):
            w.landed(core.at[1], s + 3)
            core[2] = core[0] + core[1]
            plane[p.t] = core[2]
            for n, peer in enumerate(p.peers):
                w.copy(core.at[2], plane.at[p.t], s + 4 + n, p.plane(peer)).start()

    def result(self):
        p, w = self.w.place, self.w
        values = []
        for (own, line, core, plane), s, keep in zip(self.places, self.slots, self.keep):
            for n, peer in enumerate(p.peers):
                w.landed(plane.at[peer], s + 4 + n)
            values.append(plane[...] if keep else plane[0] + plane[1] + plane[2] + plane[3])
        return values

    def drain(self):
        w = self.w
        for (own, line, core, plane), s in zip(self.places, self.slots):
            for k in (1, 2, 3):
                w.sent(own, s + k - 1)
                w.sent(core.at[2], s + 3 + k)
            w.sent(core.at[0], s + 3)


def stack_rows(v, out):
    for n in range(12):
        out[n : n + 1, :] = v[:, n * 128 : (n + 1) * 128]


class OddScatter:
    def __init__(self, w, part, home):
        self.w, self.part, self.home = w, part, home
        self.slots = [w.slot() for _ in range(3)]
        self.kept = w.held_here(part(w.place.t), home)

    def start(self):
        p = self.w.place

        @pl.when(p.t == p.z)
        def _():
            self.kept.start()
            for peer, slot in zip(p.peers, self.slots):
                self.w.copy(self.part(peer), self.home, slot, p.plane(peer)).start()

    def finish(self):
        p = self.w.place
        for peer, slot in zip(p.peers, self.slots):

            @pl.when(peer == p.z)
            def _():
                self.w.landed(self.home, slot)

        @pl.when(p.t == p.z)
        def _():
            self.kept.wait()
            for peer, slot in zip(p.peers, self.slots):
                self.w.sent(self.part(peer), slot)


def rows16(i, size=16):
    return pl.ds(pl.multiple_of(i * 16, 16), size)


def cols(b, width=128):
    return pl.ds(pl.multiple_of(b * width, width), width)


def norm_rows(v):
    return lax.rsqrt(jnp.mean(v * v, axis=1, keepdims=True) + epsilon)


def log1p_series(y):
    s = y / (2.0 + y)
    q = s * s
    total = 1.0 / 17
    for n in (15, 13, 11, 9, 7, 5, 3, 1):
        total = total * q + 1.0 / n
    return 2.0 * s * total


def turn(src, dst, j):
    @pl.loop(0, 12)
    def _(i):
        dst[cols(i), cols(j, 256)] = src[j, :, cols(i)].T


def fold(state, product):
    rows = [v[0:1, b * 128 : (b + 1) * 128] for v in (state, product) for b in range(4)]
    return jnp.concatenate(rows, axis=0)


def unfold(tile, first):
    return jnp.concatenate([jnp.broadcast_to(tile[first + b : first + b + 1, :], (8, 128)) for b in range(4)], axis=1)


def recurrence_forward(
    x_ref, gain_1d, conv_w, conv_b, gate_bias, decay, wx, wy, wo, gates, wg, wu, wd, cot,
    x1_ref, stat_ref, sm_out,
    n1t_out, win_out, wout_out, wg_out, wu_out, a2d, cot_out, gg_out,
    xb_out, zy_out, zx_out, za_out, c_out, a_out, h_out, o_out,
    win, wout, gg, n1, n1t, xb, zy, zx, za, cc, aa, hh, ac, oo, part, far, near,
    tail, sums, sm_ref, small_ref, gain_ref, send, recv, local,
):
    p = Place()
    w = Wires(p, send, recv, local)
    t, c, z = p.t, p.c, p.z
    odd = pl.ds(1024, 128)
    small_ref[...] = jnp.zeros((16, 512), f32)
    small_ref[0:4, :] = conv_w[...]
    small_ref[4:5, :] = conv_b[...].reshape(1, 512)
    small_ref[5:7, :] = gate_bias[...]
    raw = decay[...].reshape(1, 512)
    small_ref[7:8, :] = jnp.maximum(raw, 0.0) + log1p_series(jnp.exp(-jnp.abs(raw)))
    small_ref[8:9, :] = jax.nn.sigmoid(raw)
    gain_ref[...] = gain_1d[...].reshape(1, 1536)
    p.enter()

    spread_in = Spread(
        w,
        [lambda q: wx.at[:, cols(q)], lambda q: wy.at[:, cols(q)], lambda q: gates.at[:, q]],
        [
            lambda q: win.at[0, q, c, :, cols(z)],
            lambda q: win.at[1, q, c, :, cols(z)],
            lambda q: gg.at[:, z, q, c],
        ],
    )
    spread_out = Spread(w, [lambda q: wo.at[:, cols(q)]], [lambda q: wout.at[q, c, :, cols(z)]])

    def wide(weight, home, odd_home):
        return (
            Spread(w, [lambda q: weight.at[:, cols(q, 256)]], [home]),
            OneSpread(w, weight.at[:, odd], odd_home),
        )

    spreads = [
        wide(wg, lambda q: wg_out.at[q, c, :, cols(z, 256)], lambda q: wg_out.at[q, c, :, odd]),
        wide(wu, lambda q: wu_out.at[q, c, :, cols(z, 256)], lambda q: wu_out.at[q, c, :, odd]),
        wide(wd, lambda q: a2d.at[q, :, pl.ds(0, 256)], lambda q: a2d.at[q, :, pl.ds(256, 128)]),
    ]

    def wide_line(full):
        return LineGather(
            w, [(lambda b, q: full.at[:, q, :, cols(b, 256)], False), (lambda b, q: full.at[:, q, :, odd], True)]
        )

    line_in = LineGather(
        w, [(lambda b, q: win.at[:, :, q, :, cols(b)], False), (lambda b, q: gg.at[:, b, :, q], False)]
    )
    line_out = LineGather(w, [(lambda b, q: wout.at[:, q, :, cols(b)], False)])
    line_g, line_u = wide_line(wg_out), wide_line(wu_out)

    spread_in.start()
    small_slots = [w.slot() for _ in range(3)]
    for k in (1, 2, 3):
        w.copy(
            small_ref.at[:, cols(t)], sm_ref.at[:, cols(z)], small_slots[k - 1], p.line(p.around(k))
        ).start()
    sm_ref[:, cols(z)] = small_ref[:, cols(t)]

    @pl.loop(0, 16)
    def _(i):
        v = x_ref[rows16(i), :].astype(f32)
        n1[t, rows16(i), :] = (v * norm_rows(v) * gain_ref[...]).astype(bf16)

    gather = PlaneGather(w, n1)
    gather.start()
    spread_in.wait()
    line_in.first()
    turn(n1, n1t, t)
    line_in.step(2)
    gather.forward()
    spread_out.start()
    for part_spread in spreads[0] + spreads[1]:
        part_spread.start()
    turn(n1, n1t, p.tx)
    turn(n1, n1t, p.ty)
    line_in.step(3)
    spread_out.wait()
    line_out.first()
    line_in.step(4)
    line_in.finish()
    kept = [w.here(win, win_out), w.here(gg, gg_out)]
    gather.finish()
    gather_cot = PlaneGather(w, cot_out)
    gather_cot.start(cot)

    @pl.loop(0, 4)
    def _(j):
        xb[j, pl.ds(8, 256), :] = mm(n1[j], win[0].reshape(1536, 512))

    halo = w.slot()

    @pl.when(z < 3)
    def _():
        w.copy(xb.at[:, pl.ds(256, 8)], xb.at[:, pl.ds(0, 8)], halo, p.line(z + 1)).start()

    @pl.when(z == 0)
    def _():
        xb[:, 0:8, :] = jnp.zeros((4, 8, 512), f32)

    line_out.step(2)
    turn(n1, n1t, p.td)
    kept.append(w.here(n1t, n1t_out))
    for part_spread in spreads[0]:
        part_spread.wait()
    line_g.first()
    for k in (1, 2, 3):
        w.landed(sm_ref.at[:, cols(p.around(4 - k))], small_slots[k - 1])

    @pl.loop(0, 4)
    def _(j):
        zy[j] = mm(n1[j], win[1].reshape(1536, 512))

    line_out.step(3)
    kept.append(w.here(zy, zy_out))

    @pl.when(z > 0)
    def _():
        w.landed(xb.at[:, pl.ds(0, 8)], halo)

    row = lax.broadcasted_iota(jnp.int32, (8, 512), 0)
    zero = jnp.zeros((8, 512), f32)

    def convolve(j):
        @pl.loop(0, 16)
        def _(i):
            v = xb[j, rows16(i, 24), :]
            total = sm_ref[4:5, :] + sm_ref[0:1, :] * v[8:24]
            for k in (1, 2, 3):
                total = total + sm_ref[k : k + 1, :] * v[8 - k : 24 - k]
            cc[j, rows16(i), :] = total.astype(bf16)

        for b in range(4):
            lanes = pl.ds(b * 128, 128)
            left = cc[j, :, lanes]
            zx[j, :, lanes] = mm(left, gg[0, b].reshape(128, 128)) + sm_ref[5:6, lanes]
            za[j, :, lanes] = mm(left, gg[1, b].reshape(128, 128)) + sm_ref[6:7, lanes]

    def scan(j):
        def advance(i, carry):
            state, product = carry
            pre_x, pre_a = zx[j, rows16(i), :], za[j, rows16(i), :]
            rate, entry = jax.nn.sigmoid(pre_a), jax.nn.sigmoid(pre_x)
            zx[j, rows16(i), :] = entry
            za[j, rows16(i), :] = rate
            log_a = -8.0 * rate * sm_ref[7:8, :]
            decay = jnp.exp(log_a)
            mult = jnp.sqrt(one_minus_square(2.0 * log_a, decay))
            index = lax.broadcasted_iota(jnp.int32, (16, 512), 0) + i * 16 + z * 256
            mult = jnp.where(index == 0, 1.0, mult)
            inflow = mult * entry * cc[j, rows16(i), :].astype(f32)
            aa[j, rows16(i), :] = decay
            for half in (0, 8):
                dv, uv = decay[half : half + 8], inflow[half : half + 8]
                for st in (1, 2, 4):
                    ok = row >= st
                    uv = uv + jnp.where(ok, dv * pltpu.roll(uv, st, 0), 0.0)
                    dv = jnp.where(ok, dv * pltpu.roll(dv, st, 0), dv)
                hv, pv = uv + dv * state, dv * product
                hh[j, pl.ds(pl.multiple_of(i * 16 + half + 8, 8), 8), :] = hv
                ac[j, pl.ds(pl.multiple_of(i * 16 + half, 8), 8), :] = pv
                state = jnp.broadcast_to(hv[7:8, :], (8, 512))
                product = jnp.broadcast_to(pv[7:8, :], (8, 512))
            return state, product

        state, product = lax.fori_loop(0, 16, advance, (zero, zero + 1.0))
        tail[j] = fold(state, product)

    tail_slots = w.block(12)

    def tell(n, j):
        for away in (1, 2, 3):

            @pl.when(z + away <= 3)
            def _():
                w.copy(tail.at[j], sums.at[z, j], tail_slots + 3 * n + away - 1, p.line(z + away)).start()

    def settle(n, j):
        for away in (1, 2, 3):

            @pl.when(z >= away)
            def _():
                w.landed(sums.at[z - away, j], tail_slots + 3 * n + away - 1)

        enter = zero
        for src in range(3):
            tile = sums[src, j]
            enter = jnp.where(z > src, unfold(tile, 0) + unfold(tile, 4) * enter, enter)
        hh[j, 0:8, :] = enter
        first = jnp.concatenate([enter, enter], axis=0)

        @pl.loop(0, 16)
        def _(i):
            at = pl.ds(pl.multiple_of(i * 16 + 8, 8), 16)
            hv = hh[j, at, :] + ac[j, rows16(i), :] * first
            hh[j, at, :] = hv
            oo[j, rows16(i), :] = (hv * gelu_value(zy[j, rows16(i), :])).astype(bf16)

    def project(j):
        for n in range(2):
            part[j, :, n * 768 : (n + 1) * 768] = mm_nt(
                oo[j], wout[2 * n : 2 * n + 2].reshape(768, 512)
            ).astype(bf16)

    summed = PlaneSum(w, part, far, near)
    kept_out = w.held_here(wout, wout_out)

    @pl.loop(0, 5)
    def _(k):
        @pl.when(k < 4)
        def _():
            j = p.member(3 - k)
            convolve(j)
            scan(j)
            tell(k, j)

        @pl.when(k == 0)
        def _():
            line_out.step(4)
            line_g.step(2)
            for part_spread in spreads[1]:
                part_spread.wait()
            line_u.first()

        @pl.when(k == 1)
        def _():
            line_out.finish()
            kept_out.start()

        @pl.when(k == 2)
        def _():
            line_g.step(3)
            line_u.step(2)
            gather_cot.forward()

        @pl.when(k == 4)
        def _():
            line_u.step(3)

        @pl.when(k > 0)
        def _():
            j = p.member(4 - k)
            settle(k - 1, j)
            project(j)

        @pl.when(k == 1)
        def _():
            summed.diagonal()

        @pl.when(k == 3)
        def _():
            summed.arrive()
            summed.to_y()
            summed.to_x()

    for part_spread in spreads[2]:
        part_spread.start()
    kept += [w.here(xb, xb_out), w.here(cc, c_out), w.here(zx, zx_out), w.here(za, za_out)]
    kept += [kept_out, w.here(hh, h_out), w.here(oo, o_out)]
    next_slot = w.slot()

    @pl.when(z > 0)
    def _():
        w.copy(aa.at[:, pl.ds(0, 8)], aa.at[:, pl.ds(256, 8)], next_slot, p.line(z - 1)).start()

    @pl.when(z == 3)
    def _():
        aa[:, 256:264, :] = jnp.zeros((4, 8, 512), f32)

    line_g.step(4)

    @pl.when(z < 3)
    def _():
        w.landed(aa.at[:, pl.ds(256, 8)], next_slot)

    kept.append(w.here(aa, a_out))
    line_g.finish()
    gather_cot.finish()
    summed.finish()

    def last(i, carry):
        at = rows16(i)
        branch = part[t, at, :].astype(f32) + near[0, at, :].astype(f32) + near[1, at, :].astype(f32)
        stream = x_ref[at, :].astype(f32) + branch
        x1_ref[at, :] = stream
        s2, b2 = stream * stream, branch * branch
        return carry[0] + s2[0:8] + s2[8:16], carry[1] + b2[0:8] + b2[8:16]

    zw = jnp.zeros((8, 1536), f32)
    s2, b2 = lax.fori_loop(0, 16, last, (zw, zw))
    stat_ref[...] = zw
    stat_ref[0:1, :] = jnp.sum(s2, axis=0, keepdims=True)
    stat_ref[1:2, :] = jnp.sum(b2, axis=0, keepdims=True)
    sm_out[...] = sm_ref[...]
    line_u.step(4)
    line_u.finish()
    for part_spread in spreads[2]:
        part_spread.wait()
    for made in kept:
        made.wait()
    spread_in.drain()
    spread_out.drain()
    for pair in spreads:
        for part_spread in pair:
            part_spread.drain()
    for k in (1, 2, 3):
        w.sent(small_ref.at[:, cols(t)], small_slots[k - 1])
    gather.drain()
    gather_cot.drain()
    line_in.drain()
    line_out.drain()
    line_g.drain()
    line_u.drain()

    @pl.when(z < 3)
    def _():
        w.sent(xb.at[:, pl.ds(256, 8)], halo)

    for n in range(4):
        for away in (1, 2, 3):

            @pl.when(z + away <= 3)
            def _():
                w.sent(tail.at[n], tail_slots + 3 * n + away - 1)

    @pl.when(z > 0)
    def _():
        w.sent(aa.at[:, pl.ds(0, 8)], next_slot)

    summed.drain()


def shape(dims, dtype):
    return jax.ShapeDtypeStruct(dims, dtype)


def call(kernel, number, args, spaces, outs, out_spaces, scratch, wires, locals_, name):
    v = pl.BlockSpec(memory_space=pltpu.VMEM)
    a = pl.BlockSpec(memory_space=pl.ANY)
    kinds = {"v": v, "a": a}
    return pl.pallas_call(
        kernel,
        out_shape=outs,
        in_specs=[kinds[k] for k in spaces],
        out_specs=[kinds[k] for k in out_spaces],
        scratch_shapes=list(scratch)
        + [
            pltpu.SemaphoreType.DMA((wires,)),
            pltpu.SemaphoreType.DMA((wires,)),
            pltpu.SemaphoreType.DMA((locals_,)),
        ],
        compiler_params=pltpu.CompilerParams(
            collective_id=number, has_side_effects=True, vmem_limit_bytes=VMEM_BYTES
        ),
        name=name,
    )(*args)


def forward_recurrence(*args):
    V = pltpu.VMEM
    outs = [
        shape((256, 1536), f32), shape((8, 1536), f32), shape((16, 512), f32),
        shape((1536, 1024), bf16), shape((2, 4, 2, 192, 512), bf16), shape((4, 2, 192, 512), bf16),
        shape((4, 2, 192, 1152), bf16), shape((4, 2, 192, 1152), bf16), shape((4, 192, 384), bf16),
        shape((4, 256, 1536), bf16), shape((2, 4, 4, 2, 16, 128), bf16),
        shape((4, 264, 512), f32), shape((4, 256, 512), f32), shape((4, 256, 512), f32),
        shape((4, 256, 512), f32), shape((4, 256, 512), bf16), shape((4, 264, 512), f32),
        shape((4, 264, 512), f32), shape((4, 256, 512), bf16),
    ]
    scratch = [
        V((2, 4, 2, 192, 512), bf16), V((4, 2, 192, 512), bf16), V((2, 4, 4, 2, 16, 128), bf16),
        V((4, 256, 1536), bf16), V((1536, 1024), bf16), V((4, 264, 512), f32), V((4, 256, 512), f32),
        V((4, 256, 512), f32), V((4, 256, 512), f32), V((4, 256, 512), bf16),
        V((4, 264, 512), f32), V((4, 264, 512), f32), V((4, 256, 512), f32),
        V((4, 256, 512), bf16), V((4, 256, 1536), bf16), V((2, 128, 1536), bf16),
        V((2, 256, 1536), bf16),
        V((4, 8, 128), f32), V((4, 4, 8, 128), f32), V((16, 512), f32), V((16, 512), f32), V((1, 1536), f32),
    ]
    return call(
        recurrence_forward, 0, args, "v" * 6 + "a" * 8,
        outs, "vvv" + "a" * 16, scratch, 160, 32, "recurrence_forward",
    )


def half_line(w, piece, landing, odd_piece=None, odd_landing=None):
    odd = None if odd_piece is None else (odd_piece, lambda n: odd_landing.at[n])
    return LineSum(w, [(piece, lambda s, k: landing.at[s * 3 + k - 1])], odd)


def feed_forward(
    x1_ref, gain_1d, cot_ref, cot_in, wg_in, wu_in, a2d,
    dx1_ref, y_ref, stat_ref, half_out, piece_out,
    wgu, wd, n2, n2t, ct, ctt, gu, hid, dgu, part, far, near,
    gdown, cb, landing, landing_odd, gain_ref, send, recv, local,
):
    p = Place()
    w = Wires(p, send, recv, local)
    t, c, z = p.t, p.c, p.z
    gain_ref[...] = gain_1d[...].reshape(1, 1536)
    p.enter()
    odd = pl.ds(1024, 128)

    first = w.here(a2d.at[:, :, pl.ds(0, 256)], wd.at[:, c, :, cols(z, 256)])
    first_odd = w.held_here(a2d.at[:, :, pl.ds(256, 128)], wd.at[:, c, :, odd])

    @pl.when(t == z)
    def _():
        first_odd.start()

    load_gate, load_up = w.here(wg_in, wgu.at[0]), w.here(wu_in, wgu.at[1])
    load_cot = [w.here(cot_in.at[j], ct.at[j]) for j in p.peers]

    @pl.loop(0, 16)
    def _(i):
        at = rows16(i)
        v = x1_ref[at, :]
        n2[t, at, :] = (v * norm_rows(v) * gain_ref[...]).astype(bf16)
        ct[t, at, :] = cot_ref[at, :]

    gather = PlaneGather(w, n2)
    gather.start()
    first.wait()

    @pl.when(t == z)
    def _():
        first_odd.wait()

    line_d = LineGather(
        w, [(lambda b, q: wd.at[:, q, :, cols(b, 256)], False), (lambda b, q: wd.at[:, q, :, odd], True)]
    )
    line_d.first()
    load_gate.wait()
    load_up.wait()

    @pl.loop(0, 4)
    def _(k):
        @pl.when(k == 1)
        def _():
            for made in load_cot:
                made.wait()

            @pl.loop(0, 4)
            def _(n):
                turn(ct, ctt, n)

            line_d.step(2)
            gather.forward()
            line_d.step(3)

        @pl.when(k == 3)
        def _():
            gather.finish()

        j = p.member(k)

        @pl.loop(0, 2)
        def _(m):
            gu[m, j] = mm(n2[j], wgu[m].reshape(1536, 1152))

        @pl.loop(0, 16)
        def _(i):
            at = rows16(i)
            value, slope = gelu_pair(gu[0, j, at, :])
            u = gu[1, j, at, :]
            hid[j, at, :] = (value * u).astype(bf16)
            gu[0, j, at, :] = u * slope
            gu[1, j, at, :] = value

        @pl.when(k < 3)
        def _():
            turn(n2, n2t, j)

    line_d.step(4)
    line_d.finish()

    def weight_grad(left, right, out, first, count):
        @pl.loop(first, first + count)
        def _(i):
            out[i] = mm(left[cols(i, 384), :], right[...].reshape(1024, 1152)).astype(bf16).reshape(2, 192, 1152)

    def half_unit(home, u, n):
        return half_line(
            w,
            lambda j: home.at[pl.ds(2 * u, 2), c, :, cols(j, 256)],
            landing.at[n],
            home.at[pl.ds(2 * u, 2), c, :, odd],
            landing_odd.at[n],
        )

    units = [half_unit(gdown, 0, 0), half_unit(gdown, 1, 1), half_unit(wgu.at[0], 0, 2)]
    cores = [
        CoreSum(w, lambda q, u=u: gdown.at[pl.ds(2 * u, 2), q], cb.at[0, pl.ds(2 * u, 2)]) for u in range(2)
    ]
    cores_gu = [CoreSum(w, lambda q, m=m: wgu.at[m, :, q], cb.at[1 - m]) for m in range(2)]
    summed = PlaneSum(w, part, far, near)
    near_m = n2.at[pl.ds(0, 2)]
    branch = PlaneSum(w, ct, far, near_m)

    def mid(j):
        for n in range(2):
            ct[j, :, n * 768 : (n + 1) * 768] = mm_nt(
                hid[j], wd[2 * n : 2 * n + 2].reshape(768, 1152)
            ).astype(bf16)

    @pl.loop(0, 4)
    def _(k):
        j = p.member(3 - k)
        dh = mm(ct[j], wd[...].reshape(1536, 1152))
        for m in range(2):
            dgu[m, j] = (dh * gu[m, j]).astype(bf16)

        for n in range(2):
            span = pl.ds(2 * n, 2)
            part[j, :, n * 768 : (n + 1) * 768] = (
                mm_nt(dgu[0, j], wgu[0, span].reshape(768, 1152)) + mm_nt(dgu[1, j], wgu[1, span].reshape(768, 1152))
            ).astype(bf16)

        @pl.when(k == 0)
        def _():
            summed.diagonal()
            turn(n2, n2t, p.td)

        @pl.when(k == 1)
        def _():
            cores[0].finish()
            units[0].first()

        @pl.when(k == 2)
        def _():
            summed.arrive()
            summed.to_y()
            summed.to_x()
            cores[1].finish()
            units[1].first()

        @pl.when(k < 2)
        def _():
            weight_grad(ctt, hid, gdown, 2 * k, 2)

        @pl.when(k == 0)
        def _():
            cores[0].start()

        @pl.when(k == 1)
        def _():
            cores[1].start()

    units[0].step(2)

    @pl.loop(0, 2)
    def _(m):
        weight_grad(n2t, dgu.at[m], wgu.at[m], 0, 4)

        @pl.when(m == 0)
        def _():
            cores_gu[0].start()
            units[0].step(3)

        @pl.when(m == 1)
        def _():
            cores_gu[0].finish()
            cores_gu[1].start()
            units[2].first()

        for i in range(2):
            mid(p.member(3 - 2 * m - i))

    units[0].step(4)
    units[1].step(2)
    summed.finish()
    gather.drain()
    branch.diagonal()

    def dx(i, carry):
        at = rows16(i)
        v = x1_ref[at, :]
        s = norm_rows(v)
        dn = part[t, at, :].astype(f32) + near[0, at, :].astype(f32) + near[1, at, :].astype(f32)
        q = gain_ref[...] * dn
        dx1_ref[at, :] = (
            cot_ref[at, :].astype(f32) + s * q - v * (s * s * s * jnp.mean(q * v, axis=1, keepdims=True))
        )
        g2 = dn * v * s
        return carry + g2[0:8] + g2[8:16]

    zw = jnp.zeros((8, 1536), f32)
    g2 = lax.fori_loop(0, 16, dx, zw)
    stat_ref[...] = zw
    stat_ref[4:5, :] = jnp.sum(g2, axis=0, keepdims=True)
    units[1].step(3)
    cores_gu[1].finish()
    kept = [w.here(wgu.at[1, :, c], half_out.at[1])]
    branch.arrive()
    branch.to_y()
    branch.to_x()
    units[1].step(4)
    for src, dst in ((cols(z, 256), pl.ds(0, 256)), (odd, pl.ds(256, 128))):
        kept.append(w.here(gdown.at[:, c, :, src], piece_out.at[:, :, dst]))
    units[2].step(2)
    units[2].step(3)
    units[2].step(4)
    kept.append(w.here(wgu.at[0, :, c], half_out.at[0]))
    branch.finish()

    def last(i, carry):
        at = rows16(i)
        m = ct[t, at, :].astype(f32) + n2[0, at, :].astype(f32) + n2[1, at, :].astype(f32)
        y = x1_ref[at, :] + m
        y_ref[at, :] = y.astype(bf16)
        m2, y2 = m * m, y * y
        return carry[0] + m2[0:8] + m2[8:16], carry[1] + y2[0:8] + y2[8:16]

    m2, y2 = lax.fori_loop(0, 16, last, (zw, zw))
    stat_ref[2:3, :] = jnp.sum(m2, axis=0, keepdims=True)
    stat_ref[3:4, :] = jnp.sum(y2, axis=0, keepdims=True)
    for made in kept:
        made.wait()
    line_d.drain()
    summed.drain()
    branch.drain()
    for unit in units + cores + cores_gu:
        unit.drain()


def recurrence_backward(
    x_ref, gain_1d, dx1_ref, sm_ref, stat1, stat2,
    win_in, wout_in, n1t_in, xb_in, zy_in, zx_in, za_in, c_in, a_in, h_in, o_in, gg_in,
    half_in, piece_in,
    gi_ref, v1_ref, v2_ref, v3_ref, gin_out, gout_out, gff_out, gd_out, ggate_out,
    win, wout, n1t, dr, xb, zy, zx, za, cc, aa, hh, oo, gg, hgu, tmp, bc, dzy, dzx, dza,
    far, near, gin, gout, ggr, cbi, cbo, cbg, land_i, land_o, land_g, land_f, land_fo,
    tail, sums, acc8, early_own, late_own, acc8_l, acc8_c, acc8_p, early_l, early_c, early_p, late_l, late_c, late_p,
    gain_ref, acc, send, recv, local,
):
    p = Place()
    w = Wires(p, send, recv, local)
    t, c, z = p.t, p.c, p.z
    gain_ref[...] = gain_1d[...].reshape(1, 1536)
    p.enter()
    odd = pl.ds(1024, 128)

    load_half = w.here(half_in, hgu)
    load_out = w.here(wout_in, wout)
    early = [w.here(a, b) for a, b in ((zy_in, zy), (h_in, hh), (a_in, aa))]
    later = [
        w.here(a, b)
        for a, b in (
            (o_in, oo), (zx_in, zx), (za_in, za), (c_in, cc), (gg_in, gg), (n1t_in, n1t), (xb_in, xb), (win_in, win),
        )
    ]

    @pl.loop(0, 16)
    def _(i):
        dr[t, rows16(i), :] = dx1_ref[rows16(i), :].astype(bf16)

    gather = PlaneGather(w, dr)
    gather.start()
    units = [
        half_line(
            w,
            lambda j, m=m, u=u: hgu.at[m, pl.ds(2 * u, 2), :, cols(j, 256)],
            land_f.at[n],
            hgu.at[m, pl.ds(2 * u, 2), :, odd],
            land_fo.at[n],
        )
        for n, (m, u) in enumerate(((0, 1), (1, 0), (1, 1)))
    ]
    line_o = half_line(w, lambda j: gout.at[:, c, :, cols(j)], land_o)
    line_y = half_line(w, lambda j: gin.at[1, :, c, :, cols(j)], land_i.at[1])
    line_x = LineSum(
        w,
        [
            (lambda j: gin.at[0, :, c, :, cols(j)], lambda s, k: land_i.at[0, s * 3 + k - 1]),
            (lambda j: ggr.at[:, j, :, c], lambda s, k: land_g.at[s * 3 + k - 1]),
        ],
    )

    load_half.wait()
    for unit in units:
        unit.first()
    load_out.wait()
    for made in early:
        made.wait()

    row = lax.broadcasted_iota(jnp.int32, (8, 512), 0)
    zero = jnp.zeros((8, 512), f32)

    def scan_rows(j):
        tmp[...] = mm(dr[j], wout[...].reshape(1536, 512))

        def step(k, carry):
            i = 15 - k
            state, product = carry
            at = rows16(i)
            value, slope = gelu_pair(zy[j, at, :])
            do = tmp[at, :]
            h = hh[j, pl.ds(pl.multiple_of(i * 16 + 8, 8), 16), :]
            dzy[j, at, :] = (do * h * slope).astype(bf16)
            flow = do * value
            follow = aa[j, rows16(i, 24), :][1:17]
            for half in (8, 0):
                uv, dv = flow[half : half + 8], follow[half : half + 8]
                for st in (1, 2, 4):
                    ok = row < 8 - st
                    uv = uv + jnp.where(ok, dv * pltpu.roll(uv, 8 - st, 0), 0.0)
                    dv = jnp.where(ok, dv * pltpu.roll(dv, 8 - st, 0), dv)
                gv, pv = uv + dv * state, dv * product
                here = pl.ds(pl.multiple_of(i * 16 + half, 8), 8)
                zy[j, here, :] = gv
                bc[j, here, :] = pv
                state = jnp.broadcast_to(gv[0:1, :], (8, 512))
                product = jnp.broadcast_to(pv[0:1, :], (8, 512))
            return state, product

        state, product = lax.fori_loop(0, 16, step, (zero, zero + 1.0))
        tail[j] = fold(state, product)

    tail_slots = w.block(12)
    down = Spread(
        w, [lambda q: piece_in.at[q, :, pl.ds(0, 256)]], [lambda q: gd_out.at[:, cols(q, 256)]]
    )
    down_odd = OddScatter(w, lambda q: piece_in.at[q, :, pl.ds(256, 128)], gd_out.at[:, odd])

    @pl.loop(0, 4)
    def _(k):
        @pl.when(k == 1)
        def _():
            units[0].step(2)
            gather.forward()
            units[0].step(3)


        @pl.when(k == 3)
        def _():
            gather.finish()
            down.start()
            down_odd.start()

        j = p.member(k)
        scan_rows(j)
        for away in (1, 2, 3):

            @pl.when(z >= away)
            def _():
                w.copy(tail.at[j], sums.at[z, j], tail_slots + 3 * k + away - 1, p.line(z - away)).start()

    units[0].step(4)
    units[1].step(2)
    for made in later:
        made.wait()

    @pl.loop(0, 4)
    def _(i):
        gout[i] = (
            mm_tn(dr[:, :, cols(i, 384)].reshape(1024, 384), oo[...].reshape(1024, 512))
            .astype(bf16)
            .reshape(2, 192, 512)
        )

    core_o = CoreSum(w, lambda q: gout.at[:, q], cbo)
    core_o.start()
    units[1].step(3)

    def in_grad(m, right):
        @pl.loop(0, 4)
        def _(i):
            gin[m, i] = mm(n1t[cols(i, 384), :], right[...].reshape(1024, 512)).astype(bf16).reshape(2, 192, 512)

    in_grad(1, dzy)
    core_y = CoreSum(w, lambda q: gin.at[1, :, q], cbi.at[1])
    core_y.start()
    core_o.finish()
    line_o.first()
    def through(j, carry):
        after = zero
        for src in (3, 2, 1):
            tile = sums[src, j]
            after = jnp.where(z < src, unfold(tile, 0) + unfold(tile, 4) * after, after)
        after = jnp.concatenate([after, after], axis=0)

        def step(i, carry):
            sum_x, sum_a, sum_d = carry
            at = rows16(i)
            g = zy[j, at, :] + bc[j, at, :] * after
            before = hh[j, rows16(i, 24), :][7:23]
            entry, rate, value = zx[j, at, :], za[j, at, :], cc[j, at, :].astype(f32)
            log_a = -8.0 * rate * sm_ref[7:8, :]
            decay = aa[j, at, :]
            index = lax.broadcasted_iota(jnp.int32, (16, 512), 0) + i * 16 + z * 256
            start = index == 0
            mult = jnp.where(start, 1.0, jnp.sqrt(one_minus_square(2.0 * log_a, decay)))
            gm = g * mult
            d_entry = gm * value
            bc[j, at, :] = gm * entry
            low_x = (d_entry * entry * (1.0 - entry)).astype(bf16)
            dzx[j, at, :] = low_x
            d_mult = g * entry * value
            d_log = g * before * decay - jnp.where(start, 0.0, d_mult * decay * decay / mult)
            low_a = (d_log * (-8.0 * sm_ref[7:8, :]) * rate * (1.0 - rate)).astype(bf16)
            dza[j, at, :] = low_a
            wide_x, wide_a, d_decay = low_x.astype(f32), low_a.astype(f32), d_log * rate
            return (
                sum_x + wide_x[0:8] + wide_x[8:16],
                sum_a + wide_a[0:8] + wide_a[8:16],
                sum_d + d_decay[0:8] + d_decay[8:16],
            )

        carry = lax.fori_loop(0, 16, step, carry)
        for b in range(4):
            lanes = pl.ds(b * 128, 128)
            bc[j, pl.ds(0, 256), lanes] += mm_nt(
                dzx[j, :, lanes], gg[0, b].reshape(128, 128)
            ) + mm_nt(dza[j, :, lanes], gg[1, b].reshape(128, 128))
        return carry

    def taps(j, carry):
        def step(i, carry):
            at = rows16(i)
            v = bc[j, rows16(i, 24), :]
            xv = xb[j, rows16(i, 24), :]
            total = sm_ref[0:1, :] * v[0:16]
            for k in (1, 2, 3):
                total = total + sm_ref[k : k + 1, :] * v[k : k + 16]
            oo[j, at, :] = total.astype(bf16)
            now = v[0:16]
            new = []
            for k in range(4):
                product = now * xv[8 - k : 24 - k]
                new.append(carry[k] + product[0:8] + product[8:16])
            new.append(carry[4] + now[0:8] + now[8:16])
            return tuple(new)

        return lax.fori_loop(0, 16, step, carry)

    halo_slots = w.block(4)

    def tell(n, j):
        @pl.when(z > 0)
        def _():
            w.copy(
                bc.at[j, pl.ds(0, 8)], bc.at[j, pl.ds(256, 8)], halo_slots + n, p.line(z - 1)
            ).start()

    def hear(n, j):
        @pl.when(z < 3)
        def _():
            w.landed(bc.at[j, pl.ds(256, 8)], halo_slots + n)

    @pl.when(z == 3)
    def _():
        bc[:, 256:264, :] = jnp.zeros((4, 8, 512), f32)

    def gate_grads(i, right):
        for b in range(4):
            lanes = pl.ds(b * 128, 128)
            ggr[i, b] = (
                mm_tn(cc[:, :, lanes].reshape(1024, 128), right[:, :, lanes].reshape(1024, 128))
                .astype(bf16)
                .reshape(4, 2, 16, 128)
            )

    gather.drain()
    summed = PlaneSum(w, dr, far, near)
    core_x = CoreSum(w, lambda q: gin.at[0, :, q], cbi.at[0])
    core_g = CoreSum(w, lambda q: ggr.at[:, :, :, q], cbg)
    spreads = [
        Spread(
            w,
            [lambda q: hgu.at[:, q, :, cols(z, 256)]],
            [lambda q: gff_out.at[:, :, cols(q, 256)]],
        ),
        Spread(
            w,
            [lambda q: gout.at[q, c, :, cols(z)], lambda q: gin.at[1, q, c, :, cols(z)]],
            [lambda q: gout_out.at[:, cols(q)], lambda q: gin_out.at[1, :, cols(q)]],
        ),
        Spread(
            w,
            [lambda q: gin.at[0, q, c, :, cols(z)], lambda q: ggr.at[:, z, q, c]],
            [lambda q: gin_out.at[0, :, cols(q)], lambda q: ggate_out.at[:, q]],
        ),
    ]
    odds = [
        OddScatter(w, lambda q: hgu.at[:, q, :, odd], gff_out.at[:, :, odd]),
    ]

    zw = jnp.zeros((8, 1536), f32)
    stats = stat1[...] + stat2[...]
    early_own[...] = jnp.zeros((16, 128), f32)
    stack_rows(stats[4:5, :], early_own)
    for n in range(4):
        early_own[12 + n : 13 + n, :] = jnp.broadcast_to(jnp.sum(stats[n : n + 1, :], axis=1, keepdims=True), (1, 128))
    late_own[...] = jnp.zeros((16, 128), f32)
    small_early = SmallSum(
        w, [(acc8, acc8_l, acc8_c, acc8_p), (early_own, early_l, early_c, early_p)], [True, False]
    )
    small_late = SmallSum(w, [(late_own, late_l, late_c, late_p)], [False])
    acc[...] = jnp.zeros((8, 8, 512), f32)

    @pl.loop(0, 5)
    def _(k):

        @pl.when(k == 4)
        def _():
            gate_grads(0, dzx)
            gate_grads(1, dza)

        @pl.when(k < 4)
        def _():
            j = p.member(3 - k)
            for away in (1, 2, 3):

                @pl.when(z + away <= 3)
                def _():
                    w.landed(sums.at[z + away, j], tail_slots + 3 * (3 - k) + away - 1)

            for n, value in enumerate(through(j, (zero,) * 3)):
                acc[n] += value
            tell(k, j)

        @pl.when(k > 0)
        def _():
            j = p.member(4 - k)
            hear(k - 1, j)
            for n, value in enumerate(taps(j, (zero,) * 5)):
                acc[3 + n] += value
            for n in range(2):
                span = pl.ds(2 * n, 2)
                dr[j, :, n * 768 : (n + 1) * 768] = (
                    mm_nt(oo[j], win[0, span].reshape(768, 512)) + mm_nt(dzy[j], win[1, span].reshape(768, 512))
                ).astype(bf16)

        @pl.when(k == 0)
        def _():
            core_y.finish()
            line_y.first()
            units[1].step(4)
            units[2].step(2)

        @pl.when(k == 1)
        def _():
            summed.diagonal()
            units[2].step(3)

        @pl.when(k == 2)
        def _():
            units[2].step(4)
            line_o.step(2)

        @pl.when(k == 3)
        def _():
            summed.arrive()
            summed.to_y()
            summed.to_x()
            line_o.step(3)

        @pl.when(k == 4)
        def _():
            line_o.step(4)
            line_y.step(2)

    in_grad(0, oo)
    core_x.start()
    core_g.start()
    line_y.step(3)
    acc8[5:6, :] = jnp.sum(acc[0], axis=0, keepdims=True)
    acc8[6:7, :] = jnp.sum(acc[1], axis=0, keepdims=True)
    acc8[7:8, :] = -8.0 * sm_ref[8:9, :] * jnp.sum(acc[2], axis=0, keepdims=True)
    for k in range(5):
        acc8[k : k + 1, :] = jnp.sum(acc[3 + k], axis=0, keepdims=True)
    small_early.line()
    core_x.finish()
    core_g.finish()
    line_x.first()
    line_y.step(4)
    small_early.core()
    summed.finish()
    spreads[0].start()
    odds[0].start()
    spreads[1].start()
    line_x.step(2)

    def last(i, carry):
        at = rows16(i)
        v = x_ref[at, :].astype(f32)
        s = norm_rows(v)
        dn = dr[t, at, :].astype(f32) + near[0, at, :].astype(f32) + near[1, at, :].astype(f32)
        q = gain_ref[...] * dn
        gi_ref[at, :] = (
            dx1_ref[at, :] + s * q - v * (s * s * s * jnp.mean(q * v, axis=1, keepdims=True))
        ).astype(bf16)
        g1 = dn * v * s
        return carry + g1[0:8] + g1[8:16]

    g1 = lax.fori_loop(0, 16, last, zw)
    line_x.step(3)
    stack_rows(jnp.sum(g1, axis=0, keepdims=True), late_own)
    small_late.line()
    small_early.plane()
    line_x.step(4)
    spreads[2].start()
    small_late.core()
    small_late.plane()
    v2_ref[...], v1_ref[...] = small_early.result()
    (v3_ref[...],) = small_late.result()

    for made in spreads + [down]:
        made.wait()
        made.drain()
    for made in odds + [down_odd]:
        made.finish()
    small_early.drain()
    small_late.drain()
    summed.drain()
    for made in units + [line_o, line_y, line_x, core_o, core_y, core_x, core_g]:
        made.drain()

    for n in range(4):
        for away in (1, 2, 3):

            @pl.when(z >= away)
            def _():
                w.sent(tail.at[n], tail_slots + 3 * n + away - 1)

    for n in range(4):

        @pl.when(z > 0)
        def _():
            w.sent(bc.at[n, pl.ds(0, 8)], halo_slots + n)


def feed_forward_call(*args):
    V = pltpu.VMEM
    outs = [
        shape((256, 1536), f32), shape((256, 1536), bf16), shape((8, 1536), f32),
        shape((2, 4, 192, 1152), bf16), shape((4, 192, 384), bf16),
    ]
    weights = V((4, 2, 192, 1152), bf16)
    tokens, turned = V((4, 256, 1536), bf16), V((1536, 1024), bf16)
    scratch = [
        V((2, 4, 2, 192, 1152), bf16), weights, tokens, turned, tokens, turned, V((2, 4, 256, 1152), f32),
        V((4, 256, 1152), bf16), V((2, 4, 256, 1152), bf16), tokens, V((2, 128, 1536), bf16),
        V((2, 256, 1536), bf16), weights, V((2, 4, 192, 1152), bf16),
        V((3, 6, 2, 192, 256), bf16), V((3, 3, 2, 192, 128), bf16), V((1, 1536), f32),
    ]
    return call(feed_forward, 1, args, "vvvaaaa", outs, "vvvaa", scratch, 128, 24, "feed_forward")


def backward_recurrence(*args):
    V = pltpu.VMEM
    outs = [
        shape((256, 1536), bf16), shape((16, 128), f32), shape((4, 8, 512), f32), shape((16, 128), f32),
        shape((2, 192, 512), bf16), shape((192, 512), bf16), shape((2, 192, 1152), bf16), shape((192, 1152), bf16),
        shape((2, 4, 16, 128), bf16),
    ]
    tokens, turned = V((4, 256, 1536), bf16), V((1536, 1024), bf16)
    wide, padded, low = V((4, 256, 512), f32), V((4, 264, 512), f32), V((4, 256, 512), bf16)
    scratch = [
        V((2, 4, 2, 192, 512), bf16), V((4, 2, 192, 512), bf16), turned, tokens, padded, wide, wide, wide, low,
        padded, padded, low, V((2, 4, 4, 2, 16, 128), bf16), V((2, 4, 192, 1152), bf16), V((256, 512), f32),
        padded, low, low, low,
        V((2, 128, 1536), bf16), V((2, 256, 1536), bf16),
        V((2, 4, 2, 192, 512), bf16), V((4, 2, 192, 512), bf16), V((2, 4, 4, 2, 16, 128), bf16),
        V((2, 4, 192, 512), bf16), V((4, 192, 512), bf16), V((2, 4, 4, 16, 128), bf16),
        V((2, 6, 4, 192, 128), bf16), V((6, 4, 192, 128), bf16), V((6, 2, 4, 16, 128), bf16),
        V((3, 6, 2, 192, 256), bf16), V((3, 3, 2, 192, 128), bf16),
        V((4, 8, 128), f32), V((4, 4, 8, 128), f32), V((8, 512), f32),
        V((16, 128), f32), V((16, 128), f32), V((4, 8, 512), f32), V((3, 8, 512), f32), V((4, 8, 512), f32),
        V((4, 16, 128), f32), V((3, 16, 128), f32), V((4, 16, 128), f32),
        V((4, 16, 128), f32), V((3, 16, 128), f32), V((4, 16, 128), f32),
        V((1, 1536), f32), V((8, 8, 512), f32),
    ]
    return call(
        recurrence_backward, 2, args, "vvvvvv" + "a" * 14,
        outs, "vvvvaaaaa", scratch, 192, 24, "recurrence_backward",
    )


def finish(count, gin, gout, gff, gd, ggate, y, gi, v1, v2, v3,
           wx, wy, wo, wg, wu, wd, gg, y_out, gi_out, g1, g2, cw, cb, bias, decay, rms, rows, wide):
    wx[...] = gin[0].astype(f32)
    wy[...] = gin[1].astype(f32)
    wo[...] = gout[...].astype(f32)
    wg[...] = gff[0].astype(f32)
    wu[...] = gff[1].astype(f32)
    wd[...] = gd[...].astype(f32)
    y_out[...] = y[...]
    gi_out[...] = gi[...]

    @pl.when(pl.program_id(0) == 0)
    def _():
        gg[...] = ggate[...].astype(f32)
        for n in range(12):
            wide[0:1, n * 128 : (n + 1) * 128] = v3[n : n + 1, :]
            wide[1:2, n * 128 : (n + 1) * 128] = v1[n : n + 1, :]
        g1[...] = wide[0:1, :].reshape(1536)
        g2[...] = wide[1:2, :].reshape(1536)
        for t in range(4):
            for z in range(4):
                rows[:, z * 512 + t * 128 : z * 512 + (t + 1) * 128] = v2[t, :, z * 128 : (z + 1) * 128]
        cw[...] = rows[0:4, :]
        cb[...] = rows[4:5, :].reshape(2048)
        bias[...] = rows[5:7, :]
        decay[...] = rows[7:8, :].reshape(2048)
        root = jnp.sqrt(v1[12:16, :] / count)
        for i in range(4):
            rms[i] = root[i, 0]


def finish_call(count, gin, gout, gff, gd, ggate, y, gi, v1, v2, v3):
    steps = 4

    def sliced(a):
        axis = a.ndim - 2
        block = tuple(n // steps if i == axis else n for i, n in enumerate(a.shape))
        return pl.BlockSpec(block, lambda i: tuple(i if n == axis else 0 for n in range(a.ndim)))

    def whole(a):
        return pl.BlockSpec(a.shape, lambda i: (0,) * len(a.shape))

    one, two = shape((192, 512), f32), shape((192, 1152), f32)
    big = [one, one, one, two, two, two]
    small = [
        shape((1536,), f32), shape((1536,), f32), shape((4, 2048), f32), shape((2048,), f32),
        shape((2, 2048), f32), shape((2048,), f32),
    ]
    gates = shape(ggate.shape, f32)
    tokens = shape(y.shape, bf16)
    return pl.pallas_call(
        functools.partial(finish, count),
        out_shape=big + [gates, tokens, tokens] + small + [shape((4,), f32)],
        grid=(steps,),
        in_specs=[sliced(a) for a in (gin, gout, gff, gd)] + [whole(ggate)] + [sliced(a) for a in (y, gi)] + [whole(v1), whole(v2), whole(v3)],
        out_specs=[sliced(a) for a in big] + [whole(gates), sliced(tokens), sliced(tokens)]
        + [whole(a) for a in small] + [pl.BlockSpec(memory_space=pltpu.SMEM)],
        scratch_shapes=[pltpu.VMEM((8, 2048), f32), pltpu.VMEM((8, 1536), f32)],
        name="finish",
    )(gin, gout, gff, gd, ggate, y, gi, v1, v2, v3)


def fast_local(
    inputs, norm1_gain, w_in_x, w_in_y, conv_w, conv_b, gates, gate_bias, decay_param, w_out,
    norm2_gain, w_gate, w_up, w_down, cotangent,
):
    (x1, stat1, sm, n1t, win, wout, wg, wu, a2d, cot, gg, xb, zy, zx, za, cc, aa, hh, oo) = forward_recurrence(
        inputs, norm1_gain, conv_w, conv_b, gate_bias, decay_param, w_in_x, w_in_y, w_out, gates,
        w_gate, w_up, w_down, cotangent,
    )
    dx1, y, stat2, halves, piece = feed_forward_call(x1, norm2_gain, cotangent, cot, wg, wu, a2d)
    gi, v1, v2, v3, gin, gout, gff, gd, ggate = backward_recurrence(
        inputs, norm1_gain, dx1, sm, stat1, stat2, win, wout, n1t, xb, zy, zx, za, cc, aa, hh, oo, gg,
        halves, piece,
    )
    count = inputs.shape[0] * lax.axis_size("dp") * lax.axis_size("tensor") * inputs.shape[1]
    (gwx, gwy, gwo, gwg, gwu, gwd, ggates, output, grad_inputs, g1, g2, gcw, gcb, gbias, gdecay, rms) = finish_call(
        count, gin, gout, gff, gd, ggate, y, gi, v1, v2, v3
    )
    return (
        output, grad_inputs, g1, gwx, gwy, gcw, gcb, ggates, gbias, gdecay, gwo, g2, gwg, gwu, gwd, rms,
    )


def solution(mesh):
    fits = mesh.shape["dp"] == 8 and mesh.shape["tensor"] == 4
    return jax.shard_map(
        fast_local if fits else local,
        mesh=mesh,
        in_specs=(
            P(("dp", "tensor"), None),
            P(),
            P("dp", "tensor"),
            P("dp", "tensor"),
            P(None, "tensor"),
            P("tensor"),
            P(None, "tensor", "dp", None),
            P(None, "tensor"),
            P("tensor"),
            P("dp", "tensor"),
            P(),
            P("dp", "tensor"),
            P("dp", "tensor"),
            P("dp", "tensor"),
            P(("dp", "tensor"), None),
        ),
        out_specs=(
            P(("dp", "tensor"), None),
            P(("dp", "tensor"), None),
            P(),
            P("dp", "tensor"),
            P("dp", "tensor"),
            P(),
            P(),
            P(None, "tensor", "dp", None),
            P(),
            P(),
            P("dp", "tensor"),
            P(),
            P("dp", "tensor"),
            P("dp", "tensor"),
            P("dp", "tensor"),
            P(),
        ),
        check_vma=False,
    )
```
